128 devices in a mesh: head: 2 (over y_hi), block: 2 (over y_lo), tok: 32 (over z, x, core).
Axes of the slice: x: 4, y: 4 (y_hi: 2, y_lo: 2; y = y_hi * 2 + y_lo), z: 4, core: 2. Of those that a mesh axis runs over, the one named last changes fastest.
Arguments:
- tokens: bfloat16 [2, 16384, 2048], P('block', 'tok'), may hold values from -6 to 6
- input_weight: bfloat16 [2048, 3, 2048], P(None, None, 'head'), may hold values from -0.125 to 0.125
- rate_weight: bfloat16 [2048, 4], P(None, 'head'), may hold values from -0.375 to 0.375
- fast_init: bfloat16 [4, 3, 512, 512], P('head'), may hold values from -0.25 to 0.25
- output_weight: bfloat16 [2048, 2048], P('head'), may hold values from -0.125 to 0.125
Outputs:
- mixed: bfloat16 [2, 16384, 2048], P('block', 'tok', 'head')
The draws below stay inside these ranges and needn't reach their ends.
All inputs are finite; a program needn't handle non-finite values.
Results may differ from the reference program's by a relative error of at most 0.005.
Values sent between devices are 32-bit elements; how exact they have to be, the bound alone decides.
A program may use at most 128 MiB of HBM per device.

```python
import jax
import jax.numpy as jnp
from jax import lax

D = 2048
HEADS = 4
DH = 512
FH = 512
BLOCK_LEN = 16384
BLOCKS = 2


def block_scale(key, extent, shards, smallest, largest):
    factor_of, own = 1.0, jax.random.fold_in(key, 6)
    for dim, parts in shards:
        heights = jnp.exp(jax.random.uniform(jax.random.fold_in(own, dim), (parts,), jnp.float32, smallest / len(shards), largest / len(shards)))
        factor_of = factor_of * jnp.repeat(heights, extent[dim] // parts).reshape([-1 if axis == dim else 1 for axis in range(len(extent))])
    return factor_of


def gaussian(key, extent, scale, reach, pieces=(), dtype=jnp.bfloat16):
    gain = block_scale(key, extent, pieces, -0.22, 0.18) if pieces else 1.0
    result = jax.random.normal(key, extent, jnp.float32) * scale * gain
    return jnp.minimum(jnp.maximum(result, -reach), reach).astype(dtype)


def setup_inputs(seed: int = 0) -> dict:
    seeds = jax.random.split(jax.random.key(seed), 6)
    return {
        "tokens": gaussian(seeds[0], (BLOCKS, BLOCK_LEN, D), 1.0, 6.0, ((0, 2), (1, 32))),
        "input_weight": gaussian(seeds[1], (D, 3, HEADS * DH), D ** -0.5, 0.125, ((2, 2),)),
        "rate_weight": gaussian(seeds[2], (D, HEADS), (D // 9) ** -0.5, 0.375, ((1, 2),)),
        "fast_init": gaussian(seeds[3], (HEADS, 3, DH, FH), DH ** -0.5, 0.25, ((0, 2),)),
        "output_weight": gaussian(seeds[4], (HEADS * DH, D), (HEADS * DH) ** -0.5, 0.125, ((0, 2),)),
    }


epsilon = 1e-06
step_size = 0.03
highest = lax.Precision.HIGHEST

def matmul(left, right):
    return jnp.dot(left, right, precision=highest, preferred_element_type=jnp.float32)

def normalize(values):
    return values / jnp.sqrt(lax.optimization_barrier(jnp.mean(values * values, axis=-1, keepdims=True)) + epsilon)

def fast_grad(weights, keys, targets):
    gate = matmul(keys, weights[0])
    upper = matmul(keys, weights[1])
    sigma = jax.nn.sigmoid(gate)
    active = gate * sigma
    hidden = active * upper
    grad_down = matmul(targets.T, hidden)
    back = matmul(targets, weights[2])
    grad_upper = matmul(keys.T, back * active)
    grad_gate = matmul(keys.T, back * upper * sigma * (1.0 + gate * (1.0 - sigma)))
    return jnp.stack([grad_gate, grad_upper, grad_down])

def fast_step(weights, base_rms, grads):
    scale = jnp.sqrt(lax.optimization_barrier(jnp.mean(grads * grads, axis=(1, 2), keepdims=True)) + epsilon)
    moved = weights + step_size * grads / scale
    return moved * base_rms / jnp.sqrt(lax.optimization_barrier(jnp.mean(moved * moved, axis=1, keepdims=True)) + epsilon)

def fast_apply(weights, queries):
    gate = matmul(queries, weights[0])
    upper = matmul(queries, weights[1])
    hidden = gate * jax.nn.sigmoid(gate) * upper
    return normalize(matmul(hidden, weights[2].T))

def reference(tokens, input_weight, rate_weight, fast_init, output_weight):
    flattened = tokens.reshape(BLOCKS * BLOCK_LEN, D)
    projected = jnp.dot(flattened, input_weight.reshape(D, 3 * HEADS * DH), preferred_element_type=jnp.float32)
    projected = projected.reshape(BLOCKS, BLOCK_LEN, 3, HEADS, DH)
    rates = jax.nn.softplus(jnp.dot(flattened, rate_weight, preferred_element_type=jnp.float32))
    rates = rates.reshape(BLOCKS, BLOCK_LEN, HEADS)
    queries = normalize(projected[:, :, 0])
    keys = normalize(projected[:, :, 1])
    targets = projected[:, :, 2] * rates[:, :, :, None]
    results = []
    for head in range(HEADS):
        weights = fast_init[head].astype(jnp.float32)
        base_rms = jnp.sqrt(lax.optimization_barrier(jnp.mean(weights * weights, axis=1, keepdims=True)))
        outputs = []
        for block in range(BLOCKS):
            grads = fast_grad(weights, keys[block, :, head], targets[block, :, head])
            weights = fast_step(weights, base_rms, grads)
            outputs.append(fast_apply(weights, queries[block, :, head]))
        results.append(jnp.stack(outputs))
    joined = jnp.stack(results, axis=2).reshape(BLOCKS * BLOCK_LEN, HEADS * DH).astype(jnp.bfloat16)
    mixed = jnp.dot(joined, output_weight, preferred_element_type=jnp.float32).astype(jnp.bfloat16)
    return mixed.reshape(BLOCKS, BLOCK_LEN, D)
```

```python
import jax
import jax.numpy as jnp
from jax import lax
from jax.experimental import pallas as pl
from jax.experimental.pallas import tpu as pltpu
from jax.sharding import PartitionSpec as P

epsilon = 1e-06
step_size = 0.03
MESH = pl.DeviceIdType.MESH
f32 = jnp.float32
bf16 = jnp.bfloat16
N = 512
ORDER = (1, 0, 2)


def split(x):
    hi = x.astype(bf16)
    return hi, (x - hi.astype(f32)).astype(bf16)


def dot(a, b):
    return jnp.dot(a, b, preferred_element_type=f32)


def mm3(ah, al, bh, bl):
    return dot(ah, bh) + (dot(ah, bl) + dot(al, bh))


def dot_nt(a, b):
    return lax.dot_general(a, b, (((1,), (1,)), ((), ())), preferred_element_type=f32)


def mm3_nt(ah, al, bh, bl):
    return dot_nt(ah, bh) + (dot_nt(ah, bl) + dot_nt(al, bh))


def normalize(v):
    return v * (1.0 / jnp.sqrt(jnp.mean(v * v, axis=-1, keepdims=True) + epsilon))


def chain_kernel(
    k_ref, y_ref, q_ref, w0_ref, o_ref,
    k_got, y_got, q_got, o_mine, o_got,
    kh, kl, kth, ktl, yh, yl, yth, ytl,
    hh, hl, p3h, p3l, p1h, p1l,
    w, wh, wl, r0, gp, gf, gf1, r1, r2,
    rs_s, rs_r, ag_s, ag_r, a1_s, a1_r, sh_s, sh_r, ex_s, ex_r,
):
    tok = lax.axis_index("tok")
    block = lax.axis_index("block")
    core = lax.rem(tok, 2)
    chip = lax.div(tok, 2)
    x = lax.rem(chip, 4)
    z = lax.div(chip, 4)

    def at_x(d):
        return {"tok": (z * 4 + lax.rem(x + d + 4, 4)) * 2 + core}

    def at_z(d):
        return {"tok": (lax.rem(z + d + 4, 4) * 4 + x) * 2 + core}

    partner = {"tok": chip * 2 + (1 - core)}
    other_block = {"block": 1 - block}

    barrier = pltpu.get_barrier_semaphore()
    everyone = (partner, at_x(1), at_x(-1), at_z(1), at_z(-1), other_block)
    for device in everyone:
        pl.semaphore_signal(barrier, inc=1, device_id=device, device_id_type=MESH)
    pl.semaphore_wait(barrier, len(everyone))

    def rcopy(src, dst, ss, rs, device):
        return pltpu.make_async_remote_copy(
            src_ref=src, dst_ref=dst, send_sem=ss, recv_sem=rs,
            device_id=device, device_id_type=MESH,
        )

    mine = pl.ds(pl.multiple_of(core * N, N), N)
    theirs = pl.ds(pl.multiple_of((1 - core) * N, N), N)
    swaps = [
        rcopy(src.at[:, theirs], dst, ex_s.at[n], ex_r.at[n], partner)
        for n, (src, dst) in enumerate(((k_ref, k_got), (y_ref, y_got), (q_ref, q_got)))
    ]
    for copy in swaps:
        copy.start()

    for m in range(3):
        start = w0_ref[core, m].astype(f32)
        w[m] = start
        wh[m], wl[m] = split(start)
        r0[m] = jnp.sqrt(jnp.mean(start * start, axis=0, keepdims=True))

    def prepare(load, base, scale, h_ref, l_ref, th_ref, tl_ref):
        @pl.loop(0, 2)
        def _(i):
            rows = pl.ds(pl.multiple_of(i * 256, 256), 256)
            v = load(rows)
            if scale:
                v = normalize(v)
            hi, lo = split(v)
            to = pl.ds(pl.multiple_of(base + i * 256, 256), 256)
            h_ref[to, :] = hi
            l_ref[to, :] = lo
            th_ref[:, to] = hi.T
            tl_ref[:, to] = lo.T

    prepare(lambda r: k_ref[r, mine], 0, True, kh, kl, kth, ktl)
    prepare(lambda r: y_ref[r, mine], 0, False, yh, yl, yth, ytl)
    swaps[0].wait_recv()
    prepare(lambda r: k_got[r, :], N, True, kh, kl, kth, ktl)
    swaps[1].wait_recv()
    prepare(lambda r: y_got[r, :], N, False, yh, yl, yth, ytl)
    swaps[2].wait_recv()

    def rows_of(s, j1, j2=None, off=0, count=64):
        at = s * 256 + j1 * 64 + off
        if j2 is not None:
            at = at + j2 * 16
        return pl.ds(pl.multiple_of(at, 8), count)

    def reduce_stage(m, piece, n, got, store, i, go, ss, rs):
        src = gp.at[m]
        nxt, prv, far = lax.rem(i + 1, 4), lax.rem(i + 3, 4), lax.rem(i + 2, 4)
        right, left = go(1), go(-1)
        c0 = rcopy(src.at[piece(far, 0, n)], got.at[0], ss.at[0], rs.at[0], right)
        c1 = rcopy(src.at[piece(far, n, n)], got.at[1], ss.at[1], rs.at[1], left)
        c2 = rcopy(src.at[piece(nxt, n, n)], got.at[2], ss.at[2], rs.at[2], right)
        c3 = rcopy(src.at[piece(prv, 0, n)], got.at[3], ss.at[3], rs.at[3], left)
        for c in (c0, c1, c2, c3):
            c.start()
        yield
        c0.wait_recv()
        got[0] = got[0] + gp[m, piece(nxt, 0, n), :]
        c4 = rcopy(got.at[0], got.at[4], ss.at[4], rs.at[4], right)
        c4.start()
        c1.wait_recv()
        got[1] = got[1] + gp[m, piece(prv, n, n), :]
        c5 = rcopy(got.at[1], got.at[5], ss.at[5], rs.at[5], left)
        c5.start()
        yield
        for c in (c2, c3, c4, c5):
            c.wait_recv()
        store(0, gp[m, piece(i, 0, n), :] + got[3] + got[4])
        store(n, gp[m, piece(i, n, n), :] + got[2] + got[5])
        sent.extend((c0, c1, c2, c3, c4, c5))

    def gather_stage(buf, piece, n, i, go, ss, rs, done):
        nxt, prv, far = lax.rem(i + 1, 4), lax.rem(i + 3, 4), lax.rem(i + 2, 4)
        right, left = go(1), go(-1)

        def send(k, rows, device):
            return rcopy(buf.at[rows], buf.at[rows], ss.at[k], rs.at[k], device)

        c0 = send(0, piece(i, 0, 2 * n), right)
        c1 = send(1, piece(i, 0, 2 * n), left)
        c0.start()
        c1.start()
        yield
        send(0, piece(prv, 0, 2 * n), right).wait_recv()
        c2 = send(2, piece(prv, 0, n), right)
        c2.start()
        send(1, piece(nxt, 0, 2 * n), left).wait_recv()
        c3 = send(3, piece(nxt, n, n), left)
        c3.start()
        yield
        send(2, piece(far, 0, n), right).wait_recv()
        send(3, piece(far, n, n), left).wait_recv()
        done.extend((c0, c1, c2, c3))

    axes = ((x, at_x, z, at_z), (z, at_z, x, at_x))

    def gather(buf, m, s, ss, rs, done):
        i1, go1, i2, go2 = axes[s]
        yield from gather_stage(
            buf.at[m], lambda j, o, c: rows_of(s, i1, j, o, c), 8, i2, go2,
            ss.at[m, s, 0], rs.at[m, s, 0], done,
        )
        yield from gather_stage(
            buf.at[m], lambda j, o, c: rows_of(s, j, None, o, c), 32, i1, go1,
            ss.at[m, s, 1], rs.at[m, s, 1], done,
        )

    def shard(m, s):
        i1, _, i2, _ = axes[s]
        rows = rows_of(s, i1, i2, 0, 16)
        return rcopy(gf.at[m, rows], gf1.at[m, rows], sh_s.at[m, s], sh_r.at[m, s], other_block)

    sent = []

    def whole(m, s):
        i1, go1, i2, go2 = axes[s]

        def store1(o, v):
            gp[m, rows_of(s, i1, None, o, 32), :] = v

        def store2(o, v):
            gf[m, rows_of(s, i1, i2, o, 8), :] = v

        yield from reduce_stage(
            m, lambda j, o, c: rows_of(s, j, None, o, c), 32, r1.at[m, s], store1, i1, go1,
            rs_s.at[m, s, 0], rs_r.at[m, s, 0],
        )
        yield from reduce_stage(
            m, lambda j, o, c: rows_of(s, i1, j, o, c), 8, r2.at[m, s], store2, i2, go2,
            rs_s.at[m, s, 1], rs_r.at[m, s, 1],
        )

        @pl.when(block == 0)
        def _():
            shard(m, s).start()

        yield from gather(gf, m, s, ag_s, ag_r, sent)

    def update(m, g_ref):
        g = g_ref[m]
        total = jnp.sum(jnp.sum(g * g, axis=0, keepdims=True), axis=1, keepdims=True)
        scale = step_size / jnp.sqrt(total / (N * N) + epsilon)
        moved = w[m] + g * scale
        column = jnp.mean(moved * moved, axis=0, keepdims=True)
        fresh = moved * (r0[m] / jnp.sqrt(column + epsilon))
        w[m] = fresh
        wh[m], wl[m] = split(fresh)

    def drive(streams, finish):
        left = {m: list(streams[m]) for m in streams}
        while left:
            for m in [m for m in ORDER if m in left]:
                still = []
                for g in left[m]:
                    try:
                        next(g)
                        still.append(g)
                    except StopIteration:
                        pass
                left[m] = still
                if not still:
                    del left[m]
                    finish(m)

    @pl.when(block == 1)
    def _():
        done = []

        def first(m, s):
            shard(m, s).wait_recv()
            yield from gather(gf1, m, s, a1_s, a1_r, done)

        drive({m: [first(m, s) for s in range(2)] for m in range(3)}, lambda m: update(m, gf1))
        for c in done:
            c.wait_send()

    @pl.loop(0, 4)
    def _(i):
        rows = pl.ds(pl.multiple_of(i * 256, 256), 256)
        ah, al = kh[rows, :], kl[rows, :]
        gate = mm3(ah, al, wh[0], wl[0])
        upper = mm3(ah, al, wh[1], wl[1])
        back = mm3(yh[rows, :], yl[rows, :], wh[2], wl[2])
        sigma = jax.nn.sigmoid(gate)
        active = gate * sigma
        hh[rows, :], hl[rows, :] = split(active * upper)
        p3h[rows, :], p3l[rows, :] = split(back * active)
        p1h[rows, :], p1l[rows, :] = split(back * upper * sigma * (1.0 + gate * (1.0 - sigma)))

    def product(m, lth, ltl, rh, rl):
        @pl.loop(0, 4)
        def _(i):
            rows = pl.ds(pl.multiple_of(i * 128, 128), 128)
            gp[m, rows, :] = mm3(lth[rows, :], ltl[rows, :], rh[...], rl[...])

    live = {}

    def begin(m):
        live[m] = [whole(m, s) for s in range(2)]
        for g in live[m]:
            next(g)

    def advance(m):
        for g in live[m]:
            next(g)

    product(1, kth, ktl, p3h, p3l)
    begin(1)
    product(0, kth, ktl, p1h, p1l)
    begin(0)
    advance(1)
    product(2, yth, ytl, hh, hl)
    begin(2)
    drive(live, lambda m: update(m, gf))

    def apply(load, store):
        @pl.loop(0, 2)
        def _(i):
            rows = pl.ds(pl.multiple_of(i * 256, 256), 256)
            ah, al = split(normalize(load(rows)))
            gate = mm3(ah, al, wh[0], wl[0])
            upper = mm3(ah, al, wh[1], wl[1])
            bh, bl = split(gate * jax.nn.sigmoid(gate) * upper)
            store(rows, normalize(mm3_nt(bh, bl, wh[2], wl[2])).astype(bf16))

    def keep_theirs(rows, v):
        o_mine[rows, :] = v.astype(f32)

    def keep_mine(rows, v):
        o_ref[rows, mine] = v

    apply(lambda r: q_got[r, :], keep_theirs)
    out = rcopy(o_mine, o_got, ex_s.at[3], ex_r.at[3], partner)
    out.start()
    apply(lambda r: q_ref[r, mine], keep_mine)
    out.wait_recv()
    o_ref[:, theirs] = o_got[...].astype(bf16)

    for c in swaps + [out] + sent:
        c.wait_send()

    @pl.when(block == 0)
    def _():
        for m in range(3):
            for s in range(2):
                shard(m, s).wait_send()


def chain(k, y, q, fast_init):
    dma = pltpu.SemaphoreType.DMA
    square = lambda n, t: pltpu.VMEM((n, N, N), t)
    tall = pltpu.VMEM((2 * N, N), bf16)
    wide = pltpu.VMEM((N, 2 * N), bf16)
    part = pltpu.VMEM((N, N), f32)
    vmem = pl.BlockSpec(memory_space=pltpu.VMEM)
    return pl.pallas_call(
        chain_kernel,
        out_shape=jax.ShapeDtypeStruct((N, 2 * N), bf16),
        in_specs=[vmem] * 4,
        out_specs=vmem,
        scratch_shapes=[
            part, part, part, part, part,
            tall, tall, wide, wide, tall, tall, wide, wide,
            tall, tall, tall, tall, tall, tall,
            square(3, f32), square(3, bf16), square(3, bf16), pltpu.VMEM((3, 1, N), f32),
            square(3, f32), square(3, f32), square(3, f32),
            pltpu.VMEM((3, 2, 6, 32, N), f32), pltpu.VMEM((3, 2, 6, 8, N), f32),
            dma((3, 2, 2, 6)), dma((3, 2, 2, 6)),
            dma((3, 2, 2, 4)), dma((3, 2, 2, 4)),
            dma((3, 2, 2, 4)), dma((3, 2, 2, 4)),
            dma((3, 2)), dma((3, 2)),
            dma((4,)), dma((4,)),
        ],
        compiler_params=pltpu.CompilerParams(
            collective_id=0, has_side_effects=True, vmem_limit_bytes=60 * 1024 * 1024
        ),
    )(k, y, q, fast_init)


def body(tokens, input_weight, rate_weight, fast_init, output_weight):
    flat = tokens[0]
    parts = jnp.transpose(input_weight, (1, 0, 2))
    q = dot(flat, parts[0])
    k = dot(flat, parts[1])
    rates = jax.nn.softplus(dot(flat, rate_weight))
    y = dot(flat, parts[2]).reshape(N, 2, N) * rates[:, :, None]
    joined = chain(k, y.reshape(N, 2 * N), q, fast_init)
    partial_out = dot(joined, output_weight)[None]
    return lax.psum_scatter(partial_out, "head", scatter_dimension=2, tiled=True).astype(bf16)


def solution(mesh):
    placed = (
        P("block", "tok", None),
        P(None, None, "head"),
        P(None, "head"),
        P("head", None, None, None),
        P("head", None),
    )
    return jax.shard_map(
        body, mesh=mesh, in_specs=placed, out_specs=P("block", "tok", "head"), check_vma=False
    )
```

```python
import jax
import jax.numpy as jnp
from jax import lax
from jax.experimental import pallas as pl
from jax.experimental.pallas import tpu as pltpu
from jax.sharding import PartitionSpec as P

epsilon = 1e-06
step_size = 0.03
MESH = pl.DeviceIdType.MESH
f32 = jnp.float32
bf16 = jnp.bfloat16
N = 512
ORDER = (1, 0, 2)


def split(x):
    hi = x.astype(bf16)
    return hi, (x - hi.astype(f32)).astype(bf16)


def dot(a, b):
    return jnp.dot(a, b, preferred_element_type=f32)


def mm3(ah, al, bh, bl):
    return dot(ah, bh) + (dot(ah, bl) + dot(al, bh))


def dot_nt(a, b):
    return lax.dot_general(a, b, (((1,), (1,)), ((), ())), preferred_element_type=f32)


def mm3_nt(ah, al, bh, bl):
    return dot_nt(ah, bh) + (dot_nt(ah, bl) + dot_nt(al, bh))


def normalize(v):
    return v * (1.0 / jnp.sqrt(jnp.mean(v * v, axis=-1, keepdims=True) + epsilon))


def chain_kernel(
    tok_hbm, wi_hbm, rate_ref, w0_hbm, wo_hbm, o_ref,
    tok_v, wo, w0, ks, ys, qs, qm, k_got, y_got, q_got, o_mine, o_got, o_all, p_got,
    kh, kl, kth, ktl, yh, yl, yth, ytl, big,
    w, wh, wl, r0, gp, gf, gf1, r1, r2,
    rs_s, rs_r, ag_s, ag_r, a1_s, a1_r, sh_s, sh_r, ex_s, ex_r,
    pt_s, pt_r, rl_s, rl_r, in_s, wi_s,
):
    tok = lax.axis_index("tok")
    block = lax.axis_index("block")
    head = lax.axis_index("head")
    core = lax.rem(tok, 2)
    chip = lax.div(tok, 2)
    x = lax.rem(chip, 4)
    z = lax.div(chip, 4)

    def at_x(d):
        return {"tok": (z * 4 + lax.rem(x + d + 4, 4)) * 2 + core}

    def at_z(d):
        return {"tok": (lax.rem(z + d + 4, 4) * 4 + x) * 2 + core}

    partner = {"tok": chip * 2 + (1 - core)}
    other_block = {"block": 1 - block}
    diagonal = {"block": 1 - block, "head": 1 - head}
    other_head = {"head": 1 - head}

    mine = pl.ds(pl.multiple_of(core * N, N), N)
    theirs = pl.ds(pl.multiple_of((1 - core) * N, N), N)

    SEQ = ((1, theirs), (2, theirs), (1, mine), (2, mine), (0, theirs), (0, mine))

    def weights(n):
        part, columns = SEQ[n]
        return pltpu.make_async_copy(wi_hbm.at[part, :, columns], big.at[n % 3], wi_s.at[n % 3])

    load_tok = pltpu.make_async_copy(tok_hbm, tok_v, in_s.at[0])
    load_w0 = pltpu.make_async_copy(w0_hbm.at[core], w0, in_s.at[1])
    load_wo = pltpu.make_async_copy(wo_hbm, wo, in_s.at[2])
    load_tok.start()
    weights(0).start()
    weights(1).start()
    weights(2).start()
    load_w0.start()
    load_wo.start()

    barrier = pltpu.get_barrier_semaphore()
    everyone = (
        partner, at_x(1), at_x(-1), at_z(1), at_z(-1), other_block, diagonal, other_head
    )
    for device in everyone:
        pl.semaphore_signal(barrier, inc=1, device_id=device, device_id_type=MESH)
    pl.semaphore_wait(barrier, len(everyone))

    def rcopy(src, dst, ss, rs, device):
        return pltpu.make_async_remote_copy(
            src_ref=src, dst_ref=dst, send_sem=ss, recv_sem=rs,
            device_id=device, device_id_type=MESH,
        )

    swaps = [
        rcopy(src, dst, ex_s.at[n], ex_r.at[n], partner)
        for n, (src, dst) in enumerate(((ks, k_got), (ys, y_got), (qs, q_got)))
    ]

    def project(n, finish):
        weights(n).wait()

        @pl.loop(0, 2)
        def _(i):
            rows = pl.ds(pl.multiple_of(i * 256, 256), 256)
            finish(i * 256, rows, dot(tok_v[rows, :], big[n % 3]))

    def rates(rows, which):
        r = rate_ref[rows, :]
        return jnp.where(which == 0, r[:, 0:1], r[:, 1:2])

    def prepare(base, rows, v, h_ref, l_ref, th_ref, tl_ref):
        hi, lo = split(v)
        to = pl.ds(pl.multiple_of(base, 256), 256)
        h_ref[to, :] = hi
        l_ref[to, :] = lo
        th_ref[:, to] = hi.T
        tl_ref[:, to] = lo.T

    def put(ref, f):
        def finish(base, rows, v):
            ref[rows, :] = f(rows, v)

        return finish

    load_tok.wait()
    project(0, put(ks, lambda r, v: normalize(v)))
    swaps[0].start()
    weights(3).start()
    project(1, put(ys, lambda r, v: v * rates(r, 1 - core)))
    swaps[1].start()
    project(2, lambda b, r, v: prepare(b, r, normalize(v), kh, kl, kth, ktl))
    project(3, lambda b, r, v: prepare(b, r, v * rates(r, core), yh, yl, yth, ytl))

    def project_q():
        weights(4).start()
        weights(5).start()
        project(4, put(qs, lambda r, v: normalize(v)))
        swaps[2].start()
        project(5, put(qm, lambda r, v: normalize(v)))

    load_w0.wait()
    for m in range(3):
        start = w0[m].astype(f32)
        w[m] = start
        wh[m], wl[m] = split(start)
        r0[m] = jnp.sqrt(jnp.mean(start * start, axis=0, keepdims=True))

    def prepare_got(got, h_ref, l_ref, th_ref, tl_ref):
        @pl.loop(0, 2)
        def _(i):
            rows = pl.ds(pl.multiple_of(i * 256, 256), 256)
            prepare(N + i * 256, rows, got[rows, :], h_ref, l_ref, th_ref, tl_ref)

    swaps[0].wait_recv()
    prepare_got(k_got, kh, kl, kth, ktl)
    swaps[1].wait_recv()
    prepare_got(y_got, yh, yl, yth, ytl)

    def rows_of(s, j1, j2=None, off=0, count=64):
        at = s * 256 + j1 * 64 + off
        if j2 is not None:
            at = at + j2 * 16
        return pl.ds(pl.multiple_of(at, 8), count)

    def reduce_stage(m, piece, n, got, store, i, go, ss, rs):
        src = gp.at[m]
        nxt, prv, far = lax.rem(i + 1, 4), lax.rem(i + 3, 4), lax.rem(i + 2, 4)
        right, left = go(1), go(-1)
        c0 = rcopy(src.at[piece(far, 0, n)], got.at[0], ss.at[0], rs.at[0], right)
        c1 = rcopy(src.at[piece(far, n, n)], got.at[1], ss.at[1], rs.at[1], left)
        c2 = rcopy(src.at[piece(nxt, n, n)], got.at[2], ss.at[2], rs.at[2], right)
        c3 = rcopy(src.at[piece(prv, 0, n)], got.at[3], ss.at[3], rs.at[3], left)
        for c in (c0, c1, c2, c3):
            c.start()
        yield
        c0.wait_recv()
        got[0] = got[0] + gp[m, piece(nxt, 0, n), :]
        c4 = rcopy(got.at[0], got.at[4], ss.at[4], rs.at[4], right)
        c4.start()
        c1.wait_recv()
        got[1] = got[1] + gp[m, piece(prv, n, n), :]
        c5 = rcopy(got.at[1], got.at[5], ss.at[5], rs.at[5], left)
        c5.start()
        yield
        for c in (c2, c3, c4, c5):
            c.wait_recv()
        store(0, gp[m, piece(i, 0, n), :] + got[3] + got[4])
        store(n, gp[m, piece(i, n, n), :] + got[2] + got[5])
        sent.extend((c0, c1, c2, c3, c4, c5))

    def gather_stage(buf, piece, n, i, go, ss, rs, done):
        nxt, prv, far = lax.rem(i + 1, 4), lax.rem(i + 3, 4), lax.rem(i + 2, 4)
        right, left = go(1), go(-1)

        def send(k, rows, device):
            return rcopy(buf.at[rows], buf.at[rows], ss.at[k], rs.at[k], device)

        c0 = send(0, piece(i, 0, 2 * n), right)
        c1 = send(1, piece(i, 0, 2 * n), left)
        c0.start()
        c1.start()
        yield
        send(0, piece(prv, 0, 2 * n), right).wait_recv()
        c2 = send(2, piece(prv, 0, n), right)
        c2.start()
        send(1, piece(nxt, 0, 2 * n), left).wait_recv()
        c3 = send(3, piece(nxt, n, n), left)
        c3.start()
        yield
        send(2, piece(far, 0, n), right).wait_recv()
        send(3, piece(far, n, n), left).wait_recv()
        done.extend((c0, c1, c2, c3))

    axes = ((x, at_x, z, at_z), (z, at_z, x, at_x))

    def gather(buf, m, s, ss, rs, done):
        i1, go1, i2, go2 = axes[s]
        yield from gather_stage(
            buf.at[m], lambda j, o, c: rows_of(s, i1, j, o, c), 8, i2, go2,
            ss.at[m, s, 0], rs.at[m, s, 0], done,
        )
        yield from gather_stage(
            buf.at[m], lambda j, o, c: rows_of(s, j, None, o, c), 32, i1, go1,
            ss.at[m, s, 1], rs.at[m, s, 1], done,
        )

    def shard(m, s):
        i1, _, i2, _ = axes[s]
        rows = rows_of(s, i1, i2, 0, 16)
        return rcopy(gf.at[m, rows], gf1.at[m, rows], sh_s.at[m, s], sh_r.at[m, s], other_block)

    sent = []

    def whole(m, s):
        i1, go1, i2, go2 = axes[s]

        def store1(o, v):
            gp[m, rows_of(s, i1, None, o, 32), :] = v

        def store2(o, v):
            gf[m, rows_of(s, i1, i2, o, 8), :] = v

        yield from reduce_stage(
            m, lambda j, o, c: rows_of(s, j, None, o, c), 32, r1.at[m, s], store1, i1, go1,
            rs_s.at[m, s, 0], rs_r.at[m, s, 0],
        )
        yield from reduce_stage(
            m, lambda j, o, c: rows_of(s, i1, j, o, c), 8, r2.at[m, s], store2, i2, go2,
            rs_s.at[m, s, 1], rs_r.at[m, s, 1],
        )

        @pl.when(block == 0)
        def _():
            shard(m, s).start()

        yield from gather(gf, m, s, ag_s, ag_r, sent)

    def update(m, g_ref):
        def rows_at(i):
            return pl.ds(pl.multiple_of(i * 64, 64), 64)

        def squares(i, total):
            g = g_ref[m, rows_at(i), :]
            return total + jnp.sum(g * g, axis=0, keepdims=True)

        total = jnp.sum(lax.fori_loop(0, 8, squares, jnp.zeros((1, N), f32)), axis=1, keepdims=True)
        scale = step_size / jnp.sqrt(total / (N * N) + epsilon)

        def move(i, column):
            rows = rows_at(i)
            moved = w[m, rows, :] + g_ref[m, rows, :] * scale
            w[m, rows, :] = moved
            return column + jnp.sum(moved * moved, axis=0, keepdims=True)

        column = lax.fori_loop(0, 8, move, jnp.zeros((1, N), f32)) / N
        factor = r0[m] / jnp.sqrt(column + epsilon)

        @pl.loop(0, 8)
        def _(i):
            rows = rows_at(i)
            fresh = w[m, rows, :] * factor
            w[m, rows, :] = fresh
            wh[m, rows, :], wl[m, rows, :] = split(fresh)

    def drive(streams, finish):
        left = {m: list(streams[m]) for m in streams}
        while left:
            for m in [m for m in ORDER if m in left]:
                still = []
                for g in left[m]:
                    try:
                        next(g)
                        still.append(g)
                    except StopIteration:
                        pass
                left[m] = still
                if not still:
                    del left[m]
                    finish(m)

    @pl.when(block == 1)
    def _():
        project_q()
        done = []

        def first(m, s):
            shard(m, s).wait_recv()
            yield from gather(gf1, m, s, a1_s, a1_r, done)

        drive({m: [first(m, s) for s in range(2)] for m in range(3)}, lambda m: update(m, gf1))
        for c in done:
            c.wait_send()

    hh, hl = big.at[0, pl.ds(0, 2 * N)], big.at[0, pl.ds(2 * N, 2 * N)]
    p3h, p3l = big.at[1, pl.ds(0, 2 * N)], big.at[1, pl.ds(2 * N, 2 * N)]
    p1h, p1l = big.at[2, pl.ds(0, 2 * N)], big.at[2, pl.ds(2 * N, 2 * N)]

    @pl.loop(0, 4)
    def _(i):
        rows = pl.ds(pl.multiple_of(i * 256, 256), 256)
        ah, al = kh[rows, :], kl[rows, :]
        gate = mm3(ah, al, wh[0], wl[0])
        upper = mm3(ah, al, wh[1], wl[1])
        back = mm3(yh[rows, :], yl[rows, :], wh[2], wl[2])
        sigma = jax.nn.sigmoid(gate)
        active = gate * sigma
        hh[rows, :], hl[rows, :] = split(active * upper)
        p3h[rows, :], p3l[rows, :] = split(back * active)
        p1h[rows, :], p1l[rows, :] = split(back * upper * sigma * (1.0 + gate * (1.0 - sigma)))

    def product(m, lth, ltl, rh, rl):
        @pl.loop(0, 4)
        def _(i):
            rows = pl.ds(pl.multiple_of(i * 128, 128), 128)
            gp[m, rows, :] = mm3(lth[rows, :], ltl[rows, :], rh[...], rl[...])

    live = {}

    def begin(m):
        live[m] = [whole(m, s) for s in range(2)]
        for g in live[m]:
            next(g)

    def advance(m):
        for g in live[m]:
            next(g)

    product(1, kth, ktl, p3h, p3l)
    begin(1)
    product(0, kth, ktl, p1h, p1l)
    begin(0)
    advance(1)
    product(2, yth, ytl, hh, hl)
    begin(2)
    drive(live, lambda m: update(m, gf))

    @pl.when(block == 0)
    def _():
        project_q()

    def apply(load, store):
        @pl.loop(0, 2)
        def _(i):
            rows = pl.ds(pl.multiple_of(i * 256, 256), 256)
            ah, al = split(load(rows))
            gate = mm3(ah, al, wh[0], wl[0])
            upper = mm3(ah, al, wh[1], wl[1])
            bh, bl = split(gate * jax.nn.sigmoid(gate) * upper)
            store(rows, normalize(mm3_nt(bh, bl, wh[2], wl[2])).astype(bf16))

    def keep_theirs(rows, v):
        o_mine[rows, :] = v.astype(f32)

    def keep_mine(rows, v):
        o_all[rows, mine] = v

    swaps[2].wait_recv()
    apply(lambda r: q_got[r, :], keep_theirs)
    out = rcopy(o_mine, o_got, ex_s.at[3], ex_r.at[3], partner)
    out.start()
    apply(lambda r: qm[r, :], keep_mine)
    for c in sent:
        c.wait_send()
    load_wo.wait()
    out.wait_recv()
    o_all[:, theirs] = o_got[...].astype(bf16)

    own_half = pl.ds(pl.multiple_of(head * 2 * N, 2 * N), 2 * N)
    far_half = pl.ds(pl.multiple_of((1 - head) * 2 * N, 2 * N), 2 * N)

    def piece(j):
        return pl.ds(0, 2), pl.ds(pl.multiple_of(j * 32, 32), 32)

    def direct(j):
        c, r = piece(j)
        return rcopy(gp.at[c, r], p_got.at[c, r], pt_s.at[j], pt_r.at[j], other_head)

    def first_leg(j, device):
        c, r = piece(j)
        return rcopy(gp.at[c, r], gf1.at[c, r], rl_s.at[j], rl_r.at[j], device)

    def second_leg(j, device):
        c, r = piece(j)
        return rcopy(gf1.at[c, r], p_got.at[c, r], pt_s.at[j], pt_r.at[j], device)

    @pl.loop(0, 4)
    def _(i):
        rows = pl.ds(pl.multiple_of(i * 128, 128), 128)
        v = dot(o_all[rows, :], wo[:, far_half])
        gp[0, rows, :] = v[:, :N]
        gp[1, rows, :] = v[:, N:]

        @pl.when(block == 0)
        def _():
            for j in range(4):
                direct(i * 4 + j).start()

        @pl.when(block == 1)
        def _():
            for j in range(2):
                first_leg(i * 4 + 2 * j, other_block).start()
                first_leg(i * 4 + 2 * j + 1, diagonal).start()

    @pl.loop(0, 4)
    def _(i):
        rows = pl.ds(pl.multiple_of(i * 128, 128), 128)
        v = dot(o_all[rows, :], wo[:, own_half])
        w[0, rows, :] = v[:, :N]
        w[1, rows, :] = v[:, N:]

    @pl.loop(0, 16)
    def _(j):
        direct(j).wait_recv()
        _, rows = piece(j)
        for half in range(2):
            v = w[half, rows, :] + p_got[half, rows, :]
            o_ref[rows, pl.ds(half * N, N)] = v.astype(bf16)

    @pl.when(block == 0)
    def _():
        @pl.loop(0, 16)
        def _(j):
            direct(j).wait_send()

        @pl.loop(0, 8)
        def _(j):
            first_leg(2 * j, other_block).wait_recv()
            second_leg(2 * j, diagonal).start()
            first_leg(2 * j + 1, diagonal).wait_recv()
            second_leg(2 * j + 1, other_block).start()

        @pl.loop(0, 16)
        def _(j):
            second_leg(j, diagonal).wait_send()

    @pl.when(block == 1)
    def _():
        @pl.loop(0, 16)
        def _(j):
            first_leg(j, diagonal).wait_send()

    for c in swaps + [out]:
        c.wait_send()

    @pl.when(block == 0)
    def _():
        for m in range(3):
            for s in range(2):
                shard(m, s).wait_send()


def chain(tokens, weight, rates, fast_init, output_weight):
    dma = pltpu.SemaphoreType.DMA
    square = lambda n, t: pltpu.VMEM((n, N, N), t)
    tall = pltpu.VMEM((2 * N, N), bf16)
    wide = pltpu.VMEM((N, 2 * N), bf16)
    part = pltpu.VMEM((N, N), f32)
    vmem = pl.BlockSpec(memory_space=pltpu.VMEM)
    hbm = pl.BlockSpec(memory_space=pl.ANY)
    return pl.pallas_call(
        chain_kernel,
        out_shape=jax.ShapeDtypeStruct((N, 2 * N), bf16),
        in_specs=[hbm, hbm, vmem, hbm, hbm],
        out_specs=vmem,
        scratch_shapes=[
            pltpu.VMEM((N, 4 * N), bf16), pltpu.VMEM((2 * N, 4 * N), bf16), square(3, bf16),
            part, part, part, part, part, part, part, part, part,
            pltpu.VMEM((N, 2 * N), bf16), square(2, f32),
            tall, tall, wide, wide, tall, tall, wide, wide, pltpu.VMEM((3, 4 * N, N), bf16),
            square(3, f32), square(3, bf16), square(3, bf16), pltpu.VMEM((3, 1, N), f32),
            square(3, f32), square(3, f32), square(3, f32),
            pltpu.VMEM((3, 2, 6, 32, N), f32), pltpu.VMEM((3, 2, 6, 8, N), f32),
            dma((3, 2, 2, 6)), dma((3, 2, 2, 6)),
            dma((3, 2, 2, 4)), dma((3, 2, 2, 4)),
            dma((3, 2, 2, 4)), dma((3, 2, 2, 4)),
            dma((3, 2)), dma((3, 2)),
            dma((4,)), dma((4,)),
            dma((16,)), dma((16,)), dma((16,)), dma((16,)), dma((3,)), dma((3,)),
        ],
        compiler_params=pltpu.CompilerParams(
            collective_id=0, has_side_effects=True, vmem_limit_bytes=62 * 1024 * 1024
        ),
    )(tokens, weight, rates, fast_init, output_weight)


def body(tokens, input_weight, rate_weight, fast_init, output_weight):
    flat = tokens[0]
    rates = jax.nn.softplus(dot(flat, rate_weight))
    mixed = chain(flat, jnp.transpose(input_weight, (1, 0, 2)), rates, fast_init, output_weight)
    return mixed[None]


def solution(mesh):
    placed = (
        P("block", "tok", None),
        P(None, None, "head"),
        P(None, "head"),
        P("head", None, None, None),
        P("head", None),
    )
    return jax.shard_map(
        body, mesh=mesh, in_specs=placed, out_specs=P("block", "tok", "head"), check_vma=False
    )
```

```python
import jax
import jax.numpy as jnp
from jax import lax
from jax.experimental import pallas as pl
from jax.experimental.pallas import tpu as pltpu
from jax.sharding import PartitionSpec as P

epsilon = 1e-06
step_size = 0.03
MESH = pl.DeviceIdType.MESH
f32 = jnp.float32
bf16 = jnp.bfloat16
N = 512
ORDER = (1, 0, 2)


def split(x):
    hi = x.astype(bf16)
    return hi, (x - hi.astype(f32)).astype(bf16)


def dot(a, b):
    return jnp.dot(a, b, preferred_element_type=f32)


def mm3(ah, al, bh, bl):
    return dot(ah, bh) + (dot(ah, bl) + dot(al, bh))


def dot_nt(a, b):
    return lax.dot_general(a, b, (((1,), (1,)), ((), ())), preferred_element_type=f32)


def mm3_nt(ah, al, bh, bl):
    return dot_nt(ah, bh) + (dot_nt(ah, bl) + dot_nt(al, bh))


def normalize(v):
    return v * (1.0 / jnp.sqrt(jnp.mean(v * v, axis=-1, keepdims=True) + epsilon))


def chain_kernel(
    tok_hbm, wi_hbm, rate_ref, w0_hbm, wo_hbm, o_ref,
    tok_v, wo, w0, ks, ys, qs, qm, k_got, y_got, q_got, o_mine, o_got, o_all, p_got,
    kh, kl, kth, ktl, yh, yl, yth, ytl, big,
    w, wh, wl, r0, gp, gf, gf1, r1, r2,
    rs_s, rs_r, ag_s, ag_r, a1_s, a1_r, sh_s, sh_r, ex_s, ex_r,
    pt_s, pt_r, rl_s, rl_r, in_s, wi_s,
):
    tok = lax.axis_index("tok")
    block = lax.axis_index("block")
    head = lax.axis_index("head")
    core = lax.rem(tok, 2)
    chip = lax.div(tok, 2)
    x = lax.rem(chip, 4)
    z = lax.div(chip, 4)

    def at_x(d):
        return {"tok": (z * 4 + lax.rem(x + d + 4, 4)) * 2 + core}

    def at_z(d):
        return {"tok": (lax.rem(z + d + 4, 4) * 4 + x) * 2 + core}

    partner = {"tok": chip * 2 + (1 - core)}
    other_block = {"block": 1 - block}
    diagonal = {"block": 1 - block, "head": 1 - head}
    other_head = {"head": 1 - head}

    mine = pl.ds(pl.multiple_of(core * N, N), N)
    theirs = pl.ds(pl.multiple_of((1 - core) * N, N), N)

    SEQ = ((1, theirs), (2, theirs), (1, mine), (2, mine), (0, theirs), (0, mine))

    def weights(n):
        part, columns = SEQ[n]
        return pltpu.make_async_copy(wi_hbm.at[part, :, columns], big.at[n % 3], wi_s.at[n % 3])

    load_tok = pltpu.make_async_copy(tok_hbm, tok_v, in_s.at[0])
    load_w0 = pltpu.make_async_copy(w0_hbm.at[core], w0, in_s.at[1])
    load_wo = pltpu.make_async_copy(wo_hbm, wo, in_s.at[2])
    load_tok.start()
    weights(0).start()
    weights(1).start()
    weights(2).start()
    load_w0.start()
    load_wo.start()

    barrier = pltpu.get_barrier_semaphore()
    everyone = (
        partner, at_x(1), at_x(-1), at_z(1), at_z(-1), other_block, diagonal, other_head
    )
    for device in everyone:
        pl.semaphore_signal(barrier, inc=1, device_id=device, device_id_type=MESH)
    pl.semaphore_wait(barrier, len(everyone))

    def rcopy(src, dst, ss, rs, device):
        return pltpu.make_async_remote_copy(
            src_ref=src, dst_ref=dst, send_sem=ss, recv_sem=rs,
            device_id=device, device_id_type=MESH,
        )

    swaps = [
        rcopy(src, dst, ex_s.at[n], ex_r.at[n], partner)
        for n, (src, dst) in enumerate(((ks, k_got), (ys, y_got), (qs, q_got)))
    ]

    def project(n, finish):
        weights(n).wait()

        @pl.loop(0, 2)
        def _(i):
            rows = pl.ds(pl.multiple_of(i * 256, 256), 256)
            finish(i * 256, rows, dot(tok_v[rows, :], big[n % 3]))

    def rates(rows, which):
        r = jax.nn.softplus(dot_nt(tok_v[rows, :], rate_ref[...]))
        return jnp.where(which == 0, r[:, 0:1], r[:, 1:2])

    def prepare(base, rows, v, h_ref, l_ref, th_ref, tl_ref):
        hi, lo = split(v)
        to = pl.ds(pl.multiple_of(base, 256), 256)
        h_ref[to, :] = hi
        l_ref[to, :] = lo
        th_ref[:, to] = hi.T
        tl_ref[:, to] = lo.T

    def put(ref, f):
        def finish(base, rows, v):
            ref[rows, :] = f(rows, v)

        return finish

    load_tok.wait()
    project(0, put(ks, lambda r, v: normalize(v)))
    swaps[0].start()
    weights(3).start()
    project(1, put(ys, lambda r, v: v * rates(r, 1 - core)))
    swaps[1].start()
    project(2, lambda b, r, v: prepare(b, r, normalize(v), kh, kl, kth, ktl))
    project(3, lambda b, r, v: prepare(b, r, v * rates(r, core), yh, yl, yth, ytl))

    def project_q():
        weights(4).start()
        weights(5).start()
        project(4, put(qs, lambda r, v: normalize(v)))
        swaps[2].start()
        project(5, put(qm, lambda r, v: normalize(v)))

    load_w0.wait()
    for m in range(3):
        start = w0[m].astype(f32)
        w[m] = start
        wh[m], wl[m] = split(start)
        r0[m] = jnp.sqrt(jnp.mean(start * start, axis=0, keepdims=True))

    def prepare_got(got, h_ref, l_ref, th_ref, tl_ref):
        @pl.loop(0, 2)
        def _(i):
            rows = pl.ds(pl.multiple_of(i * 256, 256), 256)
            prepare(N + i * 256, rows, got[rows, :], h_ref, l_ref, th_ref, tl_ref)

    swaps[0].wait_recv()
    prepare_got(k_got, kh, kl, kth, ktl)
    swaps[1].wait_recv()
    prepare_got(y_got, yh, yl, yth, ytl)

    def rows_of(s, j1, j2=None, off=0, count=64):
        at = s * 256 + j1 * 64 + off
        if j2 is not None:
            at = at + j2 * 16
        return pl.ds(pl.multiple_of(at, 8), count)

    def reduce_stage(m, piece, n, got, store, i, go, ss, rs, sent):
        src = gp.at[m]
        nxt, prv, far = lax.rem(i + 1, 4), lax.rem(i + 3, 4), lax.rem(i + 2, 4)
        right, left = go(1), go(-1)
        c0 = rcopy(src.at[piece(far, 0, n)], got.at[0], ss.at[0], rs.at[0], right)
        c1 = rcopy(src.at[piece(far, n, n)], got.at[1], ss.at[1], rs.at[1], left)
        c2 = rcopy(src.at[piece(nxt, n, n)], got.at[2], ss.at[2], rs.at[2], right)
        c3 = rcopy(src.at[piece(prv, 0, n)], got.at[3], ss.at[3], rs.at[3], left)
        for c in (c0, c1, c2, c3):
            c.start()
        yield
        c0.wait_recv()
        got[0] = got[0] + gp[m, piece(nxt, 0, n), :]
        c4 = rcopy(got.at[0], got.at[4], ss.at[4], rs.at[4], right)
        c4.start()
        c1.wait_recv()
        got[1] = got[1] + gp[m, piece(prv, n, n), :]
        c5 = rcopy(got.at[1], got.at[5], ss.at[5], rs.at[5], left)
        c5.start()
        yield
        for c in (c2, c3, c4, c5):
            c.wait_recv()
        store(0, gp[m, piece(i, 0, n), :] + got[3] + got[4])
        store(n, gp[m, piece(i, n, n), :] + got[2] + got[5])
        sent.extend((c0, c1, c2, c3, c4, c5))

    def gather_stage(buf, piece, n, i, go, ss, rs, done):
        nxt, prv, far = lax.rem(i + 1, 4), lax.rem(i + 3, 4), lax.rem(i + 2, 4)
        right, left = go(1), go(-1)

        def send(k, rows, device):
            return rcopy(buf.at[rows], buf.at[rows], ss.at[k], rs.at[k], device)

        c0 = send(0, piece(i, 0, 2 * n), right)
        c1 = send(1, piece(i, 0, 2 * n), left)
        c0.start()
        c1.start()
        yield
        send(0, piece(prv, 0, 2 * n), right).wait_recv()
        c2 = send(2, piece(prv, 0, n), right)
        c2.start()
        send(1, piece(nxt, 0, 2 * n), left).wait_recv()
        c3 = send(3, piece(nxt, n, n), left)
        c3.start()
        yield
        send(2, piece(far, 0, n), right).wait_recv()
        send(3, piece(far, n, n), left).wait_recv()
        done.extend((c0, c1, c2, c3))

    axes = ((x, at_x, z, at_z), (z, at_z, x, at_x))

    def gather(buf, m, s, ss, rs, done):
        i1, go1, i2, go2 = axes[s]
        yield from gather_stage(
            buf.at[m], lambda j, o, c: rows_of(s, i1, j, o, c), 8, i2, go2,
            ss.at[m, s, 0], rs.at[m, s, 0], done,
        )
        yield from gather_stage(
            buf.at[m], lambda j, o, c: rows_of(s, j, None, o, c), 32, i1, go1,
            ss.at[m, s, 1], rs.at[m, s, 1], done,
        )

    def shard(m, s):
        i1, _, i2, _ = axes[s]
        rows = rows_of(s, i1, i2, 0, 16)
        return rcopy(gf.at[m, rows], gf1.at[m, rows], sh_s.at[m, s], sh_r.at[m, s], other_block)

    def reduce(m, s, sent):
        i1, go1, i2, go2 = axes[s]

        def store1(o, v):
            gp[m, rows_of(s, i1, None, o, 32), :] = v

        def store2(o, v):
            gf[m, rows_of(s, i1, i2, o, 8), :] = v

        yield from reduce_stage(
            m, lambda j, o, c: rows_of(s, j, None, o, c), 32, r1.at[m, s], store1, i1, go1,
            rs_s.at[m, s, 0], rs_r.at[m, s, 0], sent,
        )
        yield from reduce_stage(
            m, lambda j, o, c: rows_of(s, i1, j, o, c), 8, r2.at[m, s], store2, i2, go2,
            rs_s.at[m, s, 1], rs_r.at[m, s, 1], sent,
        )

    def first_block(m, s, sent):
        yield from reduce(m, s, sent)
        shard(m, s).start()
        sent.append(shard(m, s))

    def last_block(m, s, sent):
        yield from reduce(m, s, sent)
        yield from gather(gf, m, s, ag_s, ag_r, sent)

    def update(m, g_ref):
        def rows_at(i):
            return pl.ds(pl.multiple_of(i * 64, 64), 64)

        def squares(i, total):
            g = g_ref[m, rows_at(i), :]
            return total + jnp.sum(g * g, axis=0, keepdims=True)

        total = jnp.sum(lax.fori_loop(0, 8, squares, jnp.zeros((1, N), f32)), axis=1, keepdims=True)
        scale = step_size / jnp.sqrt(total / (N * N) + epsilon)

        def move(i, column):
            rows = rows_at(i)
            moved = w[m, rows, :] + g_ref[m, rows, :] * scale
            w[m, rows, :] = moved
            return column + jnp.sum(moved * moved, axis=0, keepdims=True)

        column = lax.fori_loop(0, 8, move, jnp.zeros((1, N), f32)) / N
        factor = r0[m] / jnp.sqrt(column + epsilon)

        @pl.loop(0, 8)
        def _(i):
            rows = rows_at(i)
            fresh = w[m, rows, :] * factor
            w[m, rows, :] = fresh
            wh[m, rows, :], wl[m, rows, :] = split(fresh)

    def drive(streams, finish):
        left = {m: list(streams[m]) for m in streams}
        while left:
            for m in [m for m in ORDER if m in left]:
                still = []
                for g in left[m]:
                    try:
                        next(g)
                        still.append(g)
                    except StopIteration:
                        pass
                left[m] = still
                if not still:
                    del left[m]
                    finish(m)

    @pl.when(block == 1)
    def _():
        project_q()
        done = []

        def first(m, s):
            shard(m, s).wait_recv()
            yield from gather(gf1, m, s, a1_s, a1_r, done)

        drive({m: [first(m, s) for s in range(2)] for m in range(3)}, lambda m: update(m, gf1))
        for c in done:
            c.wait_send()

    hh, hl = big.at[0, pl.ds(0, 2 * N)], big.at[0, pl.ds(2 * N, 2 * N)]
    p3h, p3l = big.at[1, pl.ds(0, 2 * N)], big.at[1, pl.ds(2 * N, 2 * N)]
    p1h, p1l = big.at[2, pl.ds(0, 2 * N)], big.at[2, pl.ds(2 * N, 2 * N)]

    @pl.loop(0, 4)
    def _(i):
        rows = pl.ds(pl.multiple_of(i * 256, 256), 256)
        ah, al = kh[rows, :], kl[rows, :]
        gate = mm3(ah, al, wh[0], wl[0])
        upper = mm3(ah, al, wh[1], wl[1])
        back = mm3(yh[rows, :], yl[rows, :], wh[2], wl[2])
        sigma = jax.nn.sigmoid(gate)
        active = gate * sigma
        hh[rows, :], hl[rows, :] = split(active * upper)
        p3h[rows, :], p3l[rows, :] = split(back * active)
        p1h[rows, :], p1l[rows, :] = split(back * upper * sigma * (1.0 + gate * (1.0 - sigma)))

    def product(m, lth, ltl, rh, rl):
        @pl.loop(0, 4)
        def _(i):
            rows = pl.ds(pl.multiple_of(i * 128, 128), 128)
            gp[m, rows, :] = mm3(lth[rows, :], ltl[rows, :], rh[...], rl[...])

    def exchange(stream, finish, sent):
        live = {}

        def begin(m):
            live[m] = [stream(m, s, sent) for s in range(2)]
            for g in live[m]:
                next(g)

        def advance(m):
            for g in live[m]:
                next(g)

        product(1, kth, ktl, p3h, p3l)
        begin(1)
        product(0, kth, ktl, p1h, p1l)
        begin(0)
        advance(1)
        product(2, yth, ytl, hh, hl)
        begin(2)
        drive(live, finish)

    @pl.when(block == 0)
    def _():
        sent = []
        exchange(first_block, lambda m: None, sent)
        drive(
            {m: [gather(gf, m, s, ag_s, ag_r, sent) for s in range(2)] for m in range(3)},
            lambda m: update(m, gf),
        )
        for c in sent:
            c.wait_send()

    @pl.when(block == 1)
    def _():
        sent = []
        exchange(last_block, lambda m: update(m, gf), sent)
        for c in sent:
            c.wait_send()

    @pl.when(block == 0)
    def _():
        project_q()

    def apply(load, store):
        @pl.loop(0, 2)
        def _(i):
            rows = pl.ds(pl.multiple_of(i * 256, 256), 256)
            ah, al = split(load(rows))
            gate = mm3(ah, al, wh[0], wl[0])
            upper = mm3(ah, al, wh[1], wl[1])
            bh, bl = split(gate * jax.nn.sigmoid(gate) * upper)
            store(rows, normalize(mm3_nt(bh, bl, wh[2], wl[2])).astype(bf16))

    def keep_theirs(rows, v):
        o_mine[rows, :] = v.astype(f32)

    def keep_mine(rows, v):
        o_all[rows, mine] = v

    swaps[2].wait_recv()
    apply(lambda r: q_got[r, :], keep_theirs)
    out = rcopy(o_mine, o_got, ex_s.at[3], ex_r.at[3], partner)
    out.start()
    apply(lambda r: qm[r, :], keep_mine)
    load_wo.wait()
    out.wait_recv()
    o_all[:, theirs] = o_got[...].astype(bf16)

    own_half = pl.ds(pl.multiple_of(head * 2 * N, 2 * N), 2 * N)
    far_half = pl.ds(pl.multiple_of((1 - head) * 2 * N, 2 * N), 2 * N)

    def piece(j):
        return pl.ds(0, 2), pl.ds(pl.multiple_of(j * 32, 32), 32)

    def direct(j):
        c, r = piece(j)
        return rcopy(gp.at[c, r], p_got.at[c, r], pt_s.at[j], pt_r.at[j], other_head)

    def first_leg(j, device):
        c, r = piece(j)
        return rcopy(gp.at[c, r], gf1.at[c, r], rl_s.at[j], rl_r.at[j], device)

    def second_leg(j, device):
        c, r = piece(j)
        return rcopy(gf1.at[c, r], p_got.at[c, r], pt_s.at[j], pt_r.at[j], device)

    @pl.loop(0, 4)
    def _(i):
        rows = pl.ds(pl.multiple_of(i * 128, 128), 128)
        v = dot(o_all[rows, :], wo[:, far_half])
        gp[0, rows, :] = v[:, :N]
        gp[1, rows, :] = v[:, N:]

        @pl.when(block == 0)
        def _():
            for j in range(4):
                direct(i * 4 + j).start()

        @pl.when(block == 1)
        def _():
            for j in range(2):
                first_leg(i * 4 + 2 * j, other_block).start()
                first_leg(i * 4 + 2 * j + 1, diagonal).start()

    @pl.loop(0, 4)
    def _(i):
        rows = pl.ds(pl.multiple_of(i * 128, 128), 128)
        v = dot(o_all[rows, :], wo[:, own_half])
        w[0, rows, :] = v[:, :N]
        w[1, rows, :] = v[:, N:]

    @pl.loop(0, 16)
    def _(j):
        direct(j).wait_recv()
        _, rows = piece(j)
        for half in range(2):
            v = w[half, rows, :] + p_got[half, rows, :]
            o_ref[rows, pl.ds(half * N, N)] = v.astype(bf16)

    @pl.when(block == 0)
    def _():
        @pl.loop(0, 16)
        def _(j):
            direct(j).wait_send()

        @pl.loop(0, 8)
        def _(j):
            first_leg(2 * j, other_block).wait_recv()
            second_leg(2 * j, diagonal).start()
            first_leg(2 * j + 1, diagonal).wait_recv()
            second_leg(2 * j + 1, other_block).start()

        @pl.loop(0, 16)
        def _(j):
            second_leg(j, diagonal).wait_send()

    @pl.when(block == 1)
    def _():
        @pl.loop(0, 16)
        def _(j):
            first_leg(j, diagonal).wait_send()

    for c in swaps + [out]:
        c.wait_send()


def chain(tokens, weight, rate_weight, fast_init, output_weight):
    dma = pltpu.SemaphoreType.DMA
    square = lambda n, t: pltpu.VMEM((n, N, N), t)
    tall = pltpu.VMEM((2 * N, N), bf16)
    wide = pltpu.VMEM((N, 2 * N), bf16)
    part = pltpu.VMEM((N, N), f32)
    vmem = pl.BlockSpec(memory_space=pltpu.VMEM)
    hbm = pl.BlockSpec(memory_space=pl.ANY)
    return pl.pallas_call(
        chain_kernel,
        out_shape=jax.ShapeDtypeStruct((N, 2 * N), bf16),
        in_specs=[hbm, hbm, vmem, hbm, hbm],
        out_specs=vmem,
        scratch_shapes=[
            pltpu.VMEM((N, 4 * N), bf16), pltpu.VMEM((2 * N, 4 * N), bf16), square(3, bf16),
            part, part, part, part, part, part, part, part, part,
            pltpu.VMEM((N, 2 * N), bf16), square(2, f32),
            tall, tall, wide, wide, tall, tall, wide, wide, pltpu.VMEM((3, 4 * N, N), bf16),
            square(3, f32), square(3, bf16), square(3, bf16), pltpu.VMEM((3, 1, N), f32),
            square(3, f32), square(3, f32), square(3, f32),
            pltpu.VMEM((3, 2, 6, 32, N), f32), pltpu.VMEM((3, 2, 6, 8, N), f32),
            dma((3, 2, 2, 6)), dma((3, 2, 2, 6)),
            dma((3, 2, 2, 4)), dma((3, 2, 2, 4)),
            dma((3, 2, 2, 4)), dma((3, 2, 2, 4)),
            dma((3, 2)), dma((3, 2)),
            dma((4,)), dma((4,)),
            dma((16,)), dma((16,)), dma((16,)), dma((16,)), dma((3,)), dma((3,)),
        ],
        compiler_params=pltpu.CompilerParams(
            collective_id=0, has_side_effects=True, vmem_limit_bytes=62 * 1024 * 1024
        ),
    )(tokens, weight, rate_weight, fast_init, output_weight)


def body(tokens, input_weight, rate_weight, fast_init, output_weight):
    flat = tokens[0]
    mixed = chain(
        flat, jnp.transpose(input_weight, (1, 0, 2)), rate_weight.T, fast_init, output_weight
    )
    return mixed[None]


def solution(mesh):
    placed = (
        P("block", "tok", None),
        P(None, None, "head"),
        P(None, "head"),
        P("head", None, None, None),
        P("head", None),
    )
    return jax.shard_map(
        body, mesh=mesh, in_specs=placed, out_specs=P("block", "tok", "head"), check_vma=False
    )
```

```python
import jax
import jax.numpy as jnp
from jax import lax
from jax.experimental import pallas as pl
from jax.experimental.pallas import tpu as pltpu
from jax.sharding import PartitionSpec as P

epsilon = 1e-06
step_size = 0.03
MESH = pl.DeviceIdType.MESH
f32 = jnp.float32
bf16 = jnp.bfloat16
N = 512
ORDER = (1, 0, 2)


def split(x):
    hi = x.astype(bf16)
    return hi, (x - hi.astype(f32)).astype(bf16)


def dot(a, b):
    return jnp.dot(a, b, preferred_element_type=f32)


def mm3(ah, al, bh, bl):
    return dot(ah, bh) + (dot(ah, bl) + dot(al, bh))


def dot_nt(a, b):
    return lax.dot_general(a, b, (((1,), (1,)), ((), ())), preferred_element_type=f32)


def mm3_nt(ah, al, bh, bl):
    return dot_nt(ah, bh) + (dot_nt(ah, bl) + dot_nt(al, bh))


def normalize(v):
    return v * (1.0 / jnp.sqrt(jnp.mean(v * v, axis=-1, keepdims=True) + epsilon))


def chain_kernel(
    tok_hbm, wi_hbm, rate_ref, w0_hbm, wo_hbm, o_ref,
    tok_v, wo, w0, ks, ys, qs, qm, k_got, y_got, q_got, o_got, o_all, o_far, seed, seed32, wog, wos,
    kh, kl, kth, ktl, yh, yl, yth, ytl, big,
    w, wh, wl, r0, gp, gf, gf1, r1, r2,
    rs_s, rs_r, ag_s, ag_r, a1_s, a1_r, sh_s, sh_r, ex_s, ex_r,
    pt_s, pt_r, rl_s, rl_r, sd_s, sd_r, wg_s, wg_r, in_s, wi_s,
):
    tok = lax.axis_index("tok")
    block = lax.axis_index("block")
    head = lax.axis_index("head")
    core = lax.rem(tok, 2)
    chip = lax.div(tok, 2)
    x = lax.rem(chip, 4)
    z = lax.div(chip, 4)

    def at_x(d):
        return {"tok": (z * 4 + lax.rem(x + d + 4, 4)) * 2 + core}

    def at_z(d):
        return {"tok": (lax.rem(z + d + 4, 4) * 4 + x) * 2 + core}

    partner = {"tok": chip * 2 + (1 - core)}
    other_block = {"block": 1 - block}
    diagonal = {"block": 1 - block, "head": 1 - head}
    other_head = {"head": 1 - head}

    mine = pl.ds(pl.multiple_of(core * N, N), N)
    theirs = pl.ds(pl.multiple_of((1 - core) * N, N), N)

    SEQ = ((1, theirs), (2, theirs), (1, mine), (2, mine), (0, theirs), (0, mine))

    def weights(n):
        part, columns = SEQ[n]
        return pltpu.make_async_copy(wi_hbm.at[part, :, columns], big.at[n % 3], wi_s.at[n % 3])

    load_tok = pltpu.make_async_copy(tok_hbm, tok_v, in_s.at[0])
    load_w0 = pltpu.make_async_copy(w0_hbm.at[core], w0, in_s.at[1])
    own_half = pl.ds(pl.multiple_of(head * 2 * N, 2 * N), 2 * N)
    far_half = pl.ds(pl.multiple_of((1 - head) * 2 * N, 2 * N), 2 * N)
    load_wo = [
        pltpu.make_async_copy(wo_hbm.at[pl.ds(n * N, N), own_half], wo.at[n], in_s.at[2 + n])
        for n in range(2)
    ]
    seed_at = ((x * 64 + z * 16), (256 + z * 64 + x * 16))
    load_seed = [
        pltpu.make_async_copy(
            wo_hbm.at[pl.ds(pl.multiple_of(core * N + seed_at[n], 16), 16), far_half],
            seed.at[n], in_s.at[4 + n],
        )
        for n in range(2)
    ]
    for copy in load_seed:
        copy.start()
    load_tok.start()
    weights(0).start()
    weights(1).start()
    weights(2).start()
    load_w0.start()
    for copy in load_wo:
        copy.start()

    barrier = pltpu.get_barrier_semaphore()
    everyone = (
        partner, at_x(1), at_x(-1), at_z(1), at_z(-1), other_block, diagonal, other_head,
        {**other_block, **partner}, {**diagonal, **partner}, {**other_head, **partner},
    )
    for device in everyone:
        pl.semaphore_signal(barrier, inc=1, device_id=device, device_id_type=MESH)
    pl.semaphore_wait(barrier, len(everyone))

    def rcopy(src, dst, ss, rs, device):
        return pltpu.make_async_remote_copy(
            src_ref=src, dst_ref=dst, send_sem=ss, recv_sem=rs,
            device_id=device, device_id_type=MESH,
        )

    swaps = [
        rcopy(src, dst, ex_s.at[n], ex_r.at[n], partner)
        for n, (src, dst) in enumerate(((ks, k_got), (ys, y_got), (qs, q_got)))
    ]

    def project(n, finish):
        weights(n).wait()

        @pl.loop(0, 2)
        def _(i):
            rows = pl.ds(pl.multiple_of(i * 256, 256), 256)
            finish(i * 256, rows, dot(tok_v[rows, :], big[n % 3]))

    def rates(rows, which):
        r = jax.nn.softplus(dot_nt(tok_v[rows, :], rate_ref[...]))
        return jnp.where(which == 0, r[:, 0:1], r[:, 1:2])

    def prepare(base, rows, v, h_ref, l_ref, th_ref, tl_ref):
        hi, lo = split(v)
        to = pl.ds(pl.multiple_of(base, 256), 256)
        h_ref[to, :] = hi
        l_ref[to, :] = lo
        th_ref[:, to] = hi.T
        tl_ref[:, to] = lo.T

    def put(ref, f):
        def finish(base, rows, v):
            ref[rows, :] = f(rows, v)

        return finish

    def rows_of(s, j1, j2=None, off=0, count=64):
        at = s * 256 + j1 * 64 + off
        if j2 is not None:
            at = at + j2 * 16
        return pl.ds(pl.multiple_of(at, 8), count)

    def gather_stage(buf, piece, n, i, go, ss, rs, done):
        nxt, prv, far = lax.rem(i + 1, 4), lax.rem(i + 3, 4), lax.rem(i + 2, 4)
        right, left = go(1), go(-1)

        def send(k, rows, device):
            return rcopy(buf.at[rows], buf.at[rows], ss.at[k], rs.at[k], device)

        c0 = send(0, piece(i, 0, 2 * n), right)
        c1 = send(1, piece(i, 0, 2 * n), left)
        c0.start()
        c1.start()
        yield
        send(0, piece(prv, 0, 2 * n), right).wait_recv()
        c2 = send(2, piece(prv, 0, n), right)
        c2.start()
        send(1, piece(nxt, 0, 2 * n), left).wait_recv()
        c3 = send(3, piece(nxt, n, n), left)
        c3.start()
        yield
        send(2, piece(far, 0, n), right).wait_recv()
        send(3, piece(far, n, n), left).wait_recv()
        done.extend((c0, c1, c2, c3))

    axes = ((x, at_x, z, at_z), (z, at_z, x, at_x))

    def gather(buf, m, s, ss, rs, done):
        i1, go1, i2, go2 = axes[s]
        yield from gather_stage(
            buf.at[m], lambda j, o, c: rows_of(s, i1, j, o, c), 8, i2, go2,
            ss.at[m, s, 0], rs.at[m, s, 0], done,
        )
        yield from gather_stage(
            buf.at[m], lambda j, o, c: rows_of(s, j, None, o, c), 32, i1, go1,
            ss.at[m, s, 1], rs.at[m, s, 1], done,
        )

    SHARDS = tuple((m, n) for m in range(2) for n in range(2))
    seeds = [
        rcopy(
            seed32.at[m, n], wog.at[m, pl.ds(pl.multiple_of(seed_at[n], 16), 16)],
            sd_s.at[m, n], sd_r.at[m, n], diagonal,
        )
        for m, n in SHARDS
    ]
    for copy in load_seed:
        copy.wait()
    for m, n in SHARDS:
        seed32[m, n] = seed[n, :, m * N:(m + 1) * N].astype(f32)
    for copy in seeds:
        copy.start()
    wo_sent = []

    def bring_weights(m, n):
        seeds[m * 2 + n].wait_recv()
        yield from gather(wog, m, n, wg_s, wg_r, wo_sent)

    bringing = [bring_weights(m, n) for m, n in SHARDS]

    def bring():
        for g in bringing:
            next(g, None)

    wo_swap = rcopy(wog, wos, ex_s.at[5], ex_r.at[5], partner)

    load_tok.wait()
    project(0, put(ks, lambda r, v: normalize(v)))
    swaps[0].start()
    weights(3).start()
    bring()
    project(1, put(ys, lambda r, v: v * rates(r, 1 - core)))
    swaps[1].start()
    bring()
    project(2, lambda b, r, v: prepare(b, r, normalize(v), kh, kl, kth, ktl))
    bring()
    project(3, lambda b, r, v: prepare(b, r, v * rates(r, core), yh, yl, yth, ytl))
    bring()

    def project_q():
        weights(4).start()
        weights(5).start()
        project(4, put(qs, lambda r, v: normalize(v)))
        swaps[2].start()
        project(5, put(qm, lambda r, v: normalize(v)))

    load_w0.wait()
    for m in range(3):
        start = w0[m].astype(f32)
        w[m] = start
        wh[m], wl[m] = split(start)
        r0[m] = jnp.sqrt(jnp.mean(start * start, axis=0, keepdims=True))

    def prepare_got(got, h_ref, l_ref, th_ref, tl_ref):
        @pl.loop(0, 2)
        def _(i):
            rows = pl.ds(pl.multiple_of(i * 256, 256), 256)
            prepare(N + i * 256, rows, got[rows, :], h_ref, l_ref, th_ref, tl_ref)

    swaps[0].wait_recv()
    prepare_got(k_got, kh, kl, kth, ktl)
    bring()
    swaps[1].wait_recv()
    prepare_got(y_got, yh, yl, yth, ytl)
    bring()
    wo_swap.start()

    def keep_weights():
        wo_swap.wait_recv()

        @pl.loop(0, 4)
        def _(i):
            rows = pl.ds(pl.multiple_of(i * 128, 128), 128)
            for m in range(2):
                columns = pl.ds(m * N, N)
                wo[2 + core, rows, columns] = wog[m, rows, :].astype(bf16)
                wo[3 - core, rows, columns] = wos[m, rows, :].astype(bf16)

    def reduce_stage(m, piece, n, got, store, i, go, ss, rs, sent):
        src = gp.at[m]
        nxt, prv, far = lax.rem(i + 1, 4), lax.rem(i + 3, 4), lax.rem(i + 2, 4)
        right, left = go(1), go(-1)
        c0 = rcopy(src.at[piece(far, 0, n)], got.at[0], ss.at[0], rs.at[0], right)
        c1 = rcopy(src.at[piece(far, n, n)], got.at[1], ss.at[1], rs.at[1], left)
        c2 = rcopy(src.at[piece(nxt, n, n)], got.at[2], ss.at[2], rs.at[2], right)
        c3 = rcopy(src.at[piece(prv, 0, n)], got.at[3], ss.at[3], rs.at[3], left)
        for c in (c0, c1, c2, c3):
            c.start()
        yield
        c0.wait_recv()
        got[0] = got[0] + gp[m, piece(nxt, 0, n), :]
        c4 = rcopy(got.at[0], got.at[4], ss.at[4], rs.at[4], right)
        c4.start()
        c1.wait_recv()
        got[1] = got[1] + gp[m, piece(prv, n, n), :]
        c5 = rcopy(got.at[1], got.at[5], ss.at[5], rs.at[5], left)
        c5.start()
        yield
        for c in (c2, c3, c4, c5):
            c.wait_recv()
        store(0, gp[m, piece(i, 0, n), :] + got[3] + got[4])
        store(n, gp[m, piece(i, n, n), :] + got[2] + got[5])
        sent.extend((c0, c1, c2, c3, c4, c5))

    def shard(m, s):
        i1, _, i2, _ = axes[s]
        rows = rows_of(s, i1, i2, 0, 16)
        return rcopy(gf.at[m, rows], gf1.at[m, rows], sh_s.at[m, s], sh_r.at[m, s], other_block)

    def reduce(m, s, sent):
        i1, go1, i2, go2 = axes[s]

        def store1(o, v):
            gp[m, rows_of(s, i1, None, o, 32), :] = v

        def store2(o, v):
            gf[m, rows_of(s, i1, i2, o, 8), :] = v

        yield from reduce_stage(
            m, lambda j, o, c: rows_of(s, j, None, o, c), 32, r1.at[m, s], store1, i1, go1,
            rs_s.at[m, s, 0], rs_r.at[m, s, 0], sent,
        )
        yield from reduce_stage(
            m, lambda j, o, c: rows_of(s, i1, j, o, c), 8, r2.at[m, s], store2, i2, go2,
            rs_s.at[m, s, 1], rs_r.at[m, s, 1], sent,
        )

    def first_block(m, s, sent):
        yield from reduce(m, s, sent)
        shard(m, s).start()
        sent.append(shard(m, s))

    def last_block(m, s, sent):
        yield from reduce(m, s, sent)
        yield from gather(gf, m, s, ag_s, ag_r, sent)

    def update(m, g_ref):
        def rows_at(i):
            return pl.ds(pl.multiple_of(i * 64, 64), 64)

        def squares(i, total):
            g = g_ref[m, rows_at(i), :]
            return total + jnp.sum(g * g, axis=0, keepdims=True)

        total = jnp.sum(lax.fori_loop(0, 8, squares, jnp.zeros((1, N), f32)), axis=1, keepdims=True)
        scale = step_size / jnp.sqrt(total / (N * N) + epsilon)

        def move(i, column):
            rows = rows_at(i)
            moved = w[m, rows, :] + g_ref[m, rows, :] * scale
            w[m, rows, :] = moved
            return column + jnp.sum(moved * moved, axis=0, keepdims=True)

        column = lax.fori_loop(0, 8, move, jnp.zeros((1, N), f32)) / N
        factor = r0[m] / jnp.sqrt(column + epsilon)

        @pl.loop(0, 8)
        def _(i):
            rows = rows_at(i)
            fresh = w[m, rows, :] * factor
            w[m, rows, :] = fresh
            wh[m, rows, :], wl[m, rows, :] = split(fresh)

    def drive(streams, finish):
        left = {m: list(streams[m]) for m in streams}
        while left:
            for m in [m for m in ORDER if m in left]:
                still = []
                for g in left[m]:
                    try:
                        next(g)
                        still.append(g)
                    except StopIteration:
                        pass
                left[m] = still
                if not still:
                    del left[m]
                    finish(m)

    @pl.when(block == 1)
    def _():
        project_q()
        keep_weights()
        done = []

        def first(m, s):
            shard(m, s).wait_recv()
            yield from gather(gf1, m, s, a1_s, a1_r, done)

        drive({m: [first(m, s) for s in range(2)] for m in range(3)}, lambda m: update(m, gf1))
        for c in done:
            c.wait_send()

    hh, hl = big.at[0, pl.ds(0, 2 * N)], big.at[0, pl.ds(2 * N, 2 * N)]
    p3h, p3l = big.at[1, pl.ds(0, 2 * N)], big.at[1, pl.ds(2 * N, 2 * N)]
    p1h, p1l = big.at[2, pl.ds(0, 2 * N)], big.at[2, pl.ds(2 * N, 2 * N)]

    @pl.loop(0, 4)
    def _(i):
        rows = pl.ds(pl.multiple_of(i * 256, 256), 256)
        ah, al = kh[rows, :], kl[rows, :]
        gate = mm3(ah, al, wh[0], wl[0])
        upper = mm3(ah, al, wh[1], wl[1])
        back = mm3(yh[rows, :], yl[rows, :], wh[2], wl[2])
        sigma = jax.nn.sigmoid(gate)
        active = gate * sigma
        hh[rows, :], hl[rows, :] = split(active * upper)
        p3h[rows, :], p3l[rows, :] = split(back * active)
        p1h[rows, :], p1l[rows, :] = split(back * upper * sigma * (1.0 + gate * (1.0 - sigma)))

    def product(m, lth, ltl, rh, rl):
        @pl.loop(0, 4)
        def _(i):
            rows = pl.ds(pl.multiple_of(i * 128, 128), 128)
            gp[m, rows, :] = mm3(lth[rows, :], ltl[rows, :], rh[...], rl[...])

    def exchange(stream, finish, sent):
        live = {}

        def begin(m):
            live[m] = [stream(m, s, sent) for s in range(2)]
            for g in live[m]:
                next(g)

        def advance(m):
            for g in live[m]:
                next(g)

        product(1, kth, ktl, p3h, p3l)
        begin(1)
        product(0, kth, ktl, p1h, p1l)
        begin(0)
        advance(1)
        product(2, yth, ytl, hh, hl)
        begin(2)
        drive(live, finish)

    @pl.when(block == 0)
    def _():
        sent = []
        exchange(first_block, lambda m: None, sent)
        live = {m: [gather(gf, m, s, ag_s, ag_r, sent) for s in range(2)] for m in range(3)}
        for m in ORDER:
            for g in live[m]:
                next(g)
        project_q()
        keep_weights()
        drive(live, lambda m: update(m, gf))
        for c in sent:
            c.wait_send()

    @pl.when(block == 1)
    def _():
        sent = []
        exchange(last_block, lambda m: update(m, gf), sent)
        for c in sent:
            c.wait_send()

    def rows_at(j):
        return pl.ds(pl.multiple_of(j * 64, 64), 64)

    receivers = ({"tok": partner["tok"]}, {})

    def direct(t, j):
        r = rows_at(j)
        device = {"head": 1 - head, **receivers[t]}
        return rcopy(gp.at[t, r], o_far.at[core, r], pt_s.at[t, j], pt_r.at[t, j], device)

    def arrival(t, j):
        r = rows_at(j)
        at = o_far.at[1 - core if t == 0 else core, r]
        return rcopy(at, at, pt_s.at[t, j], pt_r.at[t, j], other_head)

    def first_leg(t, j, device):
        r = rows_at(j)
        return rcopy(gp.at[t, r], gf1.at[t, r], rl_s.at[t, j], rl_r.at[t, j], device)

    def second_leg(t, j, device):
        r = rows_at(j)
        return rcopy(
            gf1.at[t, r], o_far.at[core, r], pt_s.at[t, 8 + j], pt_r.at[t, j],
            {**device, **receivers[t]},
        )

    def send_far(t, i):
        @pl.when(block == 0)
        def _():
            for j in range(4):
                direct(t, i * 4 + j).start()

        @pl.when(block == 1)
        def _():
            for j in range(0, 4, 2):
                first_leg(t, i * 4 + j, other_block).start()
                first_leg(t, i * 4 + j + 1, diagonal).start()

    def give(i):
        rows = pl.ds(pl.multiple_of(i * 256, 256), 256)
        return rcopy(gp.at[0, rows], o_got.at[rows], ex_s.at[3 + i], ex_r.at[3 + i], partner)

    def apply(t, q):
        @pl.loop(0, 2)
        def _(i):
            rows = pl.ds(pl.multiple_of(i * 256, 256), 256)
            ah, al = split(q[rows, :])
            gate = mm3(ah, al, wh[0], wl[0])
            upper = mm3(ah, al, wh[1], wl[1])
            bh, bl = split(gate * jax.nn.sigmoid(gate) * upper)
            o = normalize(mm3_nt(bh, bl, wh[2], wl[2])).astype(bf16)
            gp[t, rows, :] = o.astype(f32)
            if t == 1:
                o_all[rows, mine] = o
            send_far(t, i)
            if t == 0:
                give(i).start()

    swaps[2].wait_recv()
    apply(0, q_got)
    apply(1, qm)
    for copy in load_wo:
        copy.wait()
    for i in range(2):
        give(i).wait_recv()
    o_all[:, theirs] = o_got[...].astype(bf16)

    @pl.loop(0, 4)
    def _(i):
        rows = pl.ds(pl.multiple_of(i * 128, 128), 128)
        v = dot(o_all[rows, :N], wo[0]) + dot(o_all[rows, N:], wo[1])
        w[0, rows, :] = v[:, :N]
        w[1, rows, :] = v[:, N:]

    def add_theirs():
        for j in range(8):
            arrival(0, j).wait_recv()

        @pl.loop(0, 4)
        def _(i):
            rows = pl.ds(pl.multiple_of(i * 128, 128), 128)
            v = dot(o_far[1 - core, rows, :].astype(bf16), wo[3 - core])
            w[0, rows, :] = w[0, rows, :] + v[:, :N]
            w[1, rows, :] = w[1, rows, :] + v[:, N:]

    def add_mine(j):
        arrival(1, j).wait_recv()
        rows = rows_at(j)
        v = dot(o_far[core, rows, :].astype(bf16), wo[2 + core])
        o_ref[rows, :N] = (w[0, rows, :] + v[:, :N]).astype(bf16)
        o_ref[rows, N:] = (w[1, rows, :] + v[:, N:]).astype(bf16)

    def relay(t, i):
        first_leg(t, 2 * i, other_block).wait_recv()
        second_leg(t, 2 * i, diagonal).start()
        first_leg(t, 2 * i + 1, diagonal).wait_recv()
        second_leg(t, 2 * i + 1, other_block).start()

    @pl.when(block == 0)
    def _():
        @pl.loop(0, 4)
        def _(i):
            relay(0, i)

        add_theirs()

        @pl.loop(0, 4)
        def _(i):
            relay(1, i)
            add_mine(2 * i)
            add_mine(2 * i + 1)

        for t in range(2):
            @pl.loop(0, 8)
            def _(j):
                direct(t, j).wait_send()
                second_leg(t, j, diagonal).wait_send()

    @pl.when(block == 1)
    def _():
        add_theirs()

        @pl.loop(0, 8)
        def _(j):
            add_mine(j)

        for t in range(2):
            @pl.loop(0, 8)
            def _(j):
                first_leg(t, j, diagonal).wait_send()

    for c in swaps + seeds + wo_sent + [wo_swap, give(0), give(1)]:
        c.wait_send()


def chain(tokens, weight, rate_weight, fast_init, output_weight):
    dma = pltpu.SemaphoreType.DMA
    square = lambda n, t: pltpu.VMEM((n, N, N), t)
    tall = pltpu.VMEM((2 * N, N), bf16)
    wide = pltpu.VMEM((N, 2 * N), bf16)
    part = pltpu.VMEM((N, N), f32)
    vmem = pl.BlockSpec(memory_space=pltpu.VMEM)
    hbm = pl.BlockSpec(memory_space=pl.ANY)
    return pl.pallas_call(
        chain_kernel,
        out_shape=jax.ShapeDtypeStruct((N, 2 * N), bf16),
        in_specs=[hbm, hbm, vmem, hbm, hbm],
        out_specs=vmem,
        scratch_shapes=[
            pltpu.VMEM((N, 4 * N), bf16), pltpu.VMEM((4, N, 2 * N), bf16), square(3, bf16),
            part, part, part, part, part, part, part, part,
            pltpu.VMEM((N, 2 * N), bf16), square(2, f32),
            pltpu.VMEM((2, 16, 2 * N), bf16), pltpu.VMEM((2, 2, 16, N), f32),
            square(2, f32), square(2, f32),
            tall, tall, wide, wide, tall, tall, wide, wide, pltpu.VMEM((3, 4 * N, N), bf16),
            square(3, f32), square(3, bf16), square(3, bf16), pltpu.VMEM((3, 1, N), f32),
            square(3, f32), square(3, f32), square(3, f32),
            pltpu.VMEM((3, 2, 6, 32, N), f32), pltpu.VMEM((3, 2, 6, 8, N), f32),
            dma((3, 2, 2, 6)), dma((3, 2, 2, 6)),
            dma((3, 2, 2, 4)), dma((3, 2, 2, 4)),
            dma((3, 2, 2, 4)), dma((3, 2, 2, 4)),
            dma((3, 2)), dma((3, 2)),
            dma((6,)), dma((6,)),
            dma((2, 16)), dma((2, 8)), dma((2, 8)), dma((2, 8)),
            dma((2, 2)), dma((2, 2)), dma((2, 2, 2, 4)), dma((2, 2, 2, 4)),
            dma((6,)), dma((3,)),
        ],
        compiler_params=pltpu.CompilerParams(
            collective_id=0, has_side_effects=True, vmem_limit_bytes=62 * 1024 * 1024
        ),
    )(tokens, weight, rate_weight, fast_init, output_weight)


def body(tokens, input_weight, rate_weight, fast_init, output_weight):
    flat = tokens[0]
    mixed = chain(
        flat, jnp.transpose(input_weight, (1, 0, 2)), rate_weight.T, fast_init, output_weight
    )
    return mixed[None]


def solution(mesh):
    placed = (
        P("block", "tok", None),
        P(None, None, "head"),
        P(None, "head"),
        P("head", None, None, None),
        P("head", None),
    )
    return jax.shard_map(
        body, mesh=mesh, in_specs=placed, out_specs=P("block", "tok", "head"), check_vma=False
    )
```

```python
import jax
import jax.numpy as jnp
from jax import lax
from jax.experimental import pallas as pl
from jax.experimental.pallas import tpu as pltpu
from jax.sharding import PartitionSpec as P

epsilon = 1e-06
step_size = 0.03
MESH = pl.DeviceIdType.MESH
f32 = jnp.float32
bf16 = jnp.bfloat16
N = 512
ORDER = (1, 0, 2)


def split(x):
    hi = x.astype(bf16)
    return hi, (x - hi.astype(f32)).astype(bf16)


def dot(a, b):
    return jnp.dot(a, b, preferred_element_type=f32)


def mm3(ah, al, bh, bl):
    return dot(ah, bh) + (dot(ah, bl) + dot(al, bh))


def dot_nt(a, b):
    return lax.dot_general(a, b, (((1,), (1,)), ((), ())), preferred_element_type=f32)


def mm3_nt(ah, al, bh, bl):
    return dot_nt(ah, bh) + (dot_nt(ah, bl) + dot_nt(al, bh))


def normalize(v):
    return v * (1.0 / jnp.sqrt(jnp.mean(v * v, axis=-1, keepdims=True) + epsilon))


def chain_kernel(
    tok_hbm, wi_hbm, rate_ref, w0_hbm, wo_hbm, o_ref,
    tok_v, wo, w0, ks, ys, qs, qm, k32, y32, q_got, o_got, o_all, o_far, seed, seed32, wog, wos,
    kth, ktl, yth, ytl, big,
    w, wh, wl, r0, gp, gf, gf1, r1, r2,
    rs_s, rs_r, ag_s, ag_r, a1_s, a1_r, sh_s, sh_r, ex_s, ex_r,
    pt_s, pt_r, rl_s, rl_r, sd_s, sd_r, wg_s, wg_r, in_s, wi_s,
):
    tok = lax.axis_index("tok")
    block = lax.axis_index("block")
    head = lax.axis_index("head")
    core = lax.rem(tok, 2)
    chip = lax.div(tok, 2)
    x = lax.rem(chip, 4)
    z = lax.div(chip, 4)

    def at_x(d):
        return {"tok": (z * 4 + lax.rem(x + d + 4, 4)) * 2 + core}

    def at_z(d):
        return {"tok": (lax.rem(z + d + 4, 4) * 4 + x) * 2 + core}

    partner = {"tok": chip * 2 + (1 - core)}
    other_block = {"block": 1 - block}
    diagonal = {"block": 1 - block, "head": 1 - head}
    other_head = {"head": 1 - head}

    mine = pl.ds(pl.multiple_of(core * N, N), N)
    theirs = pl.ds(pl.multiple_of((1 - core) * N, N), N)

    SEQ = ((1, theirs), (2, theirs), (1, mine), (2, mine), (0, theirs), (0, mine))

    def weights(n):
        part, columns = SEQ[n]
        return pltpu.make_async_copy(wi_hbm.at[part, :, columns], big.at[n % 3], wi_s.at[n % 3])

    load_tok = pltpu.make_async_copy(tok_hbm, tok_v, in_s.at[0])
    load_w0 = pltpu.make_async_copy(w0_hbm.at[core], w0, in_s.at[1])
    own_half = pl.ds(pl.multiple_of(head * 2 * N, 2 * N), 2 * N)
    far_half = pl.ds(pl.multiple_of((1 - head) * 2 * N, 2 * N), 2 * N)
    load_wo = [
        pltpu.make_async_copy(wo_hbm.at[pl.ds(n * N, N), own_half], wo.at[n], in_s.at[2 + n])
        for n in range(2)
    ]
    seed_at = ((x * 64 + z * 16), (256 + z * 64 + x * 16))
    load_seed = [
        pltpu.make_async_copy(
            wo_hbm.at[pl.ds(pl.multiple_of(core * N + seed_at[n], 16), 16), far_half],
            seed.at[n], in_s.at[4 + n],
        )
        for n in range(2)
    ]
    for copy in load_seed:
        copy.start()
    load_tok.start()
    weights(0).start()
    weights(1).start()
    weights(2).start()
    load_w0.start()
    for copy in load_wo:
        copy.start()

    barrier = pltpu.get_barrier_semaphore()
    everyone = (
        partner, at_x(1), at_x(-1), at_z(1), at_z(-1), other_block, diagonal, other_head,
        {**other_block, **partner}, {**diagonal, **partner}, {**other_head, **partner},
    )
    for device in everyone:
        pl.semaphore_signal(barrier, inc=1, device_id=device, device_id_type=MESH)
    pl.semaphore_wait(barrier, len(everyone))

    def rcopy(src, dst, ss, rs, device):
        return pltpu.make_async_remote_copy(
            src_ref=src, dst_ref=dst, send_sem=ss, recv_sem=rs,
            device_id=device, device_id_type=MESH,
        )

    swaps = [
        rcopy(src, dst, ex_s.at[n], ex_r.at[n], partner)
        for n, (src, dst) in enumerate(
            ((ks, k32.at[pl.ds(N, N)]), (ys, y32.at[pl.ds(N, N)]), (qs, q_got))
        )
    ]

    def project(n, finish):
        weights(n).wait()

        @pl.loop(0, 2)
        def _(i):
            rows = pl.ds(pl.multiple_of(i * 256, 256), 256)
            finish(i * 256, rows, dot(tok_v[rows, :], big[n % 3]))

    def rates(rows, which):
        r = jax.nn.softplus(dot_nt(tok_v[rows, :], rate_ref[...]))
        return jnp.where(which == 0, r[:, 0:1], r[:, 1:2])

    def put(ref, f):
        def finish(base, rows, v):
            ref[rows, :] = f(rows, v)

        return finish

    def rows_of(s, j1, j2=None, off=0, count=64):
        at = s * 256 + j1 * 64 + off
        if j2 is not None:
            at = at + j2 * 16
        return pl.ds(pl.multiple_of(at, 8), count)

    def gather_stage(buf, piece, n, i, go, ss, rs, done):
        nxt, prv, far = lax.rem(i + 1, 4), lax.rem(i + 3, 4), lax.rem(i + 2, 4)
        right, left = go(1), go(-1)

        def send(k, rows, device):
            return rcopy(buf.at[rows], buf.at[rows], ss.at[k], rs.at[k], device)

        c0 = send(0, piece(i, 0, 2 * n), right)
        c1 = send(1, piece(i, 0, 2 * n), left)
        c0.start()
        c1.start()
        yield
        send(0, piece(prv, 0, 2 * n), right).wait_recv()
        c2 = send(2, piece(prv, 0, n), right)
        c2.start()
        send(1, piece(nxt, 0, 2 * n), left).wait_recv()
        c3 = send(3, piece(nxt, n, n), left)
        c3.start()
        yield
        send(2, piece(far, 0, n), right).wait_recv()
        send(3, piece(far, n, n), left).wait_recv()
        done.extend((c0, c1, c2, c3))

    axes = ((x, at_x, z, at_z), (z, at_z, x, at_x))

    def gather(buf, m, s, ss, rs, done):
        i1, go1, i2, go2 = axes[s]
        yield from gather_stage(
            buf.at[m], lambda j, o, c: rows_of(s, i1, j, o, c), 8, i2, go2,
            ss.at[m, s, 0], rs.at[m, s, 0], done,
        )
        yield from gather_stage(
            buf.at[m], lambda j, o, c: rows_of(s, j, None, o, c), 32, i1, go1,
            ss.at[m, s, 1], rs.at[m, s, 1], done,
        )

    SHARDS = tuple((m, n) for m in range(2) for n in range(2))
    seeds = [
        rcopy(
            seed32.at[m, n], wog.at[m, pl.ds(pl.multiple_of(seed_at[n], 16), 16)],
            sd_s.at[m, n], sd_r.at[m, n], diagonal,
        )
        for m, n in SHARDS
    ]
    for copy in load_seed:
        copy.wait()
    for m, n in SHARDS:
        seed32[m, n] = seed[n, :, m * N:(m + 1) * N].astype(f32)
    for copy in seeds:
        copy.start()
    def bring_weights(m, n, wo_sent):
        seeds[m * 2 + n].wait_recv()
        yield from gather(wog, m, n, wg_s, wg_r, wo_sent)

    wo_swap = rcopy(wog, wos, ex_s.at[5], ex_r.at[5], partner)

    load_tok.wait()
    project(0, put(ks, lambda r, v: normalize(v)))
    swaps[0].start()
    weights(3).start()
    project(1, put(ys, lambda r, v: v * rates(r, 1 - core)))
    swaps[1].start()
    project(2, put(k32, lambda r, v: normalize(v)))
    project(3, put(y32, lambda r, v: v * rates(r, core)))

    def project_q():
        weights(4).start()
        weights(5).start()
        project(4, put(qs, lambda r, v: normalize(v)))
        swaps[2].start()
        project(5, put(qm, lambda r, v: normalize(v)))

    load_w0.wait()
    swaps[0].wait_recv()
    swaps[1].wait_recv()

    def set_weights():
        for m in range(3):
            @pl.loop(0, 4)
            def _(i):
                rows = pl.ds(pl.multiple_of(i * 128, 128), 128)
                w[m, rows, :] = w0[m, rows, :].astype(f32)

            start = w[m]
            r0[m] = jnp.sqrt(jnp.mean(start * start, axis=0, keepdims=True))

    def keep_weights():
        wo_sent = []
        bringing = [bring_weights(m, n, wo_sent) for m, n in SHARDS]
        for _ in range(5):
            for g in bringing:
                next(g, None)
        wo_swap.start()
        wo_swap.wait_recv()

        @pl.loop(0, 4)
        def _(i):
            rows = pl.ds(pl.multiple_of(i * 128, 128), 128)
            for m in range(2):
                columns = pl.ds(m * N, N)
                wo[2 + core, rows, columns] = wog[m, rows, :].astype(bf16)
                wo[3 - core, rows, columns] = wos[m, rows, :].astype(bf16)

        for c in wo_sent:
            c.wait_send()

    def reduce_stage(m, piece, n, got, store, i, go, ss, rs, sent):
        src = gp.at[m]
        nxt, prv, far = lax.rem(i + 1, 4), lax.rem(i + 3, 4), lax.rem(i + 2, 4)
        right, left = go(1), go(-1)
        c0 = rcopy(src.at[piece(far, 0, n)], got.at[0], ss.at[0], rs.at[0], right)
        c1 = rcopy(src.at[piece(far, n, n)], got.at[1], ss.at[1], rs.at[1], left)
        c2 = rcopy(src.at[piece(nxt, n, n)], got.at[2], ss.at[2], rs.at[2], right)
        c3 = rcopy(src.at[piece(prv, 0, n)], got.at[3], ss.at[3], rs.at[3], left)
        for c in (c0, c1, c2, c3):
            c.start()
        yield
        c0.wait_recv()
        got[0] = got[0] + gp[m, piece(nxt, 0, n), :]
        c4 = rcopy(got.at[0], got.at[4], ss.at[4], rs.at[4], right)
        c4.start()
        c1.wait_recv()
        got[1] = got[1] + gp[m, piece(prv, n, n), :]
        c5 = rcopy(got.at[1], got.at[5], ss.at[5], rs.at[5], left)
        c5.start()
        yield
        for c in (c2, c3, c4, c5):
            c.wait_recv()
        store(0, gp[m, piece(i, 0, n), :] + got[3] + got[4])
        store(n, gp[m, piece(i, n, n), :] + got[2] + got[5])
        sent.extend((c0, c1, c2, c3, c4, c5))

    def shard(m, s):
        i1, _, i2, _ = axes[s]
        rows = rows_of(s, i1, i2, 0, 16)
        return rcopy(gf.at[m, rows], gf1.at[m, rows], sh_s.at[m, s], sh_r.at[m, s], other_block)

    def reduce(m, s, sent):
        i1, go1, i2, go2 = axes[s]

        def store1(o, v):
            gp[m, rows_of(s, i1, None, o, 32), :] = v

        def store2(o, v):
            gf[m, rows_of(s, i1, i2, o, 8), :] = v

        yield from reduce_stage(
            m, lambda j, o, c: rows_of(s, j, None, o, c), 32, r1.at[m, s], store1, i1, go1,
            rs_s.at[m, s, 0], rs_r.at[m, s, 0], sent,
        )
        yield from reduce_stage(
            m, lambda j, o, c: rows_of(s, i1, j, o, c), 8, r2.at[m, s], store2, i2, go2,
            rs_s.at[m, s, 1], rs_r.at[m, s, 1], sent,
        )

    def first_block(m, s, sent):
        yield from reduce(m, s, sent)
        shard(m, s).start()
        sent.append(shard(m, s))

    def last_block(m, s, sent):
        yield from reduce(m, s, sent)
        yield from gather(gf, m, s, ag_s, ag_r, sent)

    def update(m, g_ref):
        def rows_at(i):
            return pl.ds(pl.multiple_of(i * 64, 64), 64)

        def squares(i, total):
            g = g_ref[m, rows_at(i), :]
            return total + jnp.sum(g * g, axis=0, keepdims=True)

        total = jnp.sum(lax.fori_loop(0, 8, squares, jnp.zeros((1, N), f32)), axis=1, keepdims=True)
        scale = step_size / jnp.sqrt(total / (N * N) + epsilon)

        def move(i, column):
            rows = rows_at(i)
            moved = w[m, rows, :] + g_ref[m, rows, :] * scale
            w[m, rows, :] = moved
            return column + jnp.sum(moved * moved, axis=0, keepdims=True)

        column = lax.fori_loop(0, 8, move, jnp.zeros((1, N), f32)) / N
        factor = r0[m] / jnp.sqrt(column + epsilon)

        @pl.loop(0, 8)
        def _(i):
            rows = rows_at(i)
            fresh = w[m, rows, :] * factor
            w[m, rows, :] = fresh
            wh[m, rows, :], wl[m, rows, :] = split(fresh)

    def drive(streams, finish):
        left = {m: list(streams[m]) for m in streams}
        while left:
            for m in [m for m in ORDER if m in left]:
                still = []
                for g in left[m]:
                    try:
                        next(g)
                        still.append(g)
                    except StopIteration:
                        pass
                left[m] = still
                if not still:
                    del left[m]
                    finish(m)

    @pl.when(block == 1)
    def _():
        project_q()
        set_weights()
        keep_weights()
        done = []

        def first(m, s):
            shard(m, s).wait_recv()
            yield from gather(gf1, m, s, a1_s, a1_r, done)

        drive({m: [first(m, s) for s in range(2)] for m in range(3)}, lambda m: update(m, gf1))
        for c in done:
            c.wait_send()

    hh, hl = big.at[0, pl.ds(0, 2 * N)], big.at[0, pl.ds(2 * N, 2 * N)]
    p3h, p3l = big.at[1, pl.ds(0, 2 * N)], big.at[1, pl.ds(2 * N, 2 * N)]
    p1h, p1l = big.at[2, pl.ds(0, 2 * N)], big.at[2, pl.ds(2 * N, 2 * N)]

    def forward(times):
        @pl.loop(0, 4)
        def _(i):
            rows = pl.ds(pl.multiple_of(i * 256, 256), 256)
            ah, al = split(k32[rows, :])
            ch, cl = split(y32[rows, :])
            gate = times(ah, al, 0)
            upper = times(ah, al, 1)
            back = times(ch, cl, 2)
            kth[:, rows] = ah.T
            ktl[:, rows] = al.T
            yth[:, rows] = ch.T
            ytl[:, rows] = cl.T
            sigma = jax.nn.sigmoid(gate)
            active = gate * sigma
            hh[rows, :], hl[rows, :] = split(active * upper)
            p3h[rows, :], p3l[rows, :] = split(back * active)
            p1h[rows, :], p1l[rows, :] = split(back * upper * sigma * (1.0 + gate * (1.0 - sigma)))

    def product(m, lth, ltl, rh, rl):
        @pl.loop(0, 4)
        def _(i):
            rows = pl.ds(pl.multiple_of(i * 128, 128), 128)
            gp[m, rows, :] = mm3(lth[rows, :], ltl[rows, :], rh[...], rl[...])

    def exchange(stream, finish, sent):
        live = {}

        def begin(m):
            live[m] = [stream(m, s, sent) for s in range(2)]
            for g in live[m]:
                next(g)

        def advance(m):
            for g in live[m]:
                next(g)

        product(1, kth, ktl, p3h, p3l)
        begin(1)
        product(0, kth, ktl, p1h, p1l)
        advance(1)
        begin(0)
        product(2, yth, ytl, hh, hl)
        advance(1)
        advance(0)
        begin(2)
        drive(live, finish)

    @pl.when(block == 0)
    def _():
        sent = []
        forward(lambda h, l, m: dot(h, w0[m]) + dot(l, w0[m]))
        exchange(first_block, lambda m: None, sent)
        live = {m: [gather(gf, m, s, ag_s, ag_r, sent) for s in range(2)] for m in range(3)}
        for m in ORDER:
            for g in live[m]:
                next(g)
        project_q()
        set_weights()
        drive(live, lambda m: update(m, gf))
        for c in sent:
            c.wait_send()

    @pl.when(block == 1)
    def _():
        sent = []
        forward(lambda h, l, m: mm3(h, l, wh[m], wl[m]))
        exchange(last_block, lambda m: update(m, gf), sent)
        for c in sent:
            c.wait_send()

    def rows_at(j):
        return pl.ds(pl.multiple_of(j * 64, 64), 64)

    receivers = ({"tok": partner["tok"]}, {})

    def direct(t, j):
        r = rows_at(j)
        device = {"head": 1 - head, **receivers[t]}
        return rcopy(gp.at[t, r], o_far.at[core, r], pt_s.at[t, j], pt_r.at[t, j], device)

    def arrival(t, j):
        r = rows_at(j)
        at = o_far.at[1 - core if t == 0 else core, r]
        return rcopy(at, at, pt_s.at[t, j], pt_r.at[t, j], other_head)

    def first_leg(t, j, device):
        r = rows_at(j)
        return rcopy(gp.at[t, r], gf1.at[t, r], rl_s.at[t, j], rl_r.at[t, j], device)

    def second_leg(t, j, device):
        r = rows_at(j)
        return rcopy(
            gf1.at[t, r], o_far.at[core, r], pt_s.at[t, 8 + j], pt_r.at[t, j],
            {**device, **receivers[t]},
        )

    def send_far(t, i):
        @pl.when(block == 0)
        def _():
            for j in range(4):
                direct(t, i * 4 + j).start()

        @pl.when(block == 1)
        def _():
            for j in range(0, 4, 2):
                first_leg(t, i * 4 + j, other_block).start()
                first_leg(t, i * 4 + j + 1, diagonal).start()

    def give(i):
        rows = pl.ds(pl.multiple_of(i * 256, 256), 256)
        return rcopy(gp.at[0, rows], o_got.at[rows], ex_s.at[3 + i], ex_r.at[3 + i], partner)

    def apply(t, q):
        @pl.loop(0, 2)
        def _(i):
            rows = pl.ds(pl.multiple_of(i * 256, 256), 256)
            ah, al = split(q[rows, :])
            gate = mm3(ah, al, wh[0], wl[0])
            upper = mm3(ah, al, wh[1], wl[1])
            bh, bl = split(gate * jax.nn.sigmoid(gate) * upper)
            o = normalize(mm3_nt(bh, bl, wh[2], wl[2])).astype(bf16)
            gp[t, rows, :] = o.astype(f32)
            if t == 1:
                o_all[rows, mine] = o
            send_far(t, i)
            if t == 0:
                give(i).start()

    swaps[2].wait_recv()
    apply(0, q_got)
    apply(1, qm)

    @pl.when(block == 0)
    def _():
        keep_weights()

    for copy in load_wo:
        copy.wait()
    for i in range(2):
        give(i).wait_recv()
    o_all[:, theirs] = o_got[...].astype(bf16)

    @pl.loop(0, 4)
    def _(i):
        rows = pl.ds(pl.multiple_of(i * 128, 128), 128)
        v = dot(o_all[rows, :N], wo[0]) + dot(o_all[rows, N:], wo[1])
        w[0, rows, :] = v[:, :N]
        w[1, rows, :] = v[:, N:]

    def add_theirs():
        for j in range(8):
            arrival(0, j).wait_recv()

        @pl.loop(0, 4)
        def _(i):
            rows = pl.ds(pl.multiple_of(i * 128, 128), 128)
            v = dot(o_far[1 - core, rows, :].astype(bf16), wo[3 - core])
            w[0, rows, :] = w[0, rows, :] + v[:, :N]
            w[1, rows, :] = w[1, rows, :] + v[:, N:]

    def add_mine(j):
        arrival(1, j).wait_recv()
        rows = rows_at(j)
        v = dot(o_far[core, rows, :].astype(bf16), wo[2 + core])
        o_ref[rows, :N] = (w[0, rows, :] + v[:, :N]).astype(bf16)
        o_ref[rows, N:] = (w[1, rows, :] + v[:, N:]).astype(bf16)

    def relay(t, i):
        first_leg(t, 2 * i, other_block).wait_recv()
        second_leg(t, 2 * i, diagonal).start()
        first_leg(t, 2 * i + 1, diagonal).wait_recv()
        second_leg(t, 2 * i + 1, other_block).start()

    @pl.when(block == 0)
    def _():
        @pl.loop(0, 4)
        def _(i):
            relay(0, i)

        add_theirs()

        @pl.loop(0, 4)
        def _(i):
            relay(1, i)
            add_mine(2 * i)
            add_mine(2 * i + 1)

        for t in range(2):
            @pl.loop(0, 8)
            def _(j):
                direct(t, j).wait_send()
                second_leg(t, j, diagonal).wait_send()

    @pl.when(block == 1)
    def _():
        add_theirs()

        @pl.loop(0, 8)
        def _(j):
            add_mine(j)

        for t in range(2):
            @pl.loop(0, 8)
            def _(j):
                first_leg(t, j, diagonal).wait_send()

    for c in swaps + seeds + [wo_swap, give(0), give(1)]:
        c.wait_send()


def chain(tokens, weight, rate_weight, fast_init, output_weight):
    dma = pltpu.SemaphoreType.DMA
    square = lambda n, t: pltpu.VMEM((n, N, N), t)
    wide = pltpu.VMEM((N, 2 * N), bf16)
    part = pltpu.VMEM((N, N), f32)
    vmem = pl.BlockSpec(memory_space=pltpu.VMEM)
    hbm = pl.BlockSpec(memory_space=pl.ANY)
    return pl.pallas_call(
        chain_kernel,
        out_shape=jax.ShapeDtypeStruct((N, 2 * N), bf16),
        in_specs=[hbm, hbm, vmem, hbm, hbm],
        out_specs=vmem,
        scratch_shapes=[
            pltpu.VMEM((N, 4 * N), bf16), pltpu.VMEM((4, N, 2 * N), bf16), square(3, bf16),
            part, part, part, part, pltpu.VMEM((2 * N, N), f32), pltpu.VMEM((2 * N, N), f32), part, part,
            pltpu.VMEM((N, 2 * N), bf16), square(2, f32),
            pltpu.VMEM((2, 16, 2 * N), bf16), pltpu.VMEM((2, 2, 16, N), f32),
            square(2, f32), square(2, f32),
            wide, wide, wide, wide, pltpu.VMEM((3, 4 * N, N), bf16),
            square(3, f32), square(3, bf16), square(3, bf16), pltpu.VMEM((3, 1, N), f32),
            square(3, f32), square(3, f32), square(3, f32),
            pltpu.VMEM((3, 2, 6, 32, N), f32), pltpu.VMEM((3, 2, 6, 8, N), f32),
            dma((3, 2, 2, 6)), dma((3, 2, 2, 6)),
            dma((3, 2, 2, 4)), dma((3, 2, 2, 4)),
            dma((3, 2, 2, 4)), dma((3, 2, 2, 4)),
            dma((3, 2)), dma((3, 2)),
            dma((6,)), dma((6,)),
            dma((2, 16)), dma((2, 8)), dma((2, 8)), dma((2, 8)),
            dma((2, 2)), dma((2, 2)), dma((2, 2, 2, 4)), dma((2, 2, 2, 4)),
            dma((6,)), dma((3,)),
        ],
        compiler_params=pltpu.CompilerParams(
            collective_id=0, has_side_effects=True, vmem_limit_bytes=62 * 1024 * 1024
        ),
    )(tokens, weight, rate_weight, fast_init, output_weight)


def body(tokens, input_weight, rate_weight, fast_init, output_weight):
    flat = tokens[0]
    mixed = chain(
        flat, jnp.transpose(input_weight, (1, 0, 2)), rate_weight.T, fast_init, output_weight
    )
    return mixed[None]


def solution(mesh):
    placed = (
        P("block", "tok", None),
        P(None, None, "head"),
        P(None, "head"),
        P("head", None, None, None),
        P("head", None),
    )
    return jax.shard_map(
        body, mesh=mesh, in_specs=placed, out_specs=P("block", "tok", "head"), check_vma=False
    )
```

```python
import jax
import jax.numpy as jnp
from jax import lax
from jax.experimental import pallas as pl
from jax.experimental.pallas import tpu as pltpu
from jax.sharding import PartitionSpec as P

epsilon = 1e-06
step_size = 0.03
MESH = pl.DeviceIdType.MESH
f32 = jnp.float32
bf16 = jnp.bfloat16
N = 512
ORDER = (1, 0, 2)


def split(x):
    hi = x.astype(bf16)
    return hi, (x - hi.astype(f32)).astype(bf16)


def dot(a, b):
    return jnp.dot(a, b, preferred_element_type=f32)


def mm3(ah, al, bh, bl):
    return dot(ah, bh) + (dot(ah, bl) + dot(al, bh))


def dot_nt(a, b):
    return lax.dot_general(a, b, (((1,), (1,)), ((), ())), preferred_element_type=f32)


def mm3_nt(ah, al, bh, bl):
    return dot_nt(ah, bh) + (dot_nt(ah, bl) + dot_nt(al, bh))


def normalize(v):
    return v * (1.0 / jnp.sqrt(jnp.mean(v * v, axis=-1, keepdims=True) + epsilon))


def chain_kernel(
    tok_hbm, wi_hbm, rate_ref, w0_hbm, wo_hbm, o_ref,
    tok_v, wo, w0, ks, ys, k32, y32, q32, u32, rate, o_got, o_all, o_far, seed, seed32, wog, wos,
    kth, ktl, yth, ytl, big,
    w, wh, wl, r0, gp, gf, gf1, r1, r2,
    rs_s, rs_r, ag_s, ag_r, a1_s, a1_r, sh_s, sh_r, ex_s, ex_r,
    pt_s, pt_r, rl_s, rl_r, sd_s, sd_r, wg_s, wg_r, in_s, wi_s,
):
    tok = lax.axis_index("tok")
    block = lax.axis_index("block")
    head = lax.axis_index("head")
    core = lax.rem(tok, 2)
    chip = lax.div(tok, 2)
    x = lax.rem(chip, 4)
    z = lax.div(chip, 4)

    def at_x(d):
        return {"tok": (z * 4 + lax.rem(x + d + 4, 4)) * 2 + core}

    def at_z(d):
        return {"tok": (lax.rem(z + d + 4, 4) * 4 + x) * 2 + core}

    partner = {"tok": chip * 2 + (1 - core)}
    other_block = {"block": 1 - block}
    diagonal = {"block": 1 - block, "head": 1 - head}
    other_head = {"head": 1 - head}

    mine = pl.ds(pl.multiple_of(core * N, N), N)
    theirs = pl.ds(pl.multiple_of((1 - core) * N, N), N)

    SEQ = ((1, theirs), (2, theirs), (1, mine), (2, mine), (0, theirs), (0, mine))

    def weights(n):
        part, columns = SEQ[n]
        return pltpu.make_async_copy(wi_hbm.at[part, :, columns], big.at[n % 3], wi_s.at[n % 3])

    load_tok = pltpu.make_async_copy(tok_hbm, tok_v, in_s.at[0])
    load_w0 = pltpu.make_async_copy(w0_hbm.at[core], w0, in_s.at[1])
    own_half = pl.ds(pl.multiple_of(head * 2 * N, 2 * N), 2 * N)
    far_half = pl.ds(pl.multiple_of((1 - head) * 2 * N, 2 * N), 2 * N)
    load_wo = [
        pltpu.make_async_copy(wo_hbm.at[pl.ds(n * N, N), own_half], wo.at[n], in_s.at[2 + n])
        for n in range(2)
    ]
    seed_at = ((x * 64 + z * 16), (256 + z * 64 + x * 16))
    load_seed = [
        pltpu.make_async_copy(
            wo_hbm.at[pl.ds(pl.multiple_of(core * N + seed_at[n], 16), 16), far_half],
            seed.at[n], in_s.at[4 + n],
        )
        for n in range(2)
    ]
    for copy in load_seed:
        copy.start()
    load_tok.start()
    weights(0).start()
    weights(1).start()
    weights(2).start()
    load_w0.start()
    for copy in load_wo:
        copy.start()

    barrier = pltpu.get_barrier_semaphore()
    everyone = (
        partner, at_x(1), at_x(-1), at_z(1), at_z(-1), other_block, diagonal, other_head,
        {**other_block, **partner}, {**diagonal, **partner}, {**other_head, **partner},
    )
    for device in everyone:
        pl.semaphore_signal(barrier, inc=1, device_id=device, device_id_type=MESH)

    def rcopy(src, dst, ss, rs, device):
        return pltpu.make_async_remote_copy(
            src_ref=src, dst_ref=dst, send_sem=ss, recv_sem=rs,
            device_id=device, device_id_type=MESH,
        )

    swaps = [
        rcopy(src, dst, ex_s.at[n], ex_r.at[n], partner)
        for n, (src, dst) in enumerate(
            ((ks, k32.at[pl.ds(N, N)]), (ys, y32.at[pl.ds(N, N)]), (ks, q32.at[pl.ds(0, N)]))
        )
    ]

    def project(n, finish):
        weights(n).wait()
        return finish(dot(tok_v[...], big[n % 3]))

    def chosen_rate(which):
        return jnp.where(which == 0, rate[:, 0:1], rate[:, 1:2])

    def rows_of(s, j1, j2=None, off=0, count=64):
        at = s * 256 + j1 * 64 + off
        if j2 is not None:
            at = at + j2 * 16
        return pl.ds(pl.multiple_of(at, 8), count)

    def gather_stage(buf, piece, n, i, go, ss, rs, done):
        nxt, prv, far = lax.rem(i + 1, 4), lax.rem(i + 3, 4), lax.rem(i + 2, 4)
        right, left = go(1), go(-1)

        def send(k, rows, device):
            return rcopy(buf.at[rows], buf.at[rows], ss.at[k], rs.at[k], device)

        c0 = send(0, piece(i, 0, 2 * n), right)
        c1 = send(1, piece(i, 0, 2 * n), left)
        c0.start()
        c1.start()
        yield
        send(0, piece(prv, 0, 2 * n), right).wait_recv()
        c2 = send(2, piece(prv, 0, n), right)
        c2.start()
        send(1, piece(nxt, 0, 2 * n), left).wait_recv()
        c3 = send(3, piece(nxt, n, n), left)
        c3.start()
        yield
        send(2, piece(far, 0, n), right).wait_recv()
        send(3, piece(far, n, n), left).wait_recv()
        done.extend((c0, c1, c2, c3))

    axes = ((x, at_x, z, at_z), (z, at_z, x, at_x))

    def gather(buf, m, s, ss, rs, done):
        i1, go1, i2, go2 = axes[s]
        yield from gather_stage(
            buf.at[m], lambda j, o, c: rows_of(s, i1, j, o, c), 8, i2, go2,
            ss.at[m, s, 0], rs.at[m, s, 0], done,
        )
        yield from gather_stage(
            buf.at[m], lambda j, o, c: rows_of(s, j, None, o, c), 32, i1, go1,
            ss.at[m, s, 1], rs.at[m, s, 1], done,
        )

    SHARDS = tuple((m, n) for m in range(2) for n in range(2))
    seeds = [
        rcopy(
            seed32.at[m, n], wog.at[m, pl.ds(pl.multiple_of(seed_at[n], 16), 16)],
            sd_s.at[m, n], sd_r.at[m, n], diagonal,
        )
        for m, n in SHARDS
    ]
    def bring_weights(m, n, wo_sent):
        seeds[m * 2 + n].wait_recv()
        yield from gather(wog, m, n, wg_s, wg_r, wo_sent)

    wo_swap = rcopy(wog, wos, ex_s.at[5], ex_r.at[5], partner)

    load_tok.wait()
    ks[...] = project(0, normalize)
    weights(3).start()
    rate[...] = jax.nn.softplus(dot_nt(tok_v[...], rate_ref[...]))
    ys[...] = project(1, lambda v: v * chosen_rate(1 - core))
    pl.semaphore_wait(barrier, len(everyone))
    swaps[0].start()
    swaps[1].start()
    for copy in load_seed:
        copy.wait()
    for m, n in SHARDS:
        seed32[m, n] = seed[n, :, m * N:(m + 1) * N].astype(f32)
    for copy in seeds:
        copy.start()
    k32[:N, :] = project(2, normalize)
    y32[:N, :] = project(3, lambda v: v * chosen_rate(core))

    def project_q():
        weights(4).start()
        weights(5).start()
        swaps[0].wait_send()
        ks[...] = project(4, normalize)
        swaps[2].start()
        q32[N:, :] = project(5, normalize)
        swaps[2].wait_recv()

    load_w0.wait()

    def set_weights():
        for m in range(3):
            @pl.loop(0, 4)
            def _(i):
                rows = pl.ds(pl.multiple_of(i * 128, 128), 128)
                w[m, rows, :] = w0[m, rows, :].astype(f32)

            start = w[m]
            r0[m] = jnp.sqrt(jnp.mean(start * start, axis=0, keepdims=True))

    def keep_weights():
        wo_sent = []
        bringing = [bring_weights(m, n, wo_sent) for m, n in SHARDS]
        for _ in range(5):
            for g in bringing:
                next(g, None)
        wo_swap.start()
        wo_swap.wait_recv()

        @pl.loop(0, 4)
        def _(i):
            rows = pl.ds(pl.multiple_of(i * 128, 128), 128)
            for m in range(2):
                columns = pl.ds(m * N, N)
                wo[2 + core, rows, columns] = wog[m, rows, :].astype(bf16)
                wo[3 - core, rows, columns] = wos[m, rows, :].astype(bf16)

        for c in wo_sent:
            c.wait_send()

    def reduce_stage(m, piece, n, got, store, i, go, ss, rs, sent):
        src = gp.at[m]
        nxt, prv, far = lax.rem(i + 1, 4), lax.rem(i + 3, 4), lax.rem(i + 2, 4)
        right, left = go(1), go(-1)
        c0 = rcopy(src.at[piece(far, 0, n)], got.at[0], ss.at[0], rs.at[0], right)
        c1 = rcopy(src.at[piece(far, n, n)], got.at[1], ss.at[1], rs.at[1], left)
        c2 = rcopy(src.at[piece(nxt, n, n)], got.at[2], ss.at[2], rs.at[2], right)
        c3 = rcopy(src.at[piece(prv, 0, n)], got.at[3], ss.at[3], rs.at[3], left)
        for c in (c0, c1, c2, c3):
            c.start()
        yield
        c0.wait_recv()
        got[0] = got[0] + gp[m, piece(nxt, 0, n), :]
        c4 = rcopy(got.at[0], got.at[4], ss.at[4], rs.at[4], right)
        c4.start()
        c1.wait_recv()
        got[1] = got[1] + gp[m, piece(prv, n, n), :]
        c5 = rcopy(got.at[1], got.at[5], ss.at[5], rs.at[5], left)
        c5.start()
        yield
        for c in (c2, c3, c4, c5):
            c.wait_recv()
        store(0, gp[m, piece(i, 0, n), :] + got[3] + got[4])
        store(n, gp[m, piece(i, n, n), :] + got[2] + got[5])
        sent.extend((c0, c1, c2, c3, c4, c5))

    def shard(m, s):
        i1, _, i2, _ = axes[s]
        rows = rows_of(s, i1, i2, 0, 16)
        return rcopy(gf.at[m, rows], gf1.at[m, rows], sh_s.at[m, s], sh_r.at[m, s], other_block)

    def reduce(m, s, sent):
        i1, go1, i2, go2 = axes[s]

        def store1(o, v):
            gp[m, rows_of(s, i1, None, o, 32), :] = v

        def store2(o, v):
            gf[m, rows_of(s, i1, i2, o, 8), :] = v

        yield from reduce_stage(
            m, lambda j, o, c: rows_of(s, j, None, o, c), 32, r1.at[m, s], store1, i1, go1,
            rs_s.at[m, s, 0], rs_r.at[m, s, 0], sent,
        )
        yield from reduce_stage(
            m, lambda j, o, c: rows_of(s, i1, j, o, c), 8, r2.at[m, s], store2, i2, go2,
            rs_s.at[m, s, 1], rs_r.at[m, s, 1], sent,
        )

    def first_block(m, s, sent):
        yield from reduce(m, s, sent)
        shard(m, s).start()
        sent.append(shard(m, s))

    def last_block(m, s, sent):
        yield from reduce(m, s, sent)
        yield from gather(gf, m, s, ag_s, ag_r, sent)

    def update(m, g_ref):
        def rows_at(i):
            return pl.ds(pl.multiple_of(i * 64, 64), 64)

        def squares(i, total):
            g = g_ref[m, rows_at(i), :]
            return total + jnp.sum(g * g, axis=0, keepdims=True)

        total = jnp.sum(lax.fori_loop(0, 8, squares, jnp.zeros((1, N), f32)), axis=1, keepdims=True)
        scale = step_size / jnp.sqrt(total / (N * N) + epsilon)

        def move(i, column):
            rows = rows_at(i)
            moved = w[m, rows, :] + g_ref[m, rows, :] * scale
            w[m, rows, :] = moved
            return column + jnp.sum(moved * moved, axis=0, keepdims=True)

        column = lax.fori_loop(0, 8, move, jnp.zeros((1, N), f32)) / N
        factor = r0[m] / jnp.sqrt(column + epsilon)

        @pl.loop(0, 8)
        def _(i):
            rows = rows_at(i)
            fresh = w[m, rows, :] * factor
            w[m, rows, :] = fresh
            wh[m, rows, :], wl[m, rows, :] = split(fresh)

    def drive(streams, finish):
        left = {m: list(streams[m]) for m in streams}
        work = []

        def labor():
            while work:
                try:
                    next(work[0])
                    return
                except StopIteration:
                    work.pop(0)

        while left:
            for m in [m for m in ORDER if m in left]:
                still = []
                for g in left[m]:
                    try:
                        next(g)
                        still.append(g)
                    except StopIteration:
                        pass
                left[m] = still
                if not still:
                    del left[m]
                    work.append(finish(m))
                labor()
        while work:
            labor()

    def halves(f):
        for i in range(4):
            f(i, pl.ds(i * 256, 256))
            yield

    def upper_of(source):
        def one(i, rows):
            h, l = split(source[rows, :])
            u32[rows, :] = mm3(h, l, wh[1], wl[1])

        return one

    def gate_part(i):
        return i // 2, pl.ds(i % 2 * 256, 256)

    def transpose_all():
        @pl.loop(0, 2)
        def _(i):
            rows = pl.ds(pl.multiple_of(i * N, N), N)
            for source, th, tl in ((k32, kth, ktl), (y32, yth, ytl)):
                h, l = split(source[rows, :])
                th[:, rows] = h.T
                tl[:, rows] = l.T

    hh, hl = big.at[0, pl.ds(0, 2 * N)], big.at[0, pl.ds(2 * N, 2 * N)]
    p3h, p3l = big.at[1, pl.ds(0, 2 * N)], big.at[1, pl.ds(2 * N, 2 * N)]
    p1h, p1l = big.at[2, pl.ds(0, 2 * N)], big.at[2, pl.ds(2 * N, 2 * N)]

    def combine(rows, gate, upper, back):
        sigma = jax.nn.sigmoid(gate)
        active = gate * sigma
        hh[rows, :], hl[rows, :] = split(active * upper)
        p3h[rows, :], p3l[rows, :] = split(back * active)
        p1h[rows, :], p1l[rows, :] = split(back * upper * sigma * (1.0 + gate * (1.0 - sigma)))

    def learned(m):
        update(m, gf1)
        yield
        if m == 2:
            def last(i, rows):
                h, l = split(y32[rows, :])
                combine(rows, gp[gate_part(i)], u32[rows, :], mm3(h, l, wh[2], wl[2]))

            yield from halves(last)
        elif m == 0:
            def gate(i, rows):
                h, l = split(k32[rows, :])
                gp[gate_part(i)] = mm3(h, l, wh[0], wl[0])

            yield from halves(gate)
        else:
            yield from halves(upper_of(k32))

    def applied(m):
        update(m, gf)
        yield
        if m == 1:
            yield from halves(upper_of(q32))
        if m == 0:
            def hidden(i, rows):
                h, l = split(q32[rows, :])
                gate = mm3(h, l, wh[0], wl[0])
                hh[rows, :], hl[rows, :] = split(gate * jax.nn.sigmoid(gate) * u32[rows, :])

            yield from halves(hidden)

    @pl.when(block == 1)
    def _():
        swaps[0].wait_recv()
        swaps[1].wait_recv()
        project_q()
        set_weights()
        transpose_all()
        keep_weights()
        done = []

        def first(m, s):
            shard(m, s).wait_recv()
            yield from gather(gf1, m, s, a1_s, a1_r, done)

        drive({m: [first(m, s) for s in range(2)] for m in range(3)}, learned)
        for c in done:
            c.wait_send()

    def forward(i):
        rows = pl.ds(i * N, N)
        ah, al = split(k32[rows, :])
        ch, cl = split(y32[rows, :])
        gate = dot(ah, w0[0]) + dot(al, w0[0])
        upper = dot(ah, w0[1]) + dot(al, w0[1])
        back = dot(ch, w0[2]) + dot(cl, w0[2])
        kth[:, rows] = ah.T
        ktl[:, rows] = al.T
        yth[:, rows] = ch.T
        ytl[:, rows] = cl.T
        combine(rows, gate, upper, back)

    def product(m, lth, ltl, rh, rl):
        @pl.loop(0, 2)
        def _(i):
            rows = pl.ds(pl.multiple_of(i * 256, 256), 256)
            gp[m, rows, :] = mm3(lth[rows, :], ltl[rows, :], rh[...], rl[...])

    def exchange(stream, finish, sent):
        live = {}

        def begin(m):
            live[m] = [stream(m, s, sent) for s in range(2)]
            for g in live[m]:
                next(g)

        def advance(m):
            for g in live[m]:
                next(g)

        product(1, kth, ktl, p3h, p3l)
        begin(1)
        product(0, kth, ktl, p1h, p1l)
        advance(1)
        begin(0)
        product(2, yth, ytl, hh, hl)
        advance(1)
        advance(0)
        begin(2)
        drive(live, finish)

    @pl.when(block == 0)
    def _():
        sent = []
        forward(0)
        swaps[0].wait_recv()
        swaps[1].wait_recv()
        forward(1)
        exchange(first_block, lambda m: iter(()), sent)
        live = {m: [gather(gf, m, s, ag_s, ag_r, sent) for s in range(2)] for m in range(3)}
        for m in ORDER:
            for g in live[m]:
                next(g)
        project_q()
        set_weights()
        drive(live, applied)
        for c in sent:
            c.wait_send()

    @pl.when(block == 1)
    def _():
        sent = []
        exchange(last_block, applied, sent)
        for c in sent:
            c.wait_send()

    def rows_at(j):
        return pl.ds(pl.multiple_of(j * 64, 64), 64)

    receivers = ({"tok": partner["tok"]}, {})

    def direct(t, j):
        r = rows_at(j)
        device = {"head": 1 - head, **receivers[t]}
        return rcopy(gp.at[t, r], o_far.at[core, r], pt_s.at[t, j], pt_r.at[t, j], device)

    def arrival(t, j):
        r = rows_at(j)
        at = o_far.at[1 - core if t == 0 else core, r]
        return rcopy(at, at, pt_s.at[t, j], pt_r.at[t, j], other_head)

    def first_leg(t, j, device):
        r = rows_at(j)
        return rcopy(gp.at[t, r], gf1.at[t, r], rl_s.at[t, j], rl_r.at[t, j], device)

    def second_leg(t, j, device):
        r = rows_at(j)
        return rcopy(
            gf1.at[t, r], o_far.at[core, r], pt_s.at[t, 8 + j], pt_r.at[t, j],
            {**device, **receivers[t]},
        )

    def send_far(t, i):
        @pl.when(block == 0)
        def _():
            for j in range(4):
                direct(t, i * 4 + j).start()

        @pl.when(block == 1)
        def _():
            for j in range(0, 4, 2):
                first_leg(t, i * 4 + j, other_block).start()
                first_leg(t, i * 4 + j + 1, diagonal).start()

    def give(i):
        rows = pl.ds(pl.multiple_of(i * 256, 256), 256)
        return rcopy(gp.at[0, rows], o_got.at[rows], ex_s.at[3 + i], ex_r.at[3 + i], partner)

    def apply(t):
        @pl.loop(0, 2)
        def _(i):
            rows = pl.ds(pl.multiple_of(i * 256, 256), 256)
            of = pl.ds(pl.multiple_of(t * N + i * 256, 256), 256)
            o = normalize(mm3_nt(hh[of, :], hl[of, :], wh[2], wl[2])).astype(bf16)
            gp[t, rows, :] = o.astype(f32)
            if t == 1:
                o_all[rows, mine] = o
            send_far(t, i)
            if t == 0:
                give(i).start()

    apply(0)
    apply(1)

    @pl.when(block == 0)
    def _():
        keep_weights()

    for copy in load_wo:
        copy.wait()
    for i in range(2):
        give(i).wait_recv()
    o_all[:, theirs] = o_got[...].astype(bf16)

    @pl.loop(0, 2)
    def _(i):
        rows = pl.ds(pl.multiple_of(i * 256, 256), 256)
        v = dot(o_all[rows, :N], wo[0]) + dot(o_all[rows, N:], wo[1])
        w[0, rows, :] = v[:, :N]
        w[1, rows, :] = v[:, N:]

    def add_theirs():
        for j in range(8):
            arrival(0, j).wait_recv()

        @pl.loop(0, 2)
        def _(i):
            rows = pl.ds(pl.multiple_of(i * 256, 256), 256)
            v = dot(o_far[1 - core, rows, :].astype(bf16), wo[3 - core])
            w[0, rows, :] = w[0, rows, :] + v[:, :N]
            w[1, rows, :] = w[1, rows, :] + v[:, N:]

    def add_mine(j):
        arrival(1, j).wait_recv()
        rows = rows_at(j)
        v = dot(o_far[core, rows, :].astype(bf16), wo[2 + core])
        o_ref[rows, :N] = (w[0, rows, :] + v[:, :N]).astype(bf16)
        o_ref[rows, N:] = (w[1, rows, :] + v[:, N:]).astype(bf16)

    def relay(t, i):
        first_leg(t, 2 * i, other_block).wait_recv()
        second_leg(t, 2 * i, diagonal).start()
        first_leg(t, 2 * i + 1, diagonal).wait_recv()
        second_leg(t, 2 * i + 1, other_block).start()

    @pl.when(block == 0)
    def _():
        @pl.loop(0, 4)
        def _(i):
            relay(0, i)

        add_theirs()

        @pl.loop(0, 4)
        def _(i):
            relay(1, i)
            add_mine(2 * i)
            add_mine(2 * i + 1)

        for t in range(2):
            @pl.loop(0, 8)
            def _(j):
                direct(t, j).wait_send()
                second_leg(t, j, diagonal).wait_send()

    @pl.when(block == 1)
    def _():
        add_theirs()

        @pl.loop(0, 8)
        def _(j):
            add_mine(j)

        for t in range(2):
            @pl.loop(0, 8)
            def _(j):
                first_leg(t, j, diagonal).wait_send()

    for c in swaps[1:] + seeds + [wo_swap, give(0), give(1)]:
        c.wait_send()


def chain(tokens, weight, rate_weight, fast_init, output_weight):
    dma = pltpu.SemaphoreType.DMA
    square = lambda n, t: pltpu.VMEM((n, N, N), t)
    wide = pltpu.VMEM((N, 2 * N), bf16)
    part = pltpu.VMEM((N, N), f32)
    tall = pltpu.VMEM((2 * N, N), f32)
    vmem = pl.BlockSpec(memory_space=pltpu.VMEM)
    hbm = pl.BlockSpec(memory_space=pl.ANY)
    return pl.pallas_call(
        chain_kernel,
        out_shape=jax.ShapeDtypeStruct((N, 2 * N), bf16),
        in_specs=[hbm, hbm, vmem, hbm, hbm],
        out_specs=vmem,
        scratch_shapes=[
            pltpu.VMEM((N, 4 * N), bf16), pltpu.VMEM((4, N, 2 * N), bf16), square(3, bf16),
            part, part, tall, tall, tall, tall, pltpu.VMEM((N, 2), f32), part,
            pltpu.VMEM((N, 2 * N), bf16), square(2, f32),
            pltpu.VMEM((2, 16, 2 * N), bf16), pltpu.VMEM((2, 2, 16, N), f32),
            square(2, f32), square(2, f32),
            wide, wide, wide, wide, pltpu.VMEM((3, 4 * N, N), bf16),
            square(3, f32), square(3, bf16), square(3, bf16), pltpu.VMEM((3, 1, N), f32),
            square(3, f32), square(3, f32), square(3, f32),
            pltpu.VMEM((3, 2, 6, 32, N), f32), pltpu.VMEM((3, 2, 6, 8, N), f32),
            dma((3, 2, 2, 6)), dma((3, 2, 2, 6)),
            dma((3, 2, 2, 4)), dma((3, 2, 2, 4)),
            dma((3, 2, 2, 4)), dma((3, 2, 2, 4)),
            dma((3, 2)), dma((3, 2)),
            dma((6,)), dma((6,)),
            dma((2, 16)), dma((2, 8)), dma((2, 8)), dma((2, 8)),
            dma((2, 2)), dma((2, 2)), dma((2, 2, 2, 4)), dma((2, 2, 2, 4)),
            dma((6,)), dma((3,)),
        ],
        compiler_params=pltpu.CompilerParams(
            collective_id=0, has_side_effects=True, vmem_limit_bytes=67043328
        ),
    )(tokens, weight, rate_weight, fast_init, output_weight)


def body(tokens, input_weight, rate_weight, fast_init, output_weight):
    flat = tokens[0]
    mixed = chain(
        flat, jnp.transpose(input_weight, (1, 0, 2)), rate_weight.T, fast_init, output_weight
    )
    return mixed[None]


def solution(mesh):
    placed = (
        P("block", "tok", None),
        P(None, None, "head"),
        P(None, "head"),
        P("head", None, None, None),
        P("head", None),
    )
    return jax.shard_map(
        body, mesh=mesh, in_specs=placed, out_specs=P("block", "tok", "head"), check_vma=False
    )
```

```python
import jax
import jax.numpy as jnp
from jax import lax
from jax.experimental import pallas as pl
from jax.experimental.pallas import tpu as pltpu
from jax.sharding import PartitionSpec as P

epsilon = 1e-06
step_size = 0.03
MESH = pl.DeviceIdType.MESH
f32 = jnp.float32
bf16 = jnp.bfloat16
N = 512
ORDER = (1, 0, 2)


def split(x):
    hi = x.astype(bf16)
    return hi, (x - hi.astype(f32)).astype(bf16)


def dot(a, b):
    return jnp.dot(a, b, preferred_element_type=f32)


def mm3(ah, al, bh, bl):
    return dot(ah, bh) + (dot(ah, bl) + dot(al, bh))


def dot_nt(a, b):
    return lax.dot_general(a, b, (((1,), (1,)), ((), ())), preferred_element_type=f32)


def mm3_nt(ah, al, bh, bl):
    return dot_nt(ah, bh) + (dot_nt(ah, bl) + dot_nt(al, bh))


def normalize(v):
    return v * (1.0 / jnp.sqrt(jnp.mean(v * v, axis=-1, keepdims=True) + epsilon))


def chain_kernel(
    tok_hbm, wi_hbm, rate_ref, w0_hbm, wo_hbm, o_ref,
    tok_v, wo, w0, ks, ys, k32, y32, q32, rate, o_got, o_all, o_far, seed, seed32, wog, wos,
    kth, ktl, yth, ytl, big,
    w, wh, wl, r0, gp, gf, gf1, r1, r2,
    rs_s, rs_r, ag_s, ag_r, a1_s, a1_r, sh_s, sh_r, ex_s, ex_r,
    pt_s, pt_r, rl_s, rl_r, sd_s, sd_r, wg_s, wg_r, in_s, wi_s,
):
    tok = lax.axis_index("tok")
    block = lax.axis_index("block")
    head = lax.axis_index("head")
    core = lax.rem(tok, 2)
    chip = lax.div(tok, 2)
    x = lax.rem(chip, 4)
    z = lax.div(chip, 4)

    def at_x(d):
        return {"tok": (z * 4 + lax.rem(x + d, 4)) * 2 + core}

    def at_z(d):
        return {"tok": (lax.rem(z + d, 4) * 4 + x) * 2 + core}

    partner = {"tok": chip * 2 + (1 - core)}
    other_block = {"block": 1 - block}
    diagonal = {"block": 1 - block, "head": 1 - head}
    other_head = {"head": 1 - head}

    mine = pl.ds(pl.multiple_of(core * N, N), N)
    theirs = pl.ds(pl.multiple_of((1 - core) * N, N), N)

    SEQ = ((1, theirs), (2, theirs), (1, mine), (2, mine), (0, theirs), (0, mine))

    def weights(n):
        part, columns = SEQ[n]
        return pltpu.make_async_copy(wi_hbm.at[part, :, columns], big.at[n % 3], wi_s.at[n % 3])

    load_tok = pltpu.make_async_copy(tok_hbm, tok_v, in_s.at[0])
    load_w0 = pltpu.make_async_copy(w0_hbm.at[core], w0, in_s.at[1])
    own_half = pl.ds(pl.multiple_of(head * 2 * N, 2 * N), 2 * N)
    far_half = pl.ds(pl.multiple_of((1 - head) * 2 * N, 2 * N), 2 * N)
    load_wo = [
        pltpu.make_async_copy(wo_hbm.at[pl.ds(n * N, N), own_half], wo.at[n], in_s.at[2 + n])
        for n in range(2)
    ]
    seed_at = ((x * 64 + z * 16), (256 + z * 64 + x * 16))
    load_seed = [
        pltpu.make_async_copy(
            wo_hbm.at[pl.ds(pl.multiple_of(core * N + seed_at[n], 16), 16), far_half],
            seed.at[n], in_s.at[4 + n],
        )
        for n in range(2)
    ]
    for copy in load_seed:
        copy.start()
    load_tok.start()
    weights(0).start()
    weights(1).start()
    weights(2).start()
    load_w0.start()
    for copy in load_wo:
        copy.start()

    barrier = pltpu.get_barrier_semaphore()
    everyone = (
        partner, at_x(1), at_x(2), at_x(3), at_z(1), at_z(2), at_z(3), other_block, diagonal, other_head,
        {**other_block, **partner}, {**diagonal, **partner}, {**other_head, **partner},
    )
    for device in everyone:
        pl.semaphore_signal(barrier, inc=1, device_id=device, device_id_type=MESH)

    def rcopy(src, dst, ss, rs, device):
        return pltpu.make_async_remote_copy(
            src_ref=src, dst_ref=dst, send_sem=ss, recv_sem=rs,
            device_id=device, device_id_type=MESH,
        )

    swaps = [
        rcopy(src, dst, ex_s.at[n], ex_r.at[n], partner)
        for n, (src, dst) in enumerate(
            ((ks, k32.at[pl.ds(N, N)]), (ys, y32.at[pl.ds(N, N)]), (ks, q32.at[pl.ds(0, N)]))
        )
    ]

    def project(n, finish):
        weights(n).wait()
        return finish(dot(tok_v[...], big[n % 3]))

    def chosen_rate(which):
        return jnp.where(which == 0, rate[:, 0:1], rate[:, 1:2])

    def rows_of(s, j1, j2=None, off=0, count=64):
        at = s * 256 + j1 * 64 + off
        if j2 is not None:
            at = at + j2 * 16
        return pl.ds(pl.multiple_of(at, 8), count)

    def reduce_direct(m, piece, n, got, store, i, go, ss, rs, sent):
        copies = []
        for k, d in enumerate((1, 3, 2)):
            rows = piece(lax.rem(i + d, 4), 0, 2 * n)
            copies.append(rcopy(gp.at[m, rows], got.at[k], ss.at[k], rs.at[k], go(d)))
        for c in copies:
            c.start()
        yield
        for c in copies:
            c.wait_recv()
        store(0, gp[m, piece(i, 0, 2 * n), :] + got[0] + got[1] + got[2])
        sent.extend(copies)

    def gather_direct(buf, piece, n, i, go, ss, rs, done):
        rows = piece(i, 0, 2 * n)
        copies = [
            rcopy(buf.at[rows], buf.at[rows], ss.at[k], rs.at[k], go(d))
            for k, d in enumerate((1, 3, 2))
        ]
        for c in copies:
            c.start()
        yield
        for k, d in enumerate((1, 3, 2)):
            rows = piece(lax.rem(i + 4 - d, 4), 0, 2 * n)
            rcopy(buf.at[rows], buf.at[rows], ss.at[k], rs.at[k], go(d)).wait_recv()
        done.extend(copies)

    def gather_stage(buf, piece, n, i, go, ss, rs, done):
        nxt, prv, far = lax.rem(i + 1, 4), lax.rem(i + 3, 4), lax.rem(i + 2, 4)
        right, left = go(1), go(3)

        def send(k, rows, device):
            return rcopy(buf.at[rows], buf.at[rows], ss.at[k], rs.at[k], device)

        c0 = send(0, piece(i, 0, 2 * n), right)
        c1 = send(1, piece(i, 0, 2 * n), left)
        c0.start()
        c1.start()
        yield
        send(0, piece(prv, 0, 2 * n), right).wait_recv()
        c2 = send(2, piece(prv, 0, n), right)
        c2.start()
        send(1, piece(nxt, 0, 2 * n), left).wait_recv()
        c3 = send(3, piece(nxt, n, n), left)
        c3.start()
        yield
        send(2, piece(far, 0, n), right).wait_recv()
        send(3, piece(far, n, n), left).wait_recv()
        done.extend((c0, c1, c2, c3))

    axes = ((x, at_x, z, at_z), (z, at_z, x, at_x))

    def gather(buf, m, s, ss, rs, done):
        i1, go1, i2, go2 = axes[s]
        yield from gather_direct(
            buf.at[m], lambda j, o, c: rows_of(s, i1, j, o, c), 8, i2, go2,
            ss.at[m, s, 0], rs.at[m, s, 0], done,
        )
        yield from gather_stage(
            buf.at[m], lambda j, o, c: rows_of(s, j, None, o, c), 32, i1, go1,
            ss.at[m, s, 1], rs.at[m, s, 1], done,
        )

    SHARDS = tuple((m, n) for m in range(2) for n in range(2))
    seeds = [
        rcopy(
            seed32.at[m, n], wog.at[m, pl.ds(pl.multiple_of(seed_at[n], 16), 16)],
            sd_s.at[m, n], sd_r.at[m, n], diagonal,
        )
        for m, n in SHARDS
    ]
    def bring_weights(m, n, wo_sent):
        seeds[m * 2 + n].wait_recv()
        yield from gather(wog, m, n, wg_s, wg_r, wo_sent)

    wo_swap = rcopy(wog, wos, ex_s.at[5], ex_r.at[5], partner)

    load_tok.wait()
    ks[...] = project(0, normalize)
    weights(3).start()
    rate[...] = jax.nn.softplus(dot_nt(tok_v[...], rate_ref[...]))
    ys[...] = project(1, lambda v: v * chosen_rate(1 - core))
    pl.semaphore_wait(barrier, len(everyone))
    swaps[0].start()
    swaps[1].start()
    for copy in load_seed:
        copy.wait()
    for m, n in SHARDS:
        seed32[m, n] = seed[n, :, m * N:(m + 1) * N].astype(f32)
    for copy in seeds:
        copy.start()
    k32[:N, :] = project(2, normalize)
    y32[:N, :] = project(3, lambda v: v * chosen_rate(core))

    def project_q():
        weights(4).start()
        weights(5).start()
        swaps[0].wait_send()
        ks[...] = project(4, normalize)
        swaps[2].start()
        q32[N:, :] = project(5, normalize)
        swaps[2].wait_recv()

    load_w0.wait()

    def set_weights():
        for m in range(3):
            @pl.loop(0, 4)
            def _(i):
                rows = pl.ds(pl.multiple_of(i * 128, 128), 128)
                w[m, rows, :] = w0[m, rows, :].astype(f32)

            start = w[m]
            r0[m] = jnp.sqrt(jnp.mean(start * start, axis=0, keepdims=True))

    def keep_weights():
        wo_sent = []
        bringing = [bring_weights(m, n, wo_sent) for m, n in SHARDS]
        for _ in range(5):
            for g in bringing:
                next(g, None)
        wo_swap.start()
        wo_swap.wait_recv()

        @pl.loop(0, 4)
        def _(i):
            rows = pl.ds(pl.multiple_of(i * 128, 128), 128)
            for m in range(2):
                columns = pl.ds(m * N, N)
                wo[2 + core, rows, columns] = wog[m, rows, :].astype(bf16)
                wo[3 - core, rows, columns] = wos[m, rows, :].astype(bf16)

        for c in wo_sent:
            c.wait_send()

    def reduce_stage(m, piece, n, got, store, i, go, ss, rs, sent):
        src = gp.at[m]
        nxt, prv, far = lax.rem(i + 1, 4), lax.rem(i + 3, 4), lax.rem(i + 2, 4)
        right, left = go(1), go(3)
        c0 = rcopy(src.at[piece(far, 0, n)], got.at[0], ss.at[0], rs.at[0], right)
        c1 = rcopy(src.at[piece(far, n, n)], got.at[1], ss.at[1], rs.at[1], left)
        c2 = rcopy(src.at[piece(nxt, n, n)], got.at[2], ss.at[2], rs.at[2], right)
        c3 = rcopy(src.at[piece(prv, 0, n)], got.at[3], ss.at[3], rs.at[3], left)
        for c in (c0, c1, c2, c3):
            c.start()
        yield
        c0.wait_recv()
        got[0] = got[0] + gp[m, piece(nxt, 0, n), :]
        c4 = rcopy(got.at[0], got.at[4], ss.at[4], rs.at[4], right)
        c4.start()
        c1.wait_recv()
        got[1] = got[1] + gp[m, piece(prv, n, n), :]
        c5 = rcopy(got.at[1], got.at[5], ss.at[5], rs.at[5], left)
        c5.start()
        yield
        for c in (c2, c3, c4, c5):
            c.wait_recv()
        store(0, gp[m, piece(i, 0, n), :] + got[3] + got[4])
        store(n, gp[m, piece(i, n, n), :] + got[2] + got[5])
        sent.extend((c0, c1, c2, c3, c4, c5))

    def shard(m, s):
        i1, _, i2, _ = axes[s]
        rows = rows_of(s, i1, i2, 0, 16)
        return rcopy(gf.at[m, rows], gf1.at[m, rows], sh_s.at[m, s], sh_r.at[m, s], other_block)

    def reduce(m, s, sent):
        i1, go1, i2, go2 = axes[s]

        def store1(o, v):
            gp[m, rows_of(s, i1, None, o, v.shape[0]), :] = v

        def store2(o, v):
            gf[m, rows_of(s, i1, i2, o, 16), :] = v

        yield from reduce_stage(
            m, lambda j, o, c: rows_of(s, j, None, o, c), 32, r1.at[m, s], store1, i1, go1,
            rs_s.at[m, s, 0], rs_r.at[m, s, 0], sent,
        )
        yield from reduce_direct(
            m, lambda j, o, c: rows_of(s, i1, j, o, c), 8, r2.at[m, s], store2, i2, go2,
            rs_s.at[m, s, 1], rs_r.at[m, s, 1], sent,
        )

    def first_block(m, s, sent):
        yield from reduce(m, s, sent)
        shard(m, s).start()
        sent.append(shard(m, s))

    def last_block(m, s, sent):
        yield from reduce(m, s, sent)
        yield from gather(gf, m, s, ag_s, ag_r, sent)

    def update(m, g_ref):
        def rows_at(i):
            return pl.ds(pl.multiple_of(i * 64, 64), 64)

        def squares(i, total):
            g = g_ref[m, rows_at(i), :]
            return total + jnp.sum(g * g, axis=0, keepdims=True)

        total = jnp.sum(lax.fori_loop(0, 8, squares, jnp.zeros((1, N), f32)), axis=1, keepdims=True)
        scale = step_size / jnp.sqrt(total / (N * N) + epsilon)

        def move(i, column):
            rows = rows_at(i)
            moved = w[m, rows, :] + g_ref[m, rows, :] * scale
            w[m, rows, :] = moved
            return column + jnp.sum(moved * moved, axis=0, keepdims=True)

        column = lax.fori_loop(0, 8, move, jnp.zeros((1, N), f32)) / N
        factor = r0[m] / jnp.sqrt(column + epsilon)

        @pl.loop(0, 8)
        def _(i):
            rows = rows_at(i)
            fresh = w[m, rows, :] * factor
            w[m, rows, :] = fresh
            wh[m, rows, :], wl[m, rows, :] = split(fresh)

    def drive(streams, finish):
        left = {m: list(streams[m]) for m in streams}
        while left:
            for m in [m for m in ORDER if m in left]:
                still = []
                for g in left[m]:
                    try:
                        next(g)
                        still.append(g)
                    except StopIteration:
                        pass
                left[m] = still
                if not still:
                    del left[m]
                    finish(m)

    def transpose_all():
        @pl.loop(0, 2)
        def _(i):
            rows = pl.ds(pl.multiple_of(i * N, N), N)
            for source, th, tl in ((k32, kth, ktl), (y32, yth, ytl)):
                h, l = split(source[rows, :])
                th[:, rows] = h.T
                tl[:, rows] = l.T

    hh, hl = big.at[0, pl.ds(0, 2 * N)], big.at[0, pl.ds(2 * N, 2 * N)]
    p3h, p3l = big.at[1, pl.ds(0, 2 * N)], big.at[1, pl.ds(2 * N, 2 * N)]
    p1h, p1l = big.at[2, pl.ds(0, 2 * N)], big.at[2, pl.ds(2 * N, 2 * N)]

    def combine(rows, gate, upper, back):
        sigma = jax.nn.sigmoid(gate)
        active = gate * sigma
        hh[rows, :], hl[rows, :] = split(active * upper)
        p3h[rows, :], p3l[rows, :] = split(back * active)
        p1h[rows, :], p1l[rows, :] = split(back * upper * sigma * (1.0 + gate * (1.0 - sigma)))

    def learn():
        @pl.loop(0, 2)
        def _(i):
            rows = pl.ds(pl.multiple_of(i * N, N), N)
            ah, al = split(k32[rows, :])
            ch, cl = split(y32[rows, :])
            gate = mm3(ah, al, wh[0], wl[0])
            upper = mm3(ah, al, wh[1], wl[1])
            combine(rows, gate, upper, mm3(ch, cl, wh[2], wl[2]))

    @pl.when(block == 1)
    def _():
        swaps[0].wait_recv()
        swaps[1].wait_recv()
        project_q()
        set_weights()
        transpose_all()
        keep_weights()
        done = []

        def first(m, s):
            shard(m, s).wait_recv()
            yield from gather(gf1, m, s, a1_s, a1_r, done)

        drive({m: [first(m, s) for s in range(2)] for m in range(3)}, lambda m: update(m, gf1))
        learn()
        for c in done:
            c.wait_send()

    def forward(i):
        rows = pl.ds(i * N, N)
        ah, al = split(k32[rows, :])
        ch, cl = split(y32[rows, :])
        gate = dot(ah, w0[0]) + dot(al, w0[0])
        upper = dot(ah, w0[1]) + dot(al, w0[1])
        back = dot(ch, w0[2]) + dot(cl, w0[2])
        kth[:, rows] = ah.T
        ktl[:, rows] = al.T
        yth[:, rows] = ch.T
        ytl[:, rows] = cl.T
        combine(rows, gate, upper, back)

    def product(m, lth, ltl, rh, rl):
        @pl.loop(0, 2)
        def _(i):
            rows = pl.ds(pl.multiple_of(i * 256, 256), 256)
            gp[m, rows, :] = mm3(lth[rows, :], ltl[rows, :], rh[...], rl[...])

    def exchange(stream, finish, sent):
        live = {}

        def begin(m):
            live[m] = [stream(m, s, sent) for s in range(2)]
            for g in live[m]:
                next(g)

        product(1, kth, ktl, p3h, p3l)
        begin(1)
        product(0, kth, ktl, p1h, p1l)
        begin(0)
        product(2, yth, ytl, hh, hl)
        begin(2)
        drive(live, finish)

    @pl.when(block == 0)
    def _():
        sent = []
        forward(0)
        swaps[0].wait_recv()
        swaps[1].wait_recv()
        forward(1)
        exchange(first_block, lambda m: None, sent)
        live = {m: [gather(gf, m, s, ag_s, ag_r, sent) for s in range(2)] for m in range(3)}
        for m in ORDER:
            for g in live[m]:
                next(g)
        project_q()
        set_weights()
        drive(live, lambda m: update(m, gf))
        for c in sent:
            c.wait_send()

    @pl.when(block == 1)
    def _():
        sent = []
        exchange(last_block, lambda m: update(m, gf), sent)
        for c in sent:
            c.wait_send()

    def rows_at(j):
        return pl.ds(pl.multiple_of(j * 64, 64), 64)

    WAYS = (other_block, diagonal, other_block, diagonal)
    WAYS_ON = (diagonal, other_block, diagonal, other_block)

    receivers = ({"tok": partner["tok"]}, {})

    def direct(t, j):
        r = rows_at(j)
        device = {"head": 1 - head, **receivers[t]}
        return rcopy(gp.at[t, r], o_far.at[core, r], pt_s.at[t, j], pt_r.at[t, j], device)

    def arrival(t, j):
        r = rows_at(j)
        at = o_far.at[1 - core if t == 0 else core, r]
        return rcopy(at, at, pt_s.at[t, j], pt_r.at[t, j], other_head)

    def first_leg(t, j, device):
        r = rows_at(j)
        return rcopy(gp.at[t, r], gf1.at[t, r], rl_s.at[t, j], rl_r.at[t, j], device)

    def second_leg(t, j, device):
        r = rows_at(j)
        return rcopy(
            gf1.at[t, r], o_far.at[core, r], pt_s.at[t, 8 + j], pt_r.at[t, j],
            {**device, **receivers[t]},
        )

    def send_far(t, i):
        @pl.when(block == 0)
        def _():
            for j in range(4):
                direct(t, i * 4 + j).start()

        @pl.when(block == 1)
        def _():
            for j in range(4):
                first_leg(t, i * 4 + j, WAYS[j]).start()

    def give(i):
        rows = pl.ds(pl.multiple_of(i * 256, 256), 256)
        return rcopy(gp.at[0, rows], o_got.at[rows], ex_s.at[3 + i], ex_r.at[3 + i], partner)

    def apply(t):
        @pl.loop(0, 2)
        def _(i):
            rows = pl.ds(pl.multiple_of(i * 256, 256), 256)
            ah, al = split(q32[pl.ds(pl.multiple_of(t * N + i * 256, 256), 256), :])
            gate = mm3(ah, al, wh[0], wl[0])
            upper = mm3(ah, al, wh[1], wl[1])
            bh, bl = split(gate * jax.nn.sigmoid(gate) * upper)
            o = normalize(mm3_nt(bh, bl, wh[2], wl[2])).astype(bf16)
            gp[t, rows, :] = o.astype(f32)
            if t == 1:
                o_all[rows, mine] = o
            send_far(t, i)
            if t == 0:
                give(i).start()

    apply(0)
    apply(1)

    @pl.when(block == 0)
    def _():
        keep_weights()

    for copy in load_wo:
        copy.wait()
    for i in range(2):
        give(i).wait_recv()
    o_all[:, theirs] = o_got[...].astype(bf16)

    @pl.loop(0, 2)
    def _(i):
        rows = pl.ds(pl.multiple_of(i * 256, 256), 256)
        v = dot(o_all[rows, :N], wo[0]) + dot(o_all[rows, N:], wo[1])
        w[0, rows, :] = v[:, :N]
        w[1, rows, :] = v[:, N:]

    def add_theirs():
        for j in range(8):
            arrival(0, j).wait_recv()

        @pl.loop(0, 2)
        def _(i):
            rows = pl.ds(pl.multiple_of(i * 256, 256), 256)
            v = dot(o_far[1 - core, rows, :].astype(bf16), wo[3 - core])
            w[0, rows, :] = w[0, rows, :] + v[:, :N]
            w[1, rows, :] = w[1, rows, :] + v[:, N:]

    def add_mine(j):
        arrival(1, j).wait_recv()
        rows = rows_at(j)
        v = dot(o_far[core, rows, :].astype(bf16), wo[2 + core])
        o_ref[rows, :N] = (w[0, rows, :] + v[:, :N]).astype(bf16)
        o_ref[rows, N:] = (w[1, rows, :] + v[:, N:]).astype(bf16)

    def relay(t, i):
        for j in range(4):
            first_leg(t, 4 * i + j, WAYS[j]).wait_recv()
            second_leg(t, 4 * i + j, WAYS_ON[j]).start()

    @pl.when(block == 0)
    def _():
        @pl.loop(0, 2)
        def _(i):
            relay(0, i)

        add_theirs()

        @pl.loop(0, 2)
        def _(i):
            relay(1, i)
            for j in range(4):
                add_mine(4 * i + j)

        for t in range(2):
            @pl.loop(0, 8)
            def _(j):
                direct(t, j).wait_send()
                second_leg(t, j, diagonal).wait_send()

    @pl.when(block == 1)
    def _():
        add_theirs()

        @pl.loop(0, 8)
        def _(j):
            add_mine(j)

        for t in range(2):
            @pl.loop(0, 8)
            def _(j):
                first_leg(t, j, diagonal).wait_send()

    for c in swaps[1:] + seeds + [wo_swap, give(0), give(1)]:
        c.wait_send()


def chain(tokens, weight, rate_weight, fast_init, output_weight):
    dma = pltpu.SemaphoreType.DMA
    square = lambda n, t: pltpu.VMEM((n, N, N), t)
    wide = pltpu.VMEM((N, 2 * N), bf16)
    part = pltpu.VMEM((N, N), f32)
    tall = pltpu.VMEM((2 * N, N), f32)
    vmem = pl.BlockSpec(memory_space=pltpu.VMEM)
    hbm = pl.BlockSpec(memory_space=pl.ANY)
    return pl.pallas_call(
        chain_kernel,
        out_shape=jax.ShapeDtypeStruct((N, 2 * N), bf16),
        in_specs=[hbm, hbm, vmem, hbm, hbm],
        out_specs=vmem,
        scratch_shapes=[
            pltpu.VMEM((N, 4 * N), bf16), pltpu.VMEM((4, N, 2 * N), bf16), square(3, bf16),
            part, part, tall, tall, tall, pltpu.VMEM((N, 2), f32), part,
            pltpu.VMEM((N, 2 * N), bf16), square(2, f32),
            pltpu.VMEM((2, 16, 2 * N), bf16), pltpu.VMEM((2, 2, 16, N), f32),
            square(2, f32), square(2, f32),
            wide, wide, wide, wide, pltpu.VMEM((3, 4 * N, N), bf16),
            square(3, f32), square(3, bf16), square(3, bf16), pltpu.VMEM((3, 1, N), f32),
            square(3, f32), square(3, f32), square(3, f32),
            pltpu.VMEM((3, 2, 6, 32, N), f32), pltpu.VMEM((3, 2, 3, 16, N), f32),
            dma((3, 2, 2, 6)), dma((3, 2, 2, 6)),
            dma((3, 2, 2, 4)), dma((3, 2, 2, 4)),
            dma((3, 2, 2, 4)), dma((3, 2, 2, 4)),
            dma((3, 2)), dma((3, 2)),
            dma((6,)), dma((6,)),
            dma((2, 16)), dma((2, 8)), dma((2, 8)), dma((2, 8)),
            dma((2, 2)), dma((2, 2)), dma((2, 2, 2, 4)), dma((2, 2, 2, 4)),
            dma((6,)), dma((3,)),
        ],
        compiler_params=pltpu.CompilerParams(
            collective_id=0, has_side_effects=True, vmem_limit_bytes=67043328
        ),
    )(tokens, weight, rate_weight, fast_init, output_weight)


def body(tokens, input_weight, rate_weight, fast_init, output_weight):
    flat = tokens[0]
    mixed = chain(
        flat, jnp.transpose(input_weight, (1, 0, 2)), rate_weight.T, fast_init, output_weight
    )
    return mixed[None]


def solution(mesh):
    placed = (
        P("block", "tok", None),
        P(None, None, "head"),
        P(None, "head"),
        P("head", None, None, None),
        P("head", None),
    )
    return jax.shard_map(
        body, mesh=mesh, in_specs=placed, out_specs=P("block", "tok", "head"), check_vma=False
    )
```

```python
import jax
import jax.numpy as jnp
from jax import lax
from jax.experimental import pallas as pl
from jax.experimental.pallas import tpu as pltpu
from jax.sharding import PartitionSpec as P

epsilon = 1e-06
step_size = 0.03
MESH = pl.DeviceIdType.MESH
f32 = jnp.float32
bf16 = jnp.bfloat16
N = 512
ORDER = (1, 0, 2)


def split(x):
    hi = x.astype(bf16)
    return hi, (x - hi.astype(f32)).astype(bf16)


def dot(a, b):
    return jnp.dot(a, b, preferred_element_type=f32)


def mm3(ah, al, bh, bl):
    return dot(ah, bh) + (dot(ah, bl) + dot(al, bh))


def dot_nt(a, b):
    return lax.dot_general(a, b, (((1,), (1,)), ((), ())), preferred_element_type=f32)


def mm3_nt(ah, al, bh, bl):
    return dot_nt(ah, bh) + (dot_nt(ah, bl) + dot_nt(al, bh))


def normalize(v):
    return v * (1.0 / jnp.sqrt(jnp.mean(v * v, axis=-1, keepdims=True) + epsilon))


def chain_kernel(
    tok_hbm, wi_hbm, rate_ref, w0_hbm, wo_hbm, o_ref,
    tok_v, wo, w0, ks, ys, k32, y32, q32, rate, o_got, o_all, o_far, seed, seed32, wog, wos,
    kth, ktl, yth, ytl, big,
    w, wh, wl, r0, gp, gf, gf1, r1, r2,
    rs_s, rs_r, ag_s, ag_r, a1_s, a1_r, sh_s, sh_r, ex_s, ex_r,
    pt_s, pt_r, rl_s, rl_r, sd_s, sd_r, wg_s, wg_r, in_s, wi_s,
):
    tok = lax.axis_index("tok")
    block = lax.axis_index("block")
    head = lax.axis_index("head")
    core = lax.rem(tok, 2)
    chip = lax.div(tok, 2)
    x = lax.rem(chip, 4)
    z = lax.div(chip, 4)

    def at_x(d):
        return {"tok": (z * 4 + lax.rem(x + d, 4)) * 2 + core}

    def at_z(d):
        return {"tok": (lax.rem(z + d, 4) * 4 + x) * 2 + core}

    partner = {"tok": chip * 2 + (1 - core)}
    other_block = {"block": 1 - block}
    diagonal = {"block": 1 - block, "head": 1 - head}
    other_head = {"head": 1 - head}

    mine = pl.ds(pl.multiple_of(core * N, N), N)
    theirs = pl.ds(pl.multiple_of((1 - core) * N, N), N)

    SEQ = ((1, theirs), (2, theirs), (1, mine), (2, mine), (0, theirs), (0, mine))

    def weights(n):
        part, columns = SEQ[n]
        return pltpu.make_async_copy(wi_hbm.at[part, :, columns], big.at[n % 3], wi_s.at[n % 3])

    load_tok = pltpu.make_async_copy(tok_hbm, tok_v, in_s.at[0])
    load_w0 = pltpu.make_async_copy(w0_hbm.at[core], w0, in_s.at[1])
    own_half = pl.ds(pl.multiple_of(head * 2 * N, 2 * N), 2 * N)
    far_half = pl.ds(pl.multiple_of((1 - head) * 2 * N, 2 * N), 2 * N)
    load_wo = [
        pltpu.make_async_copy(wo_hbm.at[pl.ds(n * N, N), own_half], wo.at[n], in_s.at[2 + n])
        for n in range(2)
    ]
    seed_at = ((x * 64 + z * 16), (256 + z * 64 + x * 16))
    load_seed = [
        pltpu.make_async_copy(
            wo_hbm.at[pl.ds(pl.multiple_of(core * N + seed_at[n], 16), 16), far_half],
            seed.at[n], in_s.at[4 + n],
        )
        for n in range(2)
    ]
    for copy in load_seed:
        copy.start()
    load_tok.start()
    weights(0).start()
    weights(1).start()
    weights(2).start()
    load_w0.start()
    for copy in load_wo:
        copy.start()

    barrier = pltpu.get_barrier_semaphore()
    everyone = (
        partner, at_x(1), at_x(2), at_x(3), at_z(1), at_z(2), at_z(3), other_block, diagonal, other_head,
        {**other_block, **partner}, {**diagonal, **partner}, {**other_head, **partner},
    )
    for device in everyone:
        pl.semaphore_signal(barrier, inc=1, device_id=device, device_id_type=MESH)

    def rcopy(src, dst, ss, rs, device):
        return pltpu.make_async_remote_copy(
            src_ref=src, dst_ref=dst, send_sem=ss, recv_sem=rs,
            device_id=device, device_id_type=MESH,
        )

    swaps = [
        rcopy(src, dst, ex_s.at[n], ex_r.at[n], partner)
        for n, (src, dst) in enumerate(
            ((ks, k32.at[pl.ds(N, N)]), (ys, y32.at[pl.ds(N, N)]), (ks, q32.at[pl.ds(0, N)]))
        )
    ]

    def project(n, finish):
        weights(n).wait()
        return finish(dot(tok_v[...], big[n % 3]))

    def chosen_rate(which):
        return jnp.where(which == 0, rate[:, 0:1], rate[:, 1:2])

    def rows_of(s, j1, j2=None, off=0, count=64):
        at = s * 256 + j1 * 64 + off
        if j2 is not None:
            at = at + j2 * 16
        return pl.ds(pl.multiple_of(at, 8), count)

    def reduce_direct(m, piece, n, got, store, i, go, ss, rs, sent):
        copies = []
        for k, d in enumerate((1, 3, 2)):
            rows = piece(lax.rem(i + d, 4), 0, 2 * n)
            copies.append(rcopy(gp.at[m, rows], got.at[k], ss.at[k], rs.at[k], go(d)))
        for c in copies:
            c.start()
        yield
        for c in copies:
            c.wait_recv()
        store(0, gp[m, piece(i, 0, 2 * n), :] + got[0] + got[1] + got[2])
        sent.extend(copies)

    def gather_direct(buf, piece, n, i, go, ss, rs, done):
        rows = piece(i, 0, 2 * n)
        copies = [
            rcopy(buf.at[rows], buf.at[rows], ss.at[k], rs.at[k], go(d))
            for k, d in enumerate((1, 3, 2))
        ]
        for c in copies:
            c.start()
        yield
        for k, d in enumerate((1, 3, 2)):
            rows = piece(lax.rem(i + 4 - d, 4), 0, 2 * n)
            rcopy(buf.at[rows], buf.at[rows], ss.at[k], rs.at[k], go(d)).wait_recv()
        done.extend(copies)

    def gather_stage(buf, piece, n, i, go, ss, rs, done):
        nxt, prv, far = lax.rem(i + 1, 4), lax.rem(i + 3, 4), lax.rem(i + 2, 4)
        right, left = go(1), go(3)

        def send(k, rows, device):
            return rcopy(buf.at[rows], buf.at[rows], ss.at[k], rs.at[k], device)

        c0 = send(0, piece(i, 0, 2 * n), right)
        c1 = send(1, piece(i, 0, 2 * n), left)
        c0.start()
        c1.start()
        yield
        send(0, piece(prv, 0, 2 * n), right).wait_recv()
        c2 = send(2, piece(prv, 0, n), right)
        c2.start()
        send(1, piece(nxt, 0, 2 * n), left).wait_recv()
        c3 = send(3, piece(nxt, n, n), left)
        c3.start()
        yield
        send(2, piece(far, 0, n), right).wait_recv()
        send(3, piece(far, n, n), left).wait_recv()
        done.extend((c0, c1, c2, c3))

    axes = ((x, at_x, z, at_z), (z, at_z, x, at_x))

    def gather(buf, m, s, ss, rs, done):
        i1, go1, i2, go2 = axes[s]
        yield from gather_direct(
            buf.at[m], lambda j, o, c: rows_of(s, i1, j, o, c), 8, i2, go2,
            ss.at[m, s, 0], rs.at[m, s, 0], done,
        )
        yield from gather_stage(
            buf.at[m], lambda j, o, c: rows_of(s, j, None, o, c), 32, i1, go1,
            ss.at[m, s, 1], rs.at[m, s, 1], done,
        )

    SHARDS = tuple((m, n) for m in range(2) for n in range(2))
    seeds = [
        rcopy(
            seed32.at[m, n], wog.at[m, pl.ds(pl.multiple_of(seed_at[n], 16), 16)],
            sd_s.at[m, n], sd_r.at[m, n], diagonal,
        )
        for m, n in SHARDS
    ]
    def bring_weights(m, n, wo_sent):
        seeds[m * 2 + n].wait_recv()
        yield from gather(wog, m, n, wg_s, wg_r, wo_sent)

    wo_swap = rcopy(wog, wos, ex_s.at[5], ex_r.at[5], partner)

    load_tok.wait()
    ks[...] = project(0, normalize)
    weights(3).start()
    rate[...] = jax.nn.softplus(dot_nt(tok_v[...], rate_ref[...]))
    ys[...] = project(1, lambda v: v * chosen_rate(1 - core))
    pl.semaphore_wait(barrier, len(everyone))
    swaps[0].start()
    swaps[1].start()
    for copy in load_seed:
        copy.wait()
    for m, n in SHARDS:
        seed32[m, n] = seed[n, :, m * N:(m + 1) * N].astype(f32)
    for copy in seeds:
        copy.start()
    k32[:N, :] = project(2, normalize)
    y32[:N, :] = project(3, lambda v: v * chosen_rate(core))

    def project_q():
        weights(4).start()
        weights(5).start()
        swaps[0].wait_send()
        ks[...] = project(4, normalize)
        swaps[2].start()
        q32[N:, :] = project(5, normalize)

    load_w0.wait()

    def set_weights():
        for m in range(3):
            @pl.loop(0, 4)
            def _(i):
                rows = pl.ds(pl.multiple_of(i * 128, 128), 128)
                w[m, rows, :] = w0[m, rows, :].astype(f32)

            start = w[m]
            r0[m] = jnp.sqrt(jnp.mean(start * start, axis=0, keepdims=True))

    def keep_weights():
        wo_sent = []
        bringing = [bring_weights(m, n, wo_sent) for m, n in SHARDS]
        for _ in range(5):
            for g in bringing:
                next(g, None)
        wo_swap.start()
        wo_swap.wait_recv()

        @pl.loop(0, 4)
        def _(i):
            rows = pl.ds(pl.multiple_of(i * 128, 128), 128)
            for m in range(2):
                columns = pl.ds(m * N, N)
                wo[2 + core, rows, columns] = wog[m, rows, :].astype(bf16)
                wo[3 - core, rows, columns] = wos[m, rows, :].astype(bf16)

        for c in wo_sent:
            c.wait_send()

    def reduce_stage(m, piece, n, got, store, i, go, ss, rs, sent):
        src = gp.at[m]
        nxt, prv, far = lax.rem(i + 1, 4), lax.rem(i + 3, 4), lax.rem(i + 2, 4)
        right, left = go(1), go(3)
        c0 = rcopy(src.at[piece(far, 0, n)], got.at[0], ss.at[0], rs.at[0], right)
        c1 = rcopy(src.at[piece(far, n, n)], got.at[1], ss.at[1], rs.at[1], left)
        c2 = rcopy(src.at[piece(nxt, n, n)], got.at[2], ss.at[2], rs.at[2], right)
        c3 = rcopy(src.at[piece(prv, 0, n)], got.at[3], ss.at[3], rs.at[3], left)
        for c in (c0, c1, c2, c3):
            c.start()
        yield
        c0.wait_recv()
        got[0] = got[0] + gp[m, piece(nxt, 0, n), :]
        c4 = rcopy(got.at[0], got.at[4], ss.at[4], rs.at[4], right)
        c4.start()
        c1.wait_recv()
        got[1] = got[1] + gp[m, piece(prv, n, n), :]
        c5 = rcopy(got.at[1], got.at[5], ss.at[5], rs.at[5], left)
        c5.start()
        yield
        for c in (c2, c3, c4, c5):
            c.wait_recv()
        store(0, gp[m, piece(i, 0, n), :] + got[3] + got[4])
        store(n, gp[m, piece(i, n, n), :] + got[2] + got[5])
        sent.extend((c0, c1, c2, c3, c4, c5))

    def shard(m, s):
        i1, _, i2, _ = axes[s]
        rows = rows_of(s, i1, i2, 0, 16)
        return rcopy(gf.at[m, rows], gf1.at[m, rows], sh_s.at[m, s], sh_r.at[m, s], other_block)

    def reduce(m, s, sent):
        i1, go1, i2, go2 = axes[s]

        def store1(o, v):
            gp[m, rows_of(s, i1, None, o, v.shape[0]), :] = v

        def store2(o, v):
            gf[m, rows_of(s, i1, i2, o, 16), :] = v

        yield from reduce_stage(
            m, lambda j, o, c: rows_of(s, j, None, o, c), 32, r1.at[m, s], store1, i1, go1,
            rs_s.at[m, s, 0], rs_r.at[m, s, 0], sent,
        )
        yield from reduce_direct(
            m, lambda j, o, c: rows_of(s, i1, j, o, c), 8, r2.at[m, s], store2, i2, go2,
            rs_s.at[m, s, 1], rs_r.at[m, s, 1], sent,
        )

    def first_block(m, s, sent):
        yield from reduce(m, s, sent)
        shard(m, s).start()
        sent.append(shard(m, s))

    def last_block(m, s, sent):
        yield from reduce(m, s, sent)
        yield from gather(gf, m, s, ag_s, ag_r, sent)

    def update(m, g_ref):
        def rows_at(i):
            return pl.ds(pl.multiple_of(i * 64, 64), 64)

        def squares(i, total):
            g = g_ref[m, rows_at(i), :]
            return total + jnp.sum(g * g, axis=0, keepdims=True)

        total = jnp.sum(lax.fori_loop(0, 8, squares, jnp.zeros((1, N), f32)), axis=1, keepdims=True)
        scale = step_size / jnp.sqrt(total / (N * N) + epsilon)

        def move(i, column):
            rows = rows_at(i)
            moved = w[m, rows, :] + g_ref[m, rows, :] * scale
            w[m, rows, :] = moved
            return column + jnp.sum(moved * moved, axis=0, keepdims=True)

        column = lax.fori_loop(0, 8, move, jnp.zeros((1, N), f32)) / N
        factor = r0[m] / jnp.sqrt(column + epsilon)

        @pl.loop(0, 8)
        def _(i):
            rows = rows_at(i)
            fresh = w[m, rows, :] * factor
            w[m, rows, :] = fresh
            wh[m, rows, :], wl[m, rows, :] = split(fresh)

    def drive(streams, finish):
        left = {m: list(streams[m]) for m in streams}
        while left:
            for m in [m for m in ORDER if m in left]:
                still = []
                for g in left[m]:
                    try:
                        next(g)
                        still.append(g)
                    except StopIteration:
                        pass
                left[m] = still
                if not still:
                    del left[m]
                    finish(m)

    def transpose_all():
        @pl.loop(0, 2)
        def _(i):
            rows = pl.ds(pl.multiple_of(i * N, N), N)
            for source, th, tl in ((k32, kth, ktl), (y32, yth, ytl)):
                h, l = split(source[rows, :])
                th[:, rows] = h.T
                tl[:, rows] = l.T

    hh, hl = big.at[0, pl.ds(0, 2 * N)], big.at[0, pl.ds(2 * N, 2 * N)]
    p3h, p3l = big.at[1, pl.ds(0, 2 * N)], big.at[1, pl.ds(2 * N, 2 * N)]
    p1h, p1l = big.at[2, pl.ds(0, 2 * N)], big.at[2, pl.ds(2 * N, 2 * N)]

    def combine(rows, gate, upper, back):
        sigma = jax.nn.sigmoid(gate)
        active = gate * sigma
        hh[rows, :], hl[rows, :] = split(active * upper)
        p3h[rows, :], p3l[rows, :] = split(back * active)
        p1h[rows, :], p1l[rows, :] = split(back * upper * sigma * (1.0 + gate * (1.0 - sigma)))

    def learn():
        @pl.loop(0, 2)
        def _(i):
            rows = pl.ds(pl.multiple_of(i * N, N), N)
            ah, al = split(k32[rows, :])
            ch, cl = split(y32[rows, :])
            gate = mm3(ah, al, wh[0], wl[0])
            upper = mm3(ah, al, wh[1], wl[1])
            combine(rows, gate, upper, mm3(ch, cl, wh[2], wl[2]))

    @pl.when(block == 1)
    def _():
        swaps[0].wait_recv()
        swaps[1].wait_recv()
        project_q()
        set_weights()
        transpose_all()
        keep_weights()
        done = []

        def first(m, s):
            shard(m, s).wait_recv()
            yield from gather(gf1, m, s, a1_s, a1_r, done)

        drive({m: [first(m, s) for s in range(2)] for m in range(3)}, lambda m: update(m, gf1))
        learn()
        for c in done:
            c.wait_send()

    def forward(i):
        rows = pl.ds(i * N, N)
        ah, al = split(k32[rows, :])
        ch, cl = split(y32[rows, :])
        gate = dot(ah, w0[0]) + dot(al, w0[0])
        upper = dot(ah, w0[1]) + dot(al, w0[1])
        back = dot(ch, w0[2]) + dot(cl, w0[2])
        kth[:, rows] = ah.T
        ktl[:, rows] = al.T
        yth[:, rows] = ch.T
        ytl[:, rows] = cl.T
        combine(rows, gate, upper, back)

    def product(m, lth, ltl, rh, rl):
        @pl.loop(0, 2)
        def _(i):
            rows = pl.ds(pl.multiple_of(i * 256, 256), 256)
            gp[m, rows, :] = mm3(lth[rows, :], ltl[rows, :], rh[...], rl[...])

    def exchange(stream, finish, sent):
        live = {}

        def begin(m):
            live[m] = [stream(m, s, sent) for s in range(2)]
            for g in live[m]:
                next(g)

        product(1, kth, ktl, p3h, p3l)
        begin(1)
        product(0, kth, ktl, p1h, p1l)
        begin(0)
        product(2, yth, ytl, hh, hl)
        begin(2)
        drive(live, finish)

    @pl.when(block == 0)
    def _():
        sent = []
        forward(0)
        swaps[0].wait_recv()
        swaps[1].wait_recv()
        forward(1)
        exchange(first_block, lambda m: None, sent)
        live = {m: [gather(gf, m, s, ag_s, ag_r, sent) for s in range(2)] for m in range(3)}
        for m in ORDER:
            for g in live[m]:
                next(g)
        project_q()
        set_weights()
        drive(live, lambda m: update(m, gf))
        for c in sent:
            c.wait_send()

    @pl.when(block == 1)
    def _():
        sent = []
        exchange(last_block, lambda m: update(m, gf), sent)
        for c in sent:
            c.wait_send()

    def rows_at(j):
        return pl.ds(pl.multiple_of(j * 64, 64), 64)

    WAYS = (other_block, diagonal, other_block, diagonal)
    WAYS_ON = (diagonal, other_block, diagonal, other_block)

    receivers = ({"tok": partner["tok"]}, {})

    def direct(t, j):
        r = rows_at(j)
        device = {"head": 1 - head, **receivers[t]}
        return rcopy(gp.at[t, r], o_far.at[core, r], pt_s.at[t, j], pt_r.at[t, j], device)

    def arrival(t, j):
        r = rows_at(j)
        at = o_far.at[1 - core if t == 0 else core, r]
        return rcopy(at, at, pt_s.at[t, j], pt_r.at[t, j], other_head)

    def first_leg(t, j, device):
        r = rows_at(j)
        return rcopy(gp.at[t, r], gf1.at[t, r], rl_s.at[t, j], rl_r.at[t, j], device)

    def second_leg(t, j, device):
        r = rows_at(j)
        return rcopy(
            gf1.at[t, r], o_far.at[core, r], pt_s.at[t, 8 + j], pt_r.at[t, j],
            {**device, **receivers[t]},
        )

    def send_far(t, i):
        @pl.when(block == 0)
        def _():
            for j in range(4):
                direct(t, i * 4 + j).start()

        @pl.when(block == 1)
        def _():
            for j in range(4):
                first_leg(t, i * 4 + j, WAYS[j]).start()

    def give(i):
        rows = pl.ds(pl.multiple_of(i * 256, 256), 256)
        return rcopy(gp.at[0, rows], o_got.at[rows], ex_s.at[3 + i], ex_r.at[3 + i], partner)

    def apply(t):
        @pl.loop(0, 2)
        def _(i):
            rows = pl.ds(pl.multiple_of(i * 256, 256), 256)
            ah, al = split(q32[pl.ds(pl.multiple_of(t * N + i * 256, 256), 256), :])
            gate = mm3(ah, al, wh[0], wl[0])
            upper = mm3(ah, al, wh[1], wl[1])
            bh, bl = split(gate * jax.nn.sigmoid(gate) * upper)
            o = normalize(mm3_nt(bh, bl, wh[2], wl[2])).astype(bf16)
            gp[t, rows, :] = o.astype(f32)
            if t == 1:
                o_all[rows, mine] = o
            send_far(t, i)
            if t == 0:
                give(i).start()

    swaps[2].wait_recv()
    apply(0)
    apply(1)

    @pl.when(block == 0)
    def _():
        keep_weights()

    for copy in load_wo:
        copy.wait()
    for i in range(2):
        give(i).wait_recv()
    o_all[:, theirs] = o_got[...].astype(bf16)

    @pl.loop(0, 2)
    def _(i):
        rows = pl.ds(pl.multiple_of(i * 256, 256), 256)
        v = dot(o_all[rows, :N], wo[0]) + dot(o_all[rows, N:], wo[1])
        w[0, rows, :] = v[:, :N]
        w[1, rows, :] = v[:, N:]

    def add_theirs():
        for j in range(8):
            arrival(0, j).wait_recv()

        @pl.loop(0, 2)
        def _(i):
            rows = pl.ds(pl.multiple_of(i * 256, 256), 256)
            v = dot(o_far[1 - core, rows, :].astype(bf16), wo[3 - core])
            w[0, rows, :] = w[0, rows, :] + v[:, :N]
            w[1, rows, :] = w[1, rows, :] + v[:, N:]

    def add_mine(j):
        arrival(1, j).wait_recv()
        rows = rows_at(j)
        v = dot(o_far[core, rows, :].astype(bf16), wo[2 + core])
        o_ref[rows, :N] = (w[0, rows, :] + v[:, :N]).astype(bf16)
        o_ref[rows, N:] = (w[1, rows, :] + v[:, N:]).astype(bf16)

    def relay(t, i):
        for j in range(4):
            first_leg(t, 4 * i + j, WAYS[j]).wait_recv()
            second_leg(t, 4 * i + j, WAYS_ON[j]).start()

    @pl.when(block == 0)
    def _():
        @pl.loop(0, 2)
        def _(i):
            relay(0, i)

        add_theirs()

        @pl.loop(0, 2)
        def _(i):
            relay(1, i)
            for j in range(4):
                add_mine(4 * i + j)

        for t in range(2):
            @pl.loop(0, 8)
            def _(j):
                direct(t, j).wait_send()
                second_leg(t, j, diagonal).wait_send()

    @pl.when(block == 1)
    def _():
        add_theirs()

        @pl.loop(0, 8)
        def _(j):
            add_mine(j)

        for t in range(2):
            @pl.loop(0, 8)
            def _(j):
                first_leg(t, j, diagonal).wait_send()

    for c in swaps[1:] + seeds + [wo_swap, give(0), give(1)]:
        c.wait_send()


def chain(tokens, weight, rate_weight, fast_init, output_weight):
    dma = pltpu.SemaphoreType.DMA
    square = lambda n, t: pltpu.VMEM((n, N, N), t)
    wide = pltpu.VMEM((N, 2 * N), bf16)
    part = pltpu.VMEM((N, N), f32)
    tall = pltpu.VMEM((2 * N, N), f32)
    vmem = pl.BlockSpec(memory_space=pltpu.VMEM)
    hbm = pl.BlockSpec(memory_space=pl.ANY)
    return pl.pallas_call(
        chain_kernel,
        out_shape=jax.ShapeDtypeStruct((N, 2 * N), bf16),
        in_specs=[hbm, hbm, vmem, hbm, hbm],
        out_specs=vmem,
        scratch_shapes=[
            pltpu.VMEM((N, 4 * N), bf16), pltpu.VMEM((4, N, 2 * N), bf16), square(3, bf16),
            part, part, tall, tall, tall, pltpu.VMEM((N, 2), f32), part,
            pltpu.VMEM((N, 2 * N), bf16), square(2, f32),
            pltpu.VMEM((2, 16, 2 * N), bf16), pltpu.VMEM((2, 2, 16, N), f32),
            square(2, f32), square(2, f32),
            wide, wide, wide, wide, pltpu.VMEM((3, 4 * N, N), bf16),
            square(3, f32), square(3, bf16), square(3, bf16), pltpu.VMEM((3, 1, N), f32),
            square(3, f32), square(3, f32), square(3, f32),
            pltpu.VMEM((3, 2, 6, 32, N), f32), pltpu.VMEM((3, 2, 3, 16, N), f32),
            dma((3, 2, 2, 6)), dma((3, 2, 2, 6)),
            dma((3, 2, 2, 4)), dma((3, 2, 2, 4)),
            dma((3, 2, 2, 4)), dma((3, 2, 2, 4)),
            dma((3, 2)), dma((3, 2)),
            dma((6,)), dma((6,)),
            dma((2, 16)), dma((2, 8)), dma((2, 8)), dma((2, 8)),
            dma((2, 2)), dma((2, 2)), dma((2, 2, 2, 4)), dma((2, 2, 2, 4)),
            dma((6,)), dma((3,)),
        ],
        compiler_params=pltpu.CompilerParams(
            collective_id=0, has_side_effects=True, vmem_limit_bytes=67043328
        ),
    )(tokens, weight, rate_weight, fast_init, output_weight)


def body(tokens, input_weight, rate_weight, fast_init, output_weight):
    flat = tokens[0]
    mixed = chain(
        flat, jnp.transpose(input_weight, (1, 0, 2)), rate_weight.T, fast_init, output_weight
    )
    return mixed[None]


def solution(mesh):
    placed = (
        P("block", "tok", None),
        P(None, None, "head"),
        P(None, "head"),
        P("head", None, None, None),
        P("head", None),
    )
    return jax.shard_map(
        body, mesh=mesh, in_specs=placed, out_specs=P("block", "tok", "head"), check_vma=False
    )
```

```python
import jax
import jax.numpy as jnp
from jax import lax
from jax.experimental import pallas as pl
from jax.experimental.pallas import tpu as pltpu
from jax.sharding import PartitionSpec as P

epsilon = 1e-06
step_size = 0.03
MESH = pl.DeviceIdType.MESH
f32 = jnp.float32
bf16 = jnp.bfloat16
N = 512
ORDER = (1, 0, 2)


def split(x):
    hi = x.astype(bf16)
    return hi, (x - hi.astype(f32)).astype(bf16)


def dot(a, b):
    return jnp.dot(a, b, preferred_element_type=f32)


def mm3(ah, al, bh, bl):
    return dot(ah, bh) + (dot(ah, bl) + dot(al, bh))


def dot_nt(a, b):
    return lax.dot_general(a, b, (((1,), (1,)), ((), ())), preferred_element_type=f32)


def mm3_nt(ah, al, bh, bl):
    return dot_nt(ah, bh) + (dot_nt(ah, bl) + dot_nt(al, bh))


def normalize(v):
    return v * (1.0 / jnp.sqrt(jnp.mean(v * v, axis=-1, keepdims=True) + epsilon))


def chain_kernel(
    tok_hbm, wi_hbm, rate_ref, w0_hbm, wo_hbm, o_ref,
    tok_v, wo, w0, ks, ys, k32, y32, q32, rate, o_got, o_all, o_far, seed, seed32, wog, wos,
    kth, ktl, yth, ytl, big,
    w, wh, wl, r0, gp, gf, gf1, r1, r2,
    rs_s, rs_r, ag_s, ag_r, a1_s, a1_r, sh_s, sh_r, ex_s, ex_r,
    pt_s, pt_r, rl_s, rl_r, sd_s, sd_r, wg_s, wg_r, in_s, wi_s,
):
    tok = lax.axis_index("tok")
    block = lax.axis_index("block")
    head = lax.axis_index("head")
    core = lax.rem(tok, 2)
    chip = lax.div(tok, 2)
    x = lax.rem(chip, 4)
    z = lax.div(chip, 4)

    def at_x(d):
        return {"tok": (z * 4 + lax.rem(x + d, 4)) * 2 + core}

    def at_z(d):
        return {"tok": (lax.rem(z + d, 4) * 4 + x) * 2 + core}

    partner = {"tok": chip * 2 + (1 - core)}
    other_block = {"block": 1 - block}
    diagonal = {"block": 1 - block, "head": 1 - head}
    other_head = {"head": 1 - head}

    mine = pl.ds(pl.multiple_of(core * N, N), N)
    theirs = pl.ds(pl.multiple_of((1 - core) * N, N), N)

    SEQ = ((1, theirs), (2, theirs), (1, mine), (2, mine), (0, theirs), (0, mine))

    def weights(n):
        part, columns = SEQ[n]
        return pltpu.make_async_copy(wi_hbm.at[part, :, columns], big.at[n % 3], wi_s.at[n % 3])

    load_tok = pltpu.make_async_copy(tok_hbm, tok_v, in_s.at[0])
    load_w0 = pltpu.make_async_copy(w0_hbm.at[core], w0, in_s.at[1])
    own_half = pl.ds(pl.multiple_of(head * 2 * N, 2 * N), 2 * N)
    far_half = pl.ds(pl.multiple_of((1 - head) * 2 * N, 2 * N), 2 * N)
    load_wo = [
        pltpu.make_async_copy(wo_hbm.at[pl.ds(n * N, N), own_half], wo.at[n], in_s.at[2 + n])
        for n in range(2)
    ]
    seed_at = ((x * 64 + z * 16), (256 + z * 64 + x * 16))
    load_seed = [
        pltpu.make_async_copy(
            wo_hbm.at[pl.ds(pl.multiple_of(core * N + seed_at[n], 16), 16), far_half],
            seed.at[n], in_s.at[4 + n],
        )
        for n in range(2)
    ]
    for copy in load_seed:
        copy.start()
    load_tok.start()
    weights(0).start()
    weights(1).start()
    weights(2).start()
    load_w0.start()
    for copy in load_wo:
        copy.start()

    barrier = pltpu.get_barrier_semaphore()
    everyone = (
        partner, at_x(1), at_x(2), at_x(3), at_z(1), at_z(2), at_z(3), other_block, diagonal, other_head,
        {**other_block, **partner}, {**diagonal, **partner}, {**other_head, **partner},
    )
    for device in everyone:
        pl.semaphore_signal(barrier, inc=1, device_id=device, device_id_type=MESH)

    def rcopy(src, dst, ss, rs, device):
        return pltpu.make_async_remote_copy(
            src_ref=src, dst_ref=dst, send_sem=ss, recv_sem=rs,
            device_id=device, device_id_type=MESH,
        )

    swaps = [
        rcopy(src, dst, ex_s.at[n], ex_r.at[n], partner)
        for n, (src, dst) in enumerate(
            ((ks, k32.at[pl.ds(N, N)]), (ys, y32.at[pl.ds(N, N)]), (ks, q32.at[pl.ds(0, N)]))
        )
    ]

    def project(n, finish):
        weights(n).wait()
        return finish(dot(tok_v[...], big[n % 3]))

    def chosen_rate(which):
        return jnp.where(which == 0, rate[:, 0:1], rate[:, 1:2])

    def rows_of(s, j1, j2=None, off=0, count=64):
        at = s * 256 + j1 * 64 + off
        if j2 is not None:
            at = at + j2 * 16
        return pl.ds(pl.multiple_of(at, 8), count)

    def reduce_direct(m, piece, n, got, store, i, go, ss, rs, sent):
        copies = []
        for k, d in enumerate((1, 3, 2)):
            rows = piece(lax.rem(i + d, 4), 0, 2 * n)
            copies.append(rcopy(gp.at[m, rows], got.at[k], ss.at[k], rs.at[k], go(d)))
        for c in copies:
            c.start()
        yield
        for c in copies:
            c.wait_recv()
        store(0, gp[m, piece(i, 0, 2 * n), :] + got[0] + got[1] + got[2])
        sent.extend(copies)

    def gather_direct(buf, piece, n, i, go, ss, rs, done):
        rows = piece(i, 0, 2 * n)
        copies = [
            rcopy(buf.at[rows], buf.at[rows], ss.at[k], rs.at[k], go(d))
            for k, d in enumerate((1, 3, 2))
        ]
        for c in copies:
            c.start()
        yield
        for k, d in enumerate((1, 3, 2)):
            rows = piece(lax.rem(i + 4 - d, 4), 0, 2 * n)
            rcopy(buf.at[rows], buf.at[rows], ss.at[k], rs.at[k], go(d)).wait_recv()
        done.extend(copies)

    def gather_stage(buf, piece, n, i, go, ss, rs, done):
        nxt, prv, far = lax.rem(i + 1, 4), lax.rem(i + 3, 4), lax.rem(i + 2, 4)
        right, left = go(1), go(3)

        def send(k, rows, device):
            return rcopy(buf.at[rows], buf.at[rows], ss.at[k], rs.at[k], device)

        c0 = send(0, piece(i, 0, 2 * n), right)
        c1 = send(1, piece(i, 0, 2 * n), left)
        c0.start()
        c1.start()
        yield
        send(0, piece(prv, 0, 2 * n), right).wait_recv()
        c2 = send(2, piece(prv, 0, n), right)
        c2.start()
        send(1, piece(nxt, 0, 2 * n), left).wait_recv()
        c3 = send(3, piece(nxt, n, n), left)
        c3.start()
        yield
        send(2, piece(far, 0, n), right).wait_recv()
        send(3, piece(far, n, n), left).wait_recv()
        done.extend((c0, c1, c2, c3))

    axes = ((x, at_x, z, at_z), (z, at_z, x, at_x))

    def gather(buf, m, s, ss, rs, done):
        i1, go1, i2, go2 = axes[s]
        yield from gather_direct(
            buf.at[m], lambda j, o, c: rows_of(s, i1, j, o, c), 8, i2, go2,
            ss.at[m, s, 0], rs.at[m, s, 0], done,
        )
        yield from gather_stage(
            buf.at[m], lambda j, o, c: rows_of(s, j, None, o, c), 32, i1, go1,
            ss.at[m, s, 1], rs.at[m, s, 1], done,
        )

    SHARDS = tuple((m, n) for m in range(2) for n in range(2))
    seeds = [
        rcopy(
            seed32.at[m, n], wog.at[m, pl.ds(pl.multiple_of(seed_at[n], 16), 16)],
            sd_s.at[m, n], sd_r.at[m, n], diagonal,
        )
        for m, n in SHARDS
    ]
    def bring_weights(m, n, wo_sent):
        seeds[m * 2 + n].wait_recv()
        yield from gather(wog, m, n, wg_s, wg_r, wo_sent)

    wo_swap = rcopy(wog, wos, ex_s.at[5], ex_r.at[5], partner)

    load_tok.wait()
    ks[...] = project(0, normalize)
    weights(3).start()
    rate[...] = jax.nn.softplus(dot_nt(tok_v[...], rate_ref[...]))
    ys[...] = project(1, lambda v: v * chosen_rate(1 - core))
    pl.semaphore_wait(barrier, len(everyone))
    swaps[0].start()
    swaps[1].start()
    for copy in load_seed:
        copy.wait()
    for m, n in SHARDS:
        seed32[m, n] = seed[n, :, m * N:(m + 1) * N].astype(f32)
    for copy in seeds:
        copy.start()
    k32[:N, :] = project(2, normalize)
    y32[:N, :] = project(3, lambda v: v * chosen_rate(core))

    def project_q():
        weights(4).start()
        weights(5).start()
        swaps[0].wait_send()
        ks[...] = project(4, normalize)
        swaps[2].start()
        q32[N:, :] = project(5, normalize)

    load_w0.wait()

    def set_weights():
        for m in range(3):
            @pl.loop(0, 4)
            def _(i):
                rows = pl.ds(pl.multiple_of(i * 128, 128), 128)
                w[m, rows, :] = w0[m, rows, :].astype(f32)

            start = w[m]
            r0[m] = jnp.sqrt(jnp.mean(start * start, axis=0, keepdims=True))

    def keep_weights():
        wo_sent = []
        bringing = [bring_weights(m, n, wo_sent) for m, n in SHARDS]
        for _ in range(5):
            for g in bringing:
                next(g, None)
        wo_swap.start()
        wo_swap.wait_recv()

        @pl.loop(0, 4)
        def _(i):
            rows = pl.ds(pl.multiple_of(i * 128, 128), 128)
            for m in range(2):
                columns = pl.ds(m * N, N)
                wo[2 + core, rows, columns] = wog[m, rows, :].astype(bf16)
                wo[3 - core, rows, columns] = wos[m, rows, :].astype(bf16)

        for c in wo_sent:
            c.wait_send()

    def reduce_stage(m, piece, n, got, store, i, go, ss, rs, sent):
        src = gp.at[m]
        nxt, prv, far = lax.rem(i + 1, 4), lax.rem(i + 3, 4), lax.rem(i + 2, 4)
        right, left = go(1), go(3)
        c0 = rcopy(src.at[piece(far, 0, n)], got.at[0], ss.at[0], rs.at[0], right)
        c1 = rcopy(src.at[piece(far, n, n)], got.at[1], ss.at[1], rs.at[1], left)
        c2 = rcopy(src.at[piece(nxt, n, n)], got.at[2], ss.at[2], rs.at[2], right)
        c3 = rcopy(src.at[piece(prv, 0, n)], got.at[3], ss.at[3], rs.at[3], left)
        for c in (c0, c1, c2, c3):
            c.start()
        yield
        c0.wait_recv()
        got[0] = got[0] + gp[m, piece(nxt, 0, n), :]
        c4 = rcopy(got.at[0], got.at[4], ss.at[4], rs.at[4], right)
        c4.start()
        c1.wait_recv()
        got[1] = got[1] + gp[m, piece(prv, n, n), :]
        c5 = rcopy(got.at[1], got.at[5], ss.at[5], rs.at[5], left)
        c5.start()
        yield
        for c in (c2, c3, c4, c5):
            c.wait_recv()
        store(0, gp[m, piece(i, 0, n), :] + got[3] + got[4])
        store(n, gp[m, piece(i, n, n), :] + got[2] + got[5])
        sent.extend((c0, c1, c2, c3, c4, c5))

    def shard(m, s):
        i1, _, i2, _ = axes[s]
        rows = rows_of(s, i1, i2, 0, 16)
        return rcopy(gf.at[m, rows], gf1.at[m, rows], sh_s.at[m, s], sh_r.at[m, s], other_block)

    def reduce(m, s, sent):
        i1, go1, i2, go2 = axes[s]

        def store1(o, v):
            gp[m, rows_of(s, i1, None, o, v.shape[0]), :] = v

        def store2(o, v):
            gf[m, rows_of(s, i1, i2, o, 16), :] = v

        yield from reduce_stage(
            m, lambda j, o, c: rows_of(s, j, None, o, c), 32, r1.at[m, s], store1, i1, go1,
            rs_s.at[m, s, 0], rs_r.at[m, s, 0], sent,
        )
        yield from reduce_direct(
            m, lambda j, o, c: rows_of(s, i1, j, o, c), 8, r2.at[m, s], store2, i2, go2,
            rs_s.at[m, s, 1], rs_r.at[m, s, 1], sent,
        )

    def first_block(m, s, sent):
        yield from reduce(m, s, sent)
        shard(m, s).start()
        sent.append(shard(m, s))

    def last_block(m, s, sent):
        yield from reduce(m, s, sent)
        yield from gather(gf, m, s, ag_s, ag_r, sent)

    def update(m, g_ref):
        def rows_at(i):
            return pl.ds(pl.multiple_of(i * 64, 64), 64)

        def squares(i, total):
            g = g_ref[m, rows_at(i), :]
            return total + jnp.sum(g * g, axis=0, keepdims=True)

        total = jnp.sum(lax.fori_loop(0, 8, squares, jnp.zeros((1, N), f32)), axis=1, keepdims=True)
        scale = step_size / jnp.sqrt(total / (N * N) + epsilon)

        def move(i, column):
            rows = rows_at(i)
            moved = w[m, rows, :] + g_ref[m, rows, :] * scale
            w[m, rows, :] = moved
            return column + jnp.sum(moved * moved, axis=0, keepdims=True)

        column = lax.fori_loop(0, 8, move, jnp.zeros((1, N), f32)) / N
        factor = r0[m] / jnp.sqrt(column + epsilon)

        @pl.loop(0, 8)
        def _(i):
            rows = rows_at(i)
            fresh = w[m, rows, :] * factor
            w[m, rows, :] = fresh
            wh[m, rows, :], wl[m, rows, :] = split(fresh)

    def drive(streams, finish):
        left = {m: list(streams[m]) for m in streams}
        while left:
            for m in [m for m in ORDER if m in left]:
                still = []
                for g in left[m]:
                    try:
                        next(g)
                        still.append(g)
                    except StopIteration:
                        pass
                left[m] = still
                if not still:
                    del left[m]
                    finish(m)

    def transpose_all():
        @pl.loop(0, 2)
        def _(i):
            rows = pl.ds(pl.multiple_of(i * N, N), N)
            for source, th, tl in ((k32, kth, ktl), (y32, yth, ytl)):
                h, l = split(source[rows, :])
                th[:, rows] = h.T
                tl[:, rows] = l.T

    hh, hl = big.at[0, pl.ds(0, 2 * N)], big.at[0, pl.ds(2 * N, 2 * N)]
    p3h, p3l = big.at[1, pl.ds(0, 2 * N)], big.at[1, pl.ds(2 * N, 2 * N)]
    p1h, p1l = big.at[2, pl.ds(0, 2 * N)], big.at[2, pl.ds(2 * N, 2 * N)]

    def combine(rows, gate, upper, back):
        sigma = jax.nn.sigmoid(gate)
        active = gate * sigma
        hh[rows, :], hl[rows, :] = split(active * upper)
        p3h[rows, :], p3l[rows, :] = split(back * active)
        p1h[rows, :], p1l[rows, :] = split(back * upper * sigma * (1.0 + gate * (1.0 - sigma)))

    def learn():
        @pl.loop(0, 2)
        def _(i):
            rows = pl.ds(pl.multiple_of(i * N, N), N)
            ah, al = split(k32[rows, :])
            ch, cl = split(y32[rows, :])
            gate = mm3(ah, al, wh[0], wl[0])
            upper = mm3(ah, al, wh[1], wl[1])
            combine(rows, gate, upper, mm3(ch, cl, wh[2], wl[2]))

    @pl.when(block == 1)
    def _():
        swaps[0].wait_recv()
        swaps[1].wait_recv()
        project_q()
        set_weights()
        transpose_all()
        keep_weights()
        done = []

        def first(m, s):
            shard(m, s).wait_recv()
            yield from gather(gf1, m, s, a1_s, a1_r, done)

        drive({m: [first(m, s) for s in range(2)] for m in range(3)}, lambda m: update(m, gf1))
        learn()
        for c in done:
            c.wait_send()

    def forward(i):
        rows = pl.ds(i * N, N)
        ah, al = split(k32[rows, :])
        ch, cl = split(y32[rows, :])
        gate = dot(ah, w0[0]) + dot(al, w0[0])
        upper = dot(ah, w0[1]) + dot(al, w0[1])
        back = dot(ch, w0[2]) + dot(cl, w0[2])
        kth[:, rows] = ah.T
        ktl[:, rows] = al.T
        yth[:, rows] = ch.T
        ytl[:, rows] = cl.T
        combine(rows, gate, upper, back)

    def product(m, lth, ltl, rh, rl):
        @pl.loop(0, 2)
        def _(i):
            rows = pl.ds(pl.multiple_of(i * 256, 256), 256)
            gp[m, rows, :] = mm3(lth[rows, :], ltl[rows, :], rh[...], rl[...])

    def exchange(stream, finish, sent):
        live = {}

        def begin(m):
            live[m] = [stream(m, s, sent) for s in range(2)]
            for g in live[m]:
                next(g)

        product(1, kth, ktl, p3h, p3l)
        begin(1)
        product(0, kth, ktl, p1h, p1l)
        begin(0)
        product(2, yth, ytl, hh, hl)
        begin(2)
        drive(live, finish)

    @pl.when(block == 0)
    def _():
        sent = []
        forward(0)
        swaps[0].wait_recv()
        swaps[1].wait_recv()
        forward(1)
        exchange(first_block, lambda m: None, sent)
        live = {m: [gather(gf, m, s, ag_s, ag_r, sent) for s in range(2)] for m in range(3)}
        for m in ORDER:
            for g in live[m]:
                next(g)
        project_q()
        set_weights()
        drive(live, lambda m: update(m, gf))
        for c in sent:
            c.wait_send()

    @pl.when(block == 1)
    def _():
        sent = []
        exchange(last_block, lambda m: update(m, gf), sent)
        for c in sent:
            c.wait_send()

    def rows_at(j):
        return pl.ds(pl.multiple_of(j * 64, 64), 64)

    WAYS = (other_block, diagonal, other_block, diagonal)
    WAYS_ON = (diagonal, other_block, diagonal, other_block)

    receivers = ({"tok": partner["tok"]}, {})

    def direct(t, j):
        r = rows_at(j)
        device = {"head": 1 - head, **receivers[t]}
        return rcopy(gp.at[t, r], o_far.at[core, r], pt_s.at[t, j], pt_r.at[t, j], device)

    def arrival(t, j):
        r = rows_at(j)
        at = o_far.at[1 - core if t == 0 else core, r]
        return rcopy(at, at, pt_s.at[t, j], pt_r.at[t, j], other_head)

    def first_leg(t, j, device):
        r = rows_at(j)
        return rcopy(gp.at[t, r], gf1.at[t, r], rl_s.at[t, j], rl_r.at[t, j], device)

    def second_leg(t, j, device):
        r = rows_at(j)
        return rcopy(
            gf1.at[t, r], o_far.at[core, r], pt_s.at[t, 8 + j], pt_r.at[t, j],
            {**device, **receivers[t]},
        )

    def send_far(t, i):
        @pl.when(block == 0)
        def _():
            for j in range(4):
                direct(t, i * 4 + j).start()

        @pl.when(block == 1)
        def _():
            for j in range(4):
                first_leg(t, i * 4 + j, WAYS[j]).start()

    def give(i):
        rows = pl.ds(pl.multiple_of(i * 256, 256), 256)
        return rcopy(gp.at[0, rows], o_got.at[rows], ex_s.at[3 + i], ex_r.at[3 + i], partner)

    def apply(t):
        @pl.loop(0, 2)
        def _(i):
            rows = pl.ds(pl.multiple_of(i * 256, 256), 256)
            ah, al = split(q32[pl.ds(pl.multiple_of(t * N + i * 256, 256), 256), :])
            gate = mm3(ah, al, wh[0], wl[0])
            upper = mm3(ah, al, wh[1], wl[1])
            bh, bl = split(gate * jax.nn.sigmoid(gate) * upper)
            o = normalize(mm3_nt(bh, bl, wh[2], wl[2])).astype(bf16)
            gp[t, rows, :] = o.astype(f32)
            if t == 1:
                o_all[rows, mine] = o
            send_far(t, i)
            if t == 0:
                give(i).start()

    swaps[2].wait_recv()
    apply(0)
    apply(1)

    @pl.when(block == 0)
    def _():
        keep_weights()

    for copy in load_wo:
        copy.wait()
    for i in range(2):
        give(i).wait_recv()
    o_all[:, theirs] = o_got[...].astype(bf16)

    @pl.loop(0, 2)
    def _(i):
        rows = pl.ds(pl.multiple_of(i * 256, 256), 256)
        v = dot(o_all[rows, :N], wo[0]) + dot(o_all[rows, N:], wo[1])
        w[0, rows, :] = v[:, :N]
        w[1, rows, :] = v[:, N:]

    def add_theirs():
        for j in range(8):
            arrival(0, j).wait_recv()

        @pl.loop(0, 2)
        def _(i):
            rows = pl.ds(pl.multiple_of(i * 256, 256), 256)
            v = dot(o_far[1 - core, rows, :].astype(bf16), wo[3 - core])
            w[0, rows, :] = w[0, rows, :] + v[:, :N]
            w[1, rows, :] = w[1, rows, :] + v[:, N:]

    def add_mine(j):
        arrival(1, j).wait_recv()
        rows = rows_at(j)
        v = dot(o_far[core, rows, :].astype(bf16), wo[2 + core])
        o_ref[rows, :N] = (w[0, rows, :] + v[:, :N]).astype(bf16)
        o_ref[rows, N:] = (w[1, rows, :] + v[:, N:]).astype(bf16)

    def relay(t, i):
        for j in range(4):
            first_leg(t, 4 * i + j, WAYS[j]).wait_recv()
            second_leg(t, 4 * i + j, WAYS_ON[j]).start()

    @pl.when(block == 0)
    def _():
        @pl.loop(0, 2)
        def _(i):
            relay(0, i)

        @pl.loop(0, 2)
        def _(i):
            relay(1, i)

        add_theirs()

        @pl.loop(0, 8)
        def _(j):
            add_mine(j)

        for t in range(2):
            @pl.loop(0, 8)
            def _(j):
                direct(t, j).wait_send()
                second_leg(t, j, diagonal).wait_send()

    @pl.when(block == 1)
    def _():
        add_theirs()

        @pl.loop(0, 8)
        def _(j):
            add_mine(j)

        for t in range(2):
            @pl.loop(0, 8)
            def _(j):
                first_leg(t, j, diagonal).wait_send()

    for c in swaps[1:] + seeds + [wo_swap, give(0), give(1)]:
        c.wait_send()


def chain(tokens, weight, rate_weight, fast_init, output_weight):
    dma = pltpu.SemaphoreType.DMA
    square = lambda n, t: pltpu.VMEM((n, N, N), t)
    wide = pltpu.VMEM((N, 2 * N), bf16)
    part = pltpu.VMEM((N, N), f32)
    tall = pltpu.VMEM((2 * N, N), f32)
    vmem = pl.BlockSpec(memory_space=pltpu.VMEM)
    hbm = pl.BlockSpec(memory_space=pl.ANY)
    return pl.pallas_call(
        chain_kernel,
        out_shape=jax.ShapeDtypeStruct((N, 2 * N), bf16),
        in_specs=[hbm, hbm, vmem, hbm, hbm],
        out_specs=vmem,
        scratch_shapes=[
            pltpu.VMEM((N, 4 * N), bf16), pltpu.VMEM((4, N, 2 * N), bf16), square(3, bf16),
            part, part, tall, tall, tall, pltpu.VMEM((N, 2), f32), part,
            pltpu.VMEM((N, 2 * N), bf16), square(2, f32),
            pltpu.VMEM((2, 16, 2 * N), bf16), pltpu.VMEM((2, 2, 16, N), f32),
            square(2, f32), square(2, f32),
            wide, wide, wide, wide, pltpu.VMEM((3, 4 * N, N), bf16),
            square(3, f32), square(3, bf16), square(3, bf16), pltpu.VMEM((3, 1, N), f32),
            square(3, f32), square(3, f32), square(3, f32),
            pltpu.VMEM((3, 2, 6, 32, N), f32), pltpu.VMEM((3, 2, 3, 16, N), f32),
            dma((3, 2, 2, 6)), dma((3, 2, 2, 6)),
            dma((3, 2, 2, 4)), dma((3, 2, 2, 4)),
            dma((3, 2, 2, 4)), dma((3, 2, 2, 4)),
            dma((3, 2)), dma((3, 2)),
            dma((6,)), dma((6,)),
            dma((2, 16)), dma((2, 8)), dma((2, 8)), dma((2, 8)),
            dma((2, 2)), dma((2, 2)), dma((2, 2, 2, 4)), dma((2, 2, 2, 4)),
            dma((6,)), dma((3,)),
        ],
        compiler_params=pltpu.CompilerParams(
            collective_id=0, has_side_effects=True, vmem_limit_bytes=67043328
        ),
    )(tokens, weight, rate_weight, fast_init, output_weight)


def body(tokens, input_weight, rate_weight, fast_init, output_weight):
    flat = tokens[0]
    mixed = chain(
        flat, jnp.transpose(input_weight, (1, 0, 2)), rate_weight.T, fast_init, output_weight
    )
    return mixed[None]


def solution(mesh):
    placed = (
        P("block", "tok", None),
        P(None, None, "head"),
        P(None, "head"),
        P("head", None, None, None),
        P("head", None),
    )
    return jax.shard_map(
        body, mesh=mesh, in_specs=placed, out_specs=P("block", "tok", "head"), check_vma=False
    )
```
